32 devices in a mesh: dp: 2 (over core), ctx: 4 (over y, x), tensor: 4 (over z).
Axes of the slice: x: 2, y: 2, z: 4, core: 2. Of those that a mesh axis runs over, the one named last changes fastest.
Arguments:
- tokens: bfloat16 [2, 2, 1024, 2304], P(None, 'dp', 'ctx'), may hold values from -6 to 6
- span_order: int32 [8], replicated, may hold values from 0 to 7, as said below
- w_query: bfloat16 [2304, 2048], P(('dp', 'ctx'), 'tensor'), may hold values from -0.125 to 0.125
- w_key: bfloat16 [2304, 1024], P(('dp', 'ctx'), 'tensor'), may hold values from -0.125 to 0.125
- value_weight: bfloat16 [2304, 1024], P(('dp', 'ctx'), 'tensor'), may hold values from -0.125 to 0.125
- w_out: bfloat16 [2304, 2048], P(('dp', 'ctx'), 'tensor'), may hold values from -1 to 1
- w_gate: bfloat16 [2304, 9216], P(('dp', 'ctx'), 'tensor'), may hold values from -0.125 to 0.125
- w_up: bfloat16 [2304, 9216], P(('dp', 'ctx'), 'tensor'), may hold values from -0.125 to 0.125
- w_down: bfloat16 [2304, 9216], P(('dp', 'ctx'), 'tensor'), may hold values from -0.0625 to 0.0625
- gain_attn_in: bfloat16 [2304], P(('dp', 'ctx')), may hold values from -0.5 to 0.5
- gain_attn_out: bfloat16 [2304], P(('dp', 'ctx')), may hold values from -0.5 to 0.5
- gain_ffn_in: bfloat16 [2304], P(('dp', 'ctx')), may hold values from -0.5 to 0.5
- gain_ffn_out: bfloat16 [2304], P(('dp', 'ctx')), may hold values from -0.5 to 0.5
- cotangent: bfloat16 [2, 2, 1024, 2304], P(None, 'dp', 'ctx'), may hold values from -6 to 6
Outputs:
- block_out: bfloat16 [2, 2, 1024, 2304], P(None, 'dp', 'ctx')
- grad_tokens: bfloat16 [2, 2, 1024, 2304], P(None, 'dp', 'ctx')
- grad_w_query: float32 [2304, 2048], P(('dp', 'ctx'), 'tensor')
- grad_w_key: float32 [2304, 1024], P(('dp', 'ctx'), 'tensor')
- grad_w_value: float32 [2304, 1024], P(('dp', 'ctx'), 'tensor')
- grad_w_out: float32 [2304, 2048], P(('dp', 'ctx'), 'tensor')
- grad_w_gate: float32 [2304, 9216], P(('dp', 'ctx'), 'tensor')
- grad_w_up: float32 [2304, 9216], P(('dp', 'ctx'), 'tensor')
- grad_w_down: float32 [2304, 9216], P(('dp', 'ctx'), 'tensor')
- grad_gain_attn_in: float32 [2304], P(('dp', 'ctx'))
- grad_gain_attn_out: float32 [2304], P(('dp', 'ctx'))
- grad_gain_ffn_in: float32 [2304], P(('dp', 'ctx'))
- grad_gain_ffn_out: float32 [2304], P(('dp', 'ctx'))
The draws below stay inside these ranges and needn't reach their ends.
Inputs may be any that keep to these rules, and one draw needn't show every extreme that they name: `span_order`: the two slots 2 c and 2 c + 1 hold spans k and 7 - k for some k, in either order; every span appears in exactly one slot.
All inputs are finite; a program needn't handle non-finite values.
Results may differ from the reference program's by a relative error of at most 0.017.
Values may be sent and summed in bfloat16 or wider, within the bound.
No kernel may reach another device: no remote copies, remote signals or barrier semaphores. Data moves between devices by JAX's collectives and lax.ppermute only.
A program may use at most 256 MiB of HBM per device.

```python
from functools import partial
import jax
import jax.numpy as jnp
from jax import lax

MODEL_DIM = 2304
QUERY_HEADS = 8
KEY_VALUE_HEADS = 4
HEAD_SIZE = 256
FF = 9216
MICRO = 2
BATCH = 2
SEQ_LEN = 1024
SPANS = 8
SPAN = 128


def draw_span_order(key, part):
    pair_count = SPANS // 2
    order_key, flip_key = jax.random.split(key)
    pair_index = jax.random.permutation(order_key, pair_count).astype(jnp.int32)
    flip_bits = jax.random.randint(flip_key, (pair_count,), 0, 2)
    lower_span = pair_index
    upper_span = SPANS - 1 - pair_index
    first_slot = jnp.where(flip_bits == 1, upper_span, lower_span)
    second_slot = jnp.where(flip_bits == 1, lower_span, upper_span)
    return jnp.stack([first_slot, second_slot], axis=1).reshape(SPANS).astype(jnp.int32)


def block_levels(own_key, dims, shards, low, top_value):
    gain, own = 1.0, jax.random.fold_in(own_key, 6)
    for axis_at, parts in shards:
        draws = jnp.exp(jax.random.uniform(jax.random.fold_in(own, axis_at), (parts,), jnp.float32, low / len(shards), top_value / len(shards)))
        gain = gain * jnp.repeat(draws, dims[axis_at] // parts).reshape([-1 if axis == axis_at else 1 for axis in range(len(dims))])
    return gain


def scatter_about(stream_key, extent, scale, reach, shards=(), held_as=jnp.bfloat16):
    gain = block_levels(stream_key, extent, shards, -0.22, 0.18) if shards else 1.0
    values = jax.random.normal(stream_key, extent, jnp.float32) * scale * gain
    return jnp.minimum(jnp.maximum(values, -reach), reach).astype(held_as)


def setup_inputs(seed: int = 0) -> dict:
    splits = jax.random.split(jax.random.key(seed), 15)
    return {
        "tokens": scatter_about(splits[0], (MICRO, BATCH, SEQ_LEN, MODEL_DIM), 1.0, 6.0, ((1, 2), (2, 4))),
        "span_order": draw_span_order(jax.random.fold_in(splits[14], 71), 0),
        "w_query": scatter_about(splits[2], (MODEL_DIM, QUERY_HEADS * HEAD_SIZE), MODEL_DIM ** -0.5, 0.125, ((0, 8), (1, 4))),
        "w_key": scatter_about(splits[3], (MODEL_DIM, KEY_VALUE_HEADS * HEAD_SIZE), MODEL_DIM ** -0.5, 0.125, ((0, 8), (1, 4))),
        "value_weight": scatter_about(splits[4], (MODEL_DIM, KEY_VALUE_HEADS * HEAD_SIZE), MODEL_DIM ** -0.5, 0.125, ((0, 8), (1, 4))),
        "w_out": scatter_about(splits[5], (MODEL_DIM, QUERY_HEADS * HEAD_SIZE), (HEAD_SIZE // 8) ** -0.5, 1.0, ((0, 8), (1, 4))),
        "w_gate": scatter_about(splits[6], (MODEL_DIM, FF), MODEL_DIM ** -0.5, 0.125, ((0, 8), (1, 4))),
        "w_up": scatter_about(splits[7], (MODEL_DIM, FF), MODEL_DIM ** -0.5, 0.125, ((0, 8), (1, 4))),
        "w_down": scatter_about(splits[8], (MODEL_DIM, FF), FF ** -0.5, 0.0625, ((0, 8), (1, 4))),
        "gain_attn_in": jnp.clip(jax.random.uniform(splits[9], (MODEL_DIM,), jnp.float32, -0.5, 0.5) * block_levels(splits[9], (MODEL_DIM,), ((0, 8),), -0.4, 0.0), -0.5, 0.5).astype(jnp.bfloat16),
        "gain_attn_out": jnp.clip(jax.random.uniform(splits[10], (MODEL_DIM,), jnp.float32, -0.5, 0.5) * block_levels(splits[10], (MODEL_DIM,), ((0, 8),), -0.4, 0.0), -0.5, 0.5).astype(jnp.bfloat16),
        "gain_ffn_in": jnp.clip(jax.random.uniform(splits[11], (MODEL_DIM,), jnp.float32, -0.5, 0.5) * block_levels(splits[11], (MODEL_DIM,), ((0, 8),), -0.4, 0.0), -0.5, 0.5).astype(jnp.bfloat16),
        "gain_ffn_out": jnp.clip(jax.random.uniform(splits[12], (MODEL_DIM,), jnp.float32, -0.5, 0.5) * block_levels(splits[12], (MODEL_DIM,), ((0, 8),), -0.4, 0.0), -0.5, 0.5).astype(jnp.bfloat16),
        "cotangent": scatter_about(splits[13], (MICRO, BATCH, SEQ_LEN, MODEL_DIM), 1.0, 6.0, ((1, 2), (2, 4))),
    }


EPS = 1e-06
CAP = 50.0
BASE = 10000.0
HIGHEST = lax.Precision.HIGHEST

@jax.custom_vjp
def low(v):
    return lax.optimization_barrier(v.astype(jnp.bfloat16)).astype(jnp.float32)

@jax.custom_vjp
def low_back(v):
    return v

def low_keep(v):
    return (low(v), None)

def low_pass(kept, grad):
    return (grad,)

def back_keep(v):
    return (v, None)

def back_low(kept, grad):
    return (low(grad),)
low.defvjp(low_keep, low_pass)
low_back.defvjp(back_keep, back_low)

def rms_scale(values):
    return values * lax.rsqrt(lax.optimization_barrier(jnp.mean(values * values, axis=-1, keepdims=True)) + EPS)

def apply_rotary(values, token_positions):
    half_width = values.shape[-1] // 2
    inverse = BASE ** (-(jnp.arange(half_width, dtype=jnp.float32) * 2.0) / values.shape[-1])
    angles = token_positions.astype(jnp.float32)[:, None] * inverse[None, :]
    cosine = jnp.cos(angles)[:, None, :]
    sine_table = jnp.sin(angles)[:, None, :]
    leading = values[..., :half_width]
    trailing = values[..., half_width:]
    return jnp.concatenate([leading * cosine - trailing * sine_table, trailing * cosine + leading * sine_table], axis=-1)

def attend_causal(token_positions, operands):
    query_rows, key_rows, value_rows = operands
    raw = low_back(jnp.einsum('tgd,sd->gts', query_rows, key_rows, precision=HIGHEST) * HEAD_SIZE ** (-0.5))
    capped = CAP * jnp.tanh(raw / CAP)
    allowed = token_positions[None, :] <= token_positions[:, None]
    weight = jnp.where(allowed[None], jnp.exp(capped), 0.0)
    denominator = lax.optimization_barrier(jnp.sum(weight, axis=-1))
    numerator = low_back(jnp.einsum('gts,sd->tgd', low(weight), value_rows, precision=HIGHEST))
    return numerator / jnp.transpose(denominator)[:, :, None]

def block_forward(token_positions, input_rows, w_query, w_key, value_weight, w_out, w_gate, w_up, w_down, gain_attn_in, gain_attn_out, gain_ffn_in, gain_ffn_out):
    length_total = input_rows.shape[0]
    normed_input = low(rms_scale(input_rows) * (1.0 + gain_attn_in))
    query_lin = low_back(jnp.dot(normed_input, w_query, precision=HIGHEST))
    key_linear = low_back(jnp.dot(normed_input, w_key, precision=HIGHEST))
    every_value = low(low_back(jnp.dot(normed_input, value_weight, precision=HIGHEST)))
    query_matrix = low(apply_rotary(query_lin.reshape(length_total, QUERY_HEADS, HEAD_SIZE), token_positions))
    every_key = low(apply_rotary(key_linear.reshape(length_total, KEY_VALUE_HEADS, HEAD_SIZE), token_positions))
    grouped_heads = query_matrix.reshape(length_total, KEY_VALUE_HEADS, QUERY_HEADS // KEY_VALUE_HEADS, HEAD_SIZE).transpose(1, 0, 2, 3)
    head_output = lax.map(jax.checkpoint(partial(attend_causal, token_positions)), (grouped_heads, every_key.transpose(1, 0, 2), every_value.reshape(length_total, KEY_VALUE_HEADS, HEAD_SIZE).transpose(1, 0, 2)))
    attended = low(head_output.transpose(1, 0, 2, 3).reshape(length_total, QUERY_HEADS * HEAD_SIZE))
    attn_out = low_back(jnp.einsum('tk,dk->td', attended, w_out, precision=HIGHEST))
    hidden_one = input_rows + rms_scale(attn_out) * (1.0 + gain_attn_out)
    normed_two = low(rms_scale(hidden_one) * (1.0 + gain_ffn_in))
    gate_lin = low_back(jnp.dot(normed_two, w_gate, precision=HIGHEST))
    up_lin = low_back(jnp.dot(normed_two, w_up, precision=HIGHEST))
    hidden = low(jax.nn.gelu(gate_lin, approximate=True) * up_lin)
    ffn_out = low_back(jnp.einsum('tk,dk->td', hidden, w_down, precision=HIGHEST))
    return hidden_one + rms_scale(ffn_out) * (1.0 + gain_ffn_out)

def reference(tokens, span_order, w_query, w_key, value_weight, w_out, w_gate, w_up, w_down, gain_attn_in, gain_attn_out, gain_ffn_in, gain_ffn_out, cotangent):
    params = tuple((matrix.astype(jnp.float32) for matrix in (w_query, w_key, value_weight, w_out, w_gate, w_up, w_down, gain_attn_in, gain_attn_out, gain_ffn_in, gain_ffn_out)))
    row_index = jnp.arange(SEQ_LEN, dtype=jnp.int32)
    token_positions = (span_order[row_index // SPAN] * SPAN + row_index % SPAN).astype(jnp.int32)
    input_rows = tokens.astype(jnp.float32).reshape(MICRO * BATCH, SEQ_LEN, MODEL_DIM)
    upstream = cotangent.astype(jnp.float32).reshape(MICRO * BATCH, SEQ_LEN, MODEL_DIM)

    def per_sequence(running, operands):
        sequence, seq_grad = operands
        result, pullback = jax.vjp(partial(block_forward, token_positions), sequence, *params)
        gradients = pullback(seq_grad)
        return (tuple((before + fresh for before, fresh in zip(running, gradients[1:]))), (result, gradients[0]))
    zeros = tuple((jnp.zeros_like(matrix) for matrix in params))
    totals, (results, input_grads) = lax.scan(per_sequence, zeros, (input_rows, upstream))
    return (results.reshape(tokens.shape).astype(jnp.bfloat16), input_grads.reshape(tokens.shape).astype(jnp.bfloat16), totals[0], totals[1], totals[2], totals[3], totals[4], totals[5], totals[6], totals[7], totals[8], totals[9], totals[10])
```

```python
import functools

import jax
import jax.numpy as jnp
from jax import lax
from jax.experimental import pallas as pl
from jax.experimental.pallas import tpu as pltpu
from jax.sharding import PartitionSpec as P

HEAD_SIZE = 256
EPS = 1e-06
CAP = 50.0
BASE = 10000.0
BF = jnp.bfloat16
F32 = jnp.float32
PAD = 128
VMEM_LIMIT = 60 * 1024 * 1024
GELU_C = 0.7978845608028654
GELU_A = 0.044715


def apply_norm(values):
    factor = lax.rsqrt(jnp.mean(values * values, axis=-1, keepdims=True) + EPS)
    return values * factor, factor


def norm_backward(upstream, scaled, factor):
    return factor * (upstream - scaled * jnp.mean(upstream * scaled, axis=-1, keepdims=True))


def rotation(token_positions, width_size):
    half_width = width_size // 2
    inverse = BASE ** (-(jnp.arange(half_width, dtype=F32) * 2.0) / width_size)
    angles = token_positions.astype(F32)[:, None] * inverse[None, :]
    return jnp.cos(angles), jnp.sin(angles)


def mm(a, b):
    return jnp.dot(a, b, preferred_element_type=F32)


def mm_t(a, b):
    return lax.dot_general(a, b, (((1,), (1,)), ((), ())), preferred_element_type=F32)


def tmm(a, b):
    return lax.dot_general(a, b, (((0,), (0,)), ((), ())), preferred_element_type=F32)


def low(values):
    return lax.reduce_precision(values, 8, 7).astype(BF)


def call(body, out_shape, grid, in_specs, out_specs, scratch=(), flops=0, moved=0):
    return pl.pallas_call(
        body,
        out_shape=out_shape,
        grid_spec=pltpu.PrefetchScalarGridSpec(
            num_scalar_prefetch=0,
            grid=grid,
            in_specs=in_specs,
            out_specs=out_specs,
            scratch_shapes=list(scratch),
        ),
        compiler_params=pltpu.CompilerParams(
            dimension_semantics=("arbitrary",) * len(grid), vmem_limit_bytes=VMEM_LIMIT
        ),
        cost_estimate=pl.CostEstimate(flops=flops, bytes_accessed=moved, transcendentals=0),
    )


def shape(dims, dtype):
    return jax.ShapeDtypeStruct(dims, dtype)


def whole(dims):
    return pl.BlockSpec(dims, lambda *_: (0,) * len(dims))


def project_body(n_rot, x_ref, w_ref, cos_ref, sin_ref, out_ref):
    half = HEAD_SIZE // 2
    y = mm(x_ref[...], w_ref[...])
    rotate = pl.program_id(0) < n_rot
    cos = jnp.where(rotate, cos_ref[...], 1.0)
    sin = jnp.where(rotate, sin_ref[...], 0.0)
    a, b = y[:, :half], y[:, half:]
    out_ref[:, :half] = (a * cos - b * sin).astype(BF)
    out_ref[:, half:] = (b * cos + a * sin).astype(BF)


def project(normed, weights, columns, n_rot, cos, sin):
    rows, width = normed.shape
    return call(
        functools.partial(project_body, n_rot),
        shape((rows, columns), BF),
        (columns // HEAD_SIZE,),
        [
            whole((rows, width)),
            pl.BlockSpec((width, HEAD_SIZE), lambda j: (0, j)),
            whole(cos.shape),
            whole(sin.shape),
        ],
        pl.BlockSpec((rows, HEAD_SIZE), lambda j: (0, j)),
        flops=2 * rows * width * columns,
        moved=2 * (rows * width + width * columns + rows * columns),
    )(normed, weights, cos, sin)


def scores(q, k, allowed):
    soft = HEAD_SIZE ** (-0.5)
    bend = jnp.tanh(mm_t(q, k) * (soft / CAP))
    return bend, jnp.where(allowed, jnp.exp(CAP * bend), 0.0)


def attend_body(n_q, n_kv, n_pieces, *refs):
    hd = HEAD_SIZE
    q_ref, qpos_ref, kpos_ref = refs[:3]
    pieces = refs[3 : 3 + n_pieces]
    heads_ref, attended_ref, den_ref = refs[3 + n_pieces :]
    qpos = qpos_ref[...]
    for h in range(n_q):
        kv = h // (n_q // n_kv)
        q = q_ref[:, h * hd : (h + 1) * hd]
        num, den = 0.0, 0.0
        for j, piece in enumerate(pieces):
            size = piece.shape[0]
            allowed = kpos_ref[:, j * size : (j + 1) * size] <= qpos
            _, weight = scores(q, piece[:, kv * hd : (kv + 1) * hd], allowed)
            den = den + jnp.sum(weight, axis=-1, keepdims=True)
            v = piece[:, (n_kv + kv) * hd : (n_kv + kv + 1) * hd]
            num = num + mm(weight.astype(BF), v)
        heads = num / den
        heads_ref[:, h * hd : (h + 1) * hd] = heads
        attended_ref[:, h * hd : (h + 1) * hd] = heads.astype(BF)
        den_ref[:, h * PAD : (h + 1) * PAD] = jnp.broadcast_to(den, (den.shape[0], PAD))


def attend(q, q_block, pieces, qpos, kpos, n_q, n_kv):
    hd = HEAD_SIZE
    seq_dev = qpos.shape[0]
    specs = [pl.BlockSpec((seq_dev, n_q * hd), lambda i: (q_block, 0))]
    specs += [whole(qpos.shape), whole(kpos.shape)]
    arrays = [q, qpos, kpos]
    for array, size, row, col in pieces:
        specs.append(pl.BlockSpec((size, 2 * n_kv * hd), lambda i, row=row, col=col: (row, col)))
        arrays.append(array)
    seq = kpos.shape[1]
    return call(
        functools.partial(attend_body, n_q, n_kv, len(pieces)),
        (
            shape((seq_dev, n_q * hd), F32),
            shape((seq_dev, n_q * hd), BF),
            shape((seq_dev, n_q * PAD), F32),
        ),
        (1,),
        specs,
        (whole((seq_dev, n_q * hd)), whole((seq_dev, n_q * hd)), whole((seq_dev, n_q * PAD))),
        flops=4 * n_q * seq_dev * seq * hd,
        moved=2 * (2 * n_kv * hd * seq + 4 * seq_dev * n_q * hd),
    )(*arrays)


def attend_back_body(n_q, n_kv, n_pieces, *refs):
    hd = HEAD_SIZE
    half = hd // 2
    soft = hd ** (-0.5)
    q_ref, qpos_ref, kpos_ref, grad_ref, heads_ref, den_ref, cos_ref, sin_ref = refs[:8]
    pieces = refs[8 : 8 + n_pieces]
    q_back_ref = refs[8 + n_pieces]
    outs = refs[9 + n_pieces :]
    qpos = qpos_ref[...]
    group = n_q // n_kv
    for h in range(n_q):
        kv = h // group
        cols = slice(h * hd, (h + 1) * hd)
        k_cols = slice(kv * hd, (kv + 1) * hd)
        v_cols = slice((n_kv + kv) * hd, (n_kv + kv + 1) * hd)
        q = q_ref[:, cols]
        grad = grad_ref[:, cols]
        inverse = 1.0 / den_ref[:, h * PAD : h * PAD + 1]
        scaled = (grad * inverse).astype(BF)
        row_dot = jnp.sum(grad * heads_ref[:, cols], axis=-1, keepdims=True) * inverse
        q_grad = 0.0
        for j, piece in enumerate(pieces):
            size = piece.shape[0]
            allowed = kpos_ref[:, j * size : (j + 1) * size] <= qpos
            k, v = piece[:, k_cols], piece[:, v_cols]
            bend, weight = scores(q, k, allowed)
            prob = mm_t(scaled, v)
            score = (weight * (prob - row_dot) * (1.0 - bend * bend)).astype(BF)
            q_grad = q_grad + mm(score, k)
            k_term = tmm(score, q) * soft
            v_term = tmm(weight.astype(BF), scaled)
            if h % group == 0:
                outs[j][:, k_cols] = k_term
                outs[j][:, v_cols] = v_term
            else:
                outs[j][:, k_cols] += k_term
                outs[j][:, v_cols] += v_term
        q_grad = q_grad * soft
        a, b = q_grad[:, :half], q_grad[:, half:]
        q_back_ref[:, h * hd : h * hd + half] = (a * cos_ref[...] + b * sin_ref[...]).astype(BF)
        q_back_ref[:, h * hd + half : (h + 1) * hd] = (
            b * cos_ref[...] - a * sin_ref[...]
        ).astype(BF)


def attend_back(q, q_block, pieces, qpos, kpos, grad, heads, den, cos, sin, n_q, n_kv):
    hd = HEAD_SIZE
    seq_dev = qpos.shape[0]
    specs = [pl.BlockSpec((seq_dev, n_q * hd), lambda i: (q_block, 0))]
    arrays = [q, qpos, kpos, grad, heads, den, cos, sin]
    specs += [whole(a.shape) for a in arrays[1:]]
    out_shapes, out_specs = [shape((seq_dev, n_q * hd), BF)], [whole((seq_dev, n_q * hd))]
    for array, size, row, col in pieces:
        specs.append(pl.BlockSpec((size, 2 * n_kv * hd), lambda i, row=row, col=col: (row, col)))
        arrays.append(array)
        out_shapes.append(shape((size, 2 * n_kv * hd), F32))
        out_specs.append(whole((size, 2 * n_kv * hd)))
    seq = kpos.shape[1]
    return call(
        functools.partial(attend_back_body, n_q, n_kv, len(pieces)),
        tuple(out_shapes),
        (1,),
        specs,
        tuple(out_specs),
        flops=10 * n_q * seq_dev * seq * hd,
        moved=2 * (6 * n_kv * hd * seq + 8 * seq_dev * n_q * hd),
    )(*arrays)


def ffn_body(n_out, x_ref, wg_ref, wu_ref, wd_ref, gate_ref, up_ref, hid_ref, *rest):
    outs, acc = rest[:n_out], rest[n_out]
    j = pl.program_id(0)
    x = x_ref[...]
    gate = mm(x, wg_ref[...])
    up = mm(x, wu_ref[...])
    bend = jnp.tanh(GELU_C * (gate + GELU_A * gate * gate * gate))
    hidden = (0.5 * gate * (1.0 + bend) * up).astype(BF)
    gate_ref[...] = gate
    up_ref[...] = up
    hid_ref[...] = hidden
    term = mm_t(hidden, wd_ref[...])

    @pl.when(j == 0)
    def _():
        acc[...] = term

    @pl.when(j > 0)
    def _():
        acc[...] += term

    @pl.when(j == pl.num_programs(0) - 1)
    def _():
        size = acc.shape[0] // n_out
        for i, out in enumerate(outs):
            out[...] = acc[i * size : (i + 1) * size, :].astype(BF)


def ffn(x, weights, ff, n_out):
    rows, width = x.shape
    tile = 256
    steps = ff // tile
    col = lambda part: pl.BlockSpec((width, tile), lambda j: (0, part * steps + j))
    act = pl.BlockSpec((rows, tile), lambda j: (0, j))
    piece = (rows // n_out, width)
    return call(
        functools.partial(ffn_body, n_out),
        (shape((rows, ff), F32), shape((rows, ff), F32), shape((rows, ff), BF))
        + (shape(piece, BF),) * n_out,
        (steps,),
        [whole((rows, width)), col(0), col(1), col(2)],
        (act, act, act) + (whole(piece),) * n_out,
        [pltpu.VMEM((rows, width), F32)],
        flops=6 * rows * width * ff,
        moved=6 * width * ff + 4 * rows * width + 10 * rows * ff,
    )(x, weights, weights, weights)


def ffn_back_body(n_out, y_ref, wg_ref, wu_ref, wd_ref, gate_ref, up_ref, dg_ref, du_ref, *rest):
    outs, acc = rest[:n_out], rest[n_out]
    j = pl.program_id(0)
    grad = mm(y_ref[...], wd_ref[...])
    gate, up = gate_ref[...], up_ref[...]
    square = gate * gate
    bend = jnp.tanh(GELU_C * gate * (1.0 + GELU_A * square))
    rise = 0.5 * (1.0 + bend)
    slope = rise + 0.5 * gate * (1.0 - bend * bend) * (GELU_C * (1.0 + 3.0 * GELU_A * square))
    d_gate = (grad * up * slope).astype(BF)
    d_up = (grad * (gate * rise)).astype(BF)
    dg_ref[...] = d_gate
    du_ref[...] = d_up
    term = mm_t(d_gate, wg_ref[...]) + mm_t(d_up, wu_ref[...])

    @pl.when(j == 0)
    def _():
        acc[...] = term

    @pl.when(j > 0)
    def _():
        acc[...] += term

    @pl.when(j == pl.num_programs(0) - 1)
    def _():
        size = acc.shape[0] // n_out
        for i, out in enumerate(outs):
            out[...] = acc[i * size : (i + 1) * size, :].astype(BF)


def ffn_back(y, weights, gate, up, ff, n_out):
    rows, width = y.shape
    tile = 256
    steps = ff // tile
    col = lambda part: pl.BlockSpec((width, tile), lambda j: (0, part * steps + j))
    act = pl.BlockSpec((rows, tile), lambda j: (0, j))
    piece = (rows // n_out, width)
    return call(
        functools.partial(ffn_back_body, n_out),
        (shape((rows, ff), BF), shape((rows, ff), BF)) + (shape(piece, BF),) * n_out,
        (steps,),
        [whole((rows, width)), col(0), col(1), col(2), act, act],
        (act, act) + (whole(piece),) * n_out,
        [pltpu.VMEM((rows, width), F32)],
        flops=6 * rows * width * ff,
        moved=6 * width * ff + 4 * rows * width + 12 * rows * ff,
    )(y, weights, weights, weights, gate, up)


class Chain:
    def __init__(self):
        self.token = None

    def after(self, *values):
        if self.token is None:
            return values
        return lax.optimization_barrier((*values, self.token))[:-1]

    def mark(self, value):
        self.token = value
        return value


class Reduce:
    def __init__(self, chain):
        self.chain, self.piece, self.first = chain, {}, {}
        self.sums, self.second, self.total, self.third = {}, {}, {}, {}
        self.line = lax.axis_size("tensor") == 4

    def send(self, k, piece):
        self.piece[k] = piece
        if self.line:
            self.first[k] = lax.ppermute(piece, "tensor", [(0, 1), (3, 2)])
        else:
            self.total[k] = lax.psum(piece.astype(F32), "tensor")

    def add(self, k):
        if self.line:
            piece, first = self.chain.after(self.piece[k], self.first[k])
            total = low(piece.astype(F32) + first.astype(F32))
            self.sums[k] = self.chain.mark(total)
            self.second[k] = lax.ppermute(total, "tensor", [(1, 2), (2, 1)])

    def join(self, k):
        if self.line:
            sums, second = self.chain.after(self.sums[k], self.second[k])
            total = low(sums.astype(F32) + second.astype(F32))
            self.total[k] = self.chain.mark(total)
            self.third[k] = lax.ppermute(total, "tensor", [(1, 0), (2, 3)])

    def take(self, *ks):
        totals = [self.total[k] for k in ks]
        if self.line:
            zi = lax.axis_index("tensor")
            inner = (zi == 1) | (zi == 2)
            got = self.chain.after(*totals, *[self.third[k] for k in ks])
            n = len(ks)
            totals = [jnp.where(inner, got[i], got[n + i]) for i in range(n)]
        else:
            totals = list(self.chain.after(*totals))
        return jnp.concatenate(totals, axis=0).astype(F32)


def local(
    tokens,
    span_order,
    w_query,
    w_key,
    value_weight,
    w_out,
    w_gate,
    w_up,
    w_down,
    gain_attn_in,
    gain_attn_out,
    gain_ffn_in,
    gain_ffn_out,
    cotangent,
):
    micros, batch, seq_dev, width = tokens.shape
    n_dp, n_ctx, n_t = lax.axis_size("dp"), lax.axis_size("ctx"), lax.axis_size("tensor")
    dpi, ctx, zi = lax.axis_index("dp"), lax.axis_index("ctx"), lax.axis_index("tensor")
    seq = seq_dev * n_ctx
    span_len = seq // span_order.shape[0]
    hd = HEAD_SIZE
    n_kv = w_key.shape[1] // hd
    n_q = w_query.shape[1] // hd
    ff = w_gate.shape[1]
    qc, kc, oc = w_query.shape[1], w_key.shape[1], w_out.shape[1]
    n_seqs, chunks = micros * batch, 2
    swap = n_ctx == 4
    pair = n_dp == 2

    row_index = jnp.arange(seq, dtype=jnp.int32)
    all_pos = span_order[row_index // span_len] * span_len + row_index % span_len
    by_dev = all_pos.reshape(n_ctx, seq_dev)
    query_pos = lax.dynamic_index_in_dim(by_dev, ctx, 0, keepdims=False)
    if swap:
        key_pos = jnp.concatenate(
            [lax.dynamic_index_in_dim(by_dev, ctx ^ j, 0, keepdims=False) for j in range(n_ctx)]
        )
    else:
        key_pos = all_pos
    qpos, kpos = query_pos[:, None], key_pos[None, :]
    cos, sin = rotation(query_pos, hd)

    gains = jnp.stack([gain_attn_in, gain_attn_out, gain_ffn_in, gain_ffn_out], axis=1)
    gains = jnp.pad(gains, ((0, 0), (0, PAD - gains.shape[1])))
    pack_attn = jnp.concatenate([w_query, w_key, value_weight, w_out, gains], axis=1)
    pack_ffn = jnp.concatenate([w_gate, w_up, w_down], axis=1)
    full_attn = lax.all_gather(pack_attn, ("dp", "ctx"), axis=0, tiled=True)
    full_ffn = lax.all_gather(pack_ffn, ("dp", "ctx"), axis=0, tiled=True)
    at_out = qc + 2 * kc
    full_qkv = full_attn[:, :at_out]
    full_out = full_attn[:, at_out : at_out + oc]
    pick = jnp.eye(8, PAD, dtype=BF)
    gain_rows = mm_t(pick, full_attn[:, at_out + oc :])
    scale_in, scale_attn, scale_mid, scale_fin = (1.0 + gain_rows[i : i + 1] for i in range(4))

    flips = [[(i, i ^ j) for i in range(n_ctx)] for j in range(n_ctx)]

    def half(full, owner):
        return lax.dynamic_slice_in_dim(full, owner * (width // 2), width // 2, 1)

    def swap_core(value):
        return lax.ppermute(value, "dp", [(0, 1), (1, 0)])

    def grad_operands(lefts, rights):
        left, right = jnp.concatenate(lefts, axis=0), jnp.concatenate(rights, axis=0)
        if not pair:
            return left, right
        other_left = [swap_core(half(v, 1 - dpi)) for v in lefts]
        other_right = [swap_core(v) for v in rights]
        return (
            jnp.concatenate([half(v, dpi) for v in lefts] + other_left, axis=0),
            jnp.concatenate(list(rights) + other_right, axis=0),
        )

    def scatter(grad):
        axes = "ctx" if pair else ("dp", "ctx")
        return lax.psum_scatter(grad, axes, scatter_dimension=0, tiled=True)

    def mine(full):
        size = full.shape[0] // n_t
        return lax.dynamic_slice_in_dim(full, zi * size, size, 0)

    xs = tokens.astype(F32).reshape(n_seqs * seq_dev, width)
    xhats, fac_in = apply_norm(xs)
    normed = (xhats * scale_in).astype(BF)
    cos_all, sin_all = jnp.tile(cos, (n_seqs, 1)), jnp.tile(sin, (n_seqs, 1))
    qkv = project(normed, full_attn, qc + 2 * kc, n_q + n_kv, cos_all, sin_all)
    kv = qkv[:, qc:]
    if swap:
        others = [lax.ppermute(kv, "ctx", flips[j]) for j in range(1, n_ctx)]
        pieces = [[(a, seq_dev, m, 0) for a in [kv] + others] for m in range(n_seqs)]
    else:
        every = lax.all_gather(kv.reshape(n_seqs, seq_dev, 2 * kc), "ctx", axis=1, tiled=True)
        every = every.reshape(n_seqs * seq, 2 * kc)
        pieces = [[(every, seq, m, 0)] for m in range(n_seqs)]

    def rows_of(value, m):
        return value[m * seq_dev : (m + 1) * seq_dev]

    def split(value):
        size = value.shape[0] // 2
        return value[:size], value[size:]

    chain = Chain()
    st = [{}, {}]
    assert n_seqs == 2
    red = Reduce(chain)
    for m in (0, 1):
        s = st[m]
        (first, *rest) = chain.after(*[p[0] for p in pieces[m]])
        tied = [(v,) + p[1:] for v, p in zip([first, *rest], pieces[m])]
        s["pieces"] = tied
        s["heads"], s["attended"], s["den"] = attend(qkv, m, tied, qpos, kpos, n_q, n_kv)
        for i, rows in enumerate(split(s["attended"])):
            red.send(2 * m + i, chain.mark(mm_t(rows, full_out).astype(BF)))

    def drain(red):
        red.add(0), red.add(1), red.join(0), red.add(2)
        red.join(1), red.add(3), red.join(2)

    def post_attend(m, red):
        s = st[m]
        s["ahat"], s["fac_attn"] = apply_norm(red.take(2 * m, 2 * m + 1))
        s["hidden_one"] = rows_of(xs, m) + s["ahat"] * scale_attn
        s["h1hat"], s["fac_mid"] = apply_norm(s["hidden_one"])
        s["normed_two"] = chain.mark((s["h1hat"] * scale_mid).astype(BF))

    drain(red)
    red.join(3)
    post_attend(0, red)
    post_attend(1, red)

    red = Reduce(chain)
    for m in (0, 1):
        s = st[m]
        (value,) = chain.after(s["normed_two"])
        s["gate"], s["up"], s["hidden"], *part = ffn(value, full_ffn, ff, chunks)
        chain.mark(part[0])
        for i in range(2):
            red.send(2 * m + i, part[i])
    outputs = []
    dys = cotangent.astype(F32).reshape(n_seqs * seq_dev, width)
    gain_sums = [0.0] * 4

    def post_ffn(m, red):
        s = st[m]
        fhat, fac_out = apply_norm(red.take(2 * m, 2 * m + 1))
        outputs.append((s["hidden_one"] + fhat * scale_fin).astype(BF))
        dy = rows_of(dys, m)
        gain_sums[3] = gain_sums[3] + jnp.sum(mine(dy * fhat), axis=0)
        s["ffn_grad"] = chain.mark(norm_backward(dy * scale_fin, fhat, fac_out).astype(BF))

    def run_ffn_back(m, red):
        s = st[m]
        (value,) = chain.after(s["ffn_grad"])
        s["gate_grad"], s["up_grad"], *part = ffn_back(
            value, full_ffn, s["gate"], s["up"], ff, chunks
        )
        chain.mark(part[0])
        for i in range(2):
            red.send(2 * m + i, part[i])

    def every(name):
        return [s[name] for s in st]

    def chained_grad(lefts, rights):
        left, right = chain.after(*grad_operands(lefts, rights))
        return chain.mark(tmm(left, right).astype(BF))

    drain(red)
    post_ffn(0, red)
    red.join(3)
    back = Reduce(chain)
    run_ffn_back(0, back)
    post_ffn(1, red)
    run_ffn_back(1, back)
    red = back

    red.add(0), red.add(1)
    g_down = scatter(chained_grad(every("ffn_grad"), every("hidden")))
    red.join(0), red.add(2), red.join(1), red.add(3)
    both = [jnp.concatenate([s["gate_grad"], s["up_grad"]], axis=1) for s in st]
    g_gate_up = scatter(chained_grad(every("normed_two"), both))
    red.join(2)

    def post_mid(m, red):
        s = st[m]
        mid = red.take(2 * m, 2 * m + 1)
        gain_sums[2] = gain_sums[2] + jnp.sum(mine(mid * s["h1hat"]), axis=0)
        s["one_grad"] = rows_of(dys, m) + norm_backward(mid * scale_mid, s["h1hat"], s["fac_mid"])
        gain_sums[1] = gain_sums[1] + jnp.sum(mine(s["one_grad"] * s["ahat"]), axis=0)
        s["attn_grad"] = chain.mark(
            norm_backward(s["one_grad"] * scale_attn, s["ahat"], s["fac_attn"]).astype(BF)
        )

    def attention_back(m):
        s = st[m]
        (value,) = chain.after(s["attn_grad"])
        heads_grad = mm(value, full_out)
        s["q_back"], *s["terms"] = attend_back(
            qkv, m, s["pieces"], qpos, kpos, heads_grad, s["heads"], s["den"], cos, sin, n_q, n_kv
        )
        chain.mark(s["q_back"])
        if swap:
            s["moved"] = [
                lax.ppermute(s["terms"][j].astype(BF), "ctx", flips[j]) for j in range(1, n_ctx)
            ]
        else:
            s["moved"] = [lax.psum_scatter(s["terms"][0], "ctx", scatter_dimension=0, tiled=True)]

    def input_back(m, red):
        s = st[m]
        moved = chain.after(*s["moved"])
        kv_grad = s["terms"][0] if swap else 0.0
        for value in moved:
            kv_grad = kv_grad + value.astype(F32)
        backs = [s["q_back"]]
        for h in range(n_kv):
            a = kv_grad[:, h * hd : h * hd + hd // 2]
            b = kv_grad[:, h * hd + hd // 2 : (h + 1) * hd]
            backs += [(a * cos + b * sin).astype(BF), (b * cos - a * sin).astype(BF)]
        backs.append(kv_grad[:, kc:].astype(BF))
        s["qkv_back"] = jnp.concatenate(backs, axis=1)
        terms = mm_t(s["qkv_back"], full_qkv)
        gain_sums[0] = gain_sums[0] + jnp.sum(terms * rows_of(xhats, m), axis=0)
        for i, rows in enumerate(split(terms.astype(BF))):
            red.send(2 * m + i, chain.mark(rows))

    post_mid(0, red)
    attention_back(0)
    red.join(3)
    post_mid(1, red)
    attention_back(1)
    red = Reduce(chain)
    (g_down,) = chain.after(g_down)
    chain.mark(g_down)
    input_back(0, red)
    input_back(1, red)
    normed_list = [rows_of(normed, m) for m in range(n_seqs)]
    d_qkv = chained_grad(normed_list, every("qkv_back"))
    red.add(0), red.add(1)
    d_out = chained_grad(every("attn_grad"), every("attended"))
    gain_cols = jnp.stack(gain_sums, axis=1)
    if pair:
        keep = lax.dynamic_slice_in_dim(gain_cols, dpi * (width // 2), width // 2, 0)
        give = lax.dynamic_slice_in_dim(gain_cols, (1 - dpi) * (width // 2), width // 2, 0)
        gain_cols = keep + swap_core(give)
    gain_cols = jnp.pad(gain_cols.astype(BF), ((0, 0), (0, PAD - gain_cols.shape[1])))
    tail = jnp.concatenate([d_qkv, d_out, gain_cols], axis=1)
    if pair:
        tail = tail.reshape(n_ctx, tail.shape[0] // n_ctx, tail.shape[1])
        g_tail = lax.all_to_all(tail, "ctx", 0, 0)
    else:
        g_tail = scatter(tail)[None]
    red.join(0), red.add(2), red.join(1), red.add(3), red.join(2)

    input_grads = []

    def post_in(m, red):
        s = st[m]
        in_grad = red.take(2 * m, 2 * m + 1)
        grad = norm_backward(in_grad * scale_in, rows_of(xhats, m), rows_of(fac_in, m))
        input_grads.append(chain.mark((s["one_grad"] + grad).astype(BF)))

    post_in(0, red)
    red.join(3)
    (g_tail,) = chain.after(g_tail)
    g_tail = chain.mark(jnp.sum(g_tail.astype(F32), axis=0))
    g_gains = mm_t(pick.astype(F32), g_tail[:, at_out + oc :])
    g_gains = lax.all_to_all(
        jnp.broadcast_to(g_gains[None], (n_t,) + g_gains.shape), "tensor", 0, 0
    )
    post_in(1, red)
    g_gains = jnp.sum(g_gains, axis=0)
    g_gate_up = g_gate_up.astype(F32)
    return (
        jnp.concatenate(outputs, axis=0).reshape(tokens.shape),
        jnp.concatenate(input_grads, axis=0).reshape(tokens.shape),
        g_tail[:, :qc],
        g_tail[:, qc : qc + kc],
        g_tail[:, qc + kc : qc + 2 * kc],
        g_tail[:, at_out : at_out + oc],
        g_gate_up[:, :ff],
        g_gate_up[:, ff:],
        g_down.astype(F32),
        g_gains[0],
        g_gains[1],
        g_gains[2],
        g_gains[3],
    )


def solution(mesh):
    act = P(None, "dp", "ctx", None)
    mat = P(("dp", "ctx"), "tensor")
    vec = P(("dp", "ctx"))
    return jax.shard_map(
        local,
        mesh=mesh,
        in_specs=(act, P()) + (mat,) * 7 + (vec,) * 4 + (act,),
        out_specs=(act, act) + (mat,) * 7 + (vec,) * 4,
        check_vma=False,
    )
```

```python
import functools

import jax
import jax.numpy as jnp
from jax import lax
from jax.experimental import pallas as pl
from jax.experimental.pallas import tpu as pltpu
from jax.sharding import PartitionSpec as P

HEAD_SIZE = 256
EPS = 1e-06
CAP = 50.0
BASE = 10000.0
BF = jnp.bfloat16
F32 = jnp.float32
PAD = 128
VMEM_LIMIT = 60 * 1024 * 1024
GELU_C = 0.7978845608028654
GELU_A = 0.044715


def apply_norm(values):
    factor = lax.rsqrt(jnp.mean(values * values, axis=-1, keepdims=True) + EPS)
    return values * factor, factor


def norm_backward(upstream, scaled, factor):
    return factor * (upstream - scaled * jnp.mean(upstream * scaled, axis=-1, keepdims=True))


def rotation(token_positions, width_size):
    half_width = width_size // 2
    inverse = BASE ** (-(jnp.arange(half_width, dtype=F32) * 2.0) / width_size)
    angles = token_positions.astype(F32)[:, None] * inverse[None, :]
    return jnp.cos(angles), jnp.sin(angles)


def mm(a, b):
    return jnp.dot(a, b, preferred_element_type=F32)


def mm_t(a, b):
    return lax.dot_general(a, b, (((1,), (1,)), ((), ())), preferred_element_type=F32)


def tmm(a, b):
    return lax.dot_general(a, b, (((0,), (0,)), ((), ())), preferred_element_type=F32)


def low(values):
    return lax.reduce_precision(values, 8, 7).astype(BF)


def call(body, out_shape, grid, in_specs, out_specs, scratch=(), flops=0, moved=0):
    return pl.pallas_call(
        body,
        out_shape=out_shape,
        grid_spec=pltpu.PrefetchScalarGridSpec(
            num_scalar_prefetch=0,
            grid=grid,
            in_specs=in_specs,
            out_specs=out_specs,
            scratch_shapes=list(scratch),
        ),
        compiler_params=pltpu.CompilerParams(
            dimension_semantics=("arbitrary",) * len(grid), vmem_limit_bytes=VMEM_LIMIT
        ),
        cost_estimate=pl.CostEstimate(flops=flops, bytes_accessed=moved, transcendentals=0),
    )


def shape(dims, dtype):
    return jax.ShapeDtypeStruct(dims, dtype)


def whole(dims):
    return pl.BlockSpec(dims, lambda *_: (0,) * len(dims))


def project_body(n_rot, x_ref, w_ref, cos_ref, sin_ref, out_ref):
    half = HEAD_SIZE // 2
    y = mm(x_ref[...], w_ref[...])
    rotate = pl.program_id(0) < n_rot
    cos = jnp.where(rotate, cos_ref[...], 1.0)
    sin = jnp.where(rotate, sin_ref[...], 0.0)
    a, b = y[:, :half], y[:, half:]
    out_ref[:, :half] = (a * cos - b * sin).astype(BF)
    out_ref[:, half:] = (b * cos + a * sin).astype(BF)


def project(normed, weights, columns, n_rot, cos, sin):
    rows, width = normed.shape
    return call(
        functools.partial(project_body, n_rot),
        shape((rows, columns), BF),
        (columns // HEAD_SIZE,),
        [
            whole((rows, width)),
            pl.BlockSpec((width, HEAD_SIZE), lambda j: (0, j)),
            whole(cos.shape),
            whole(sin.shape),
        ],
        pl.BlockSpec((rows, HEAD_SIZE), lambda j: (0, j)),
        flops=2 * rows * width * columns,
        moved=2 * (rows * width + width * columns + rows * columns),
    )(normed, weights, cos, sin)


def scores(q, k, allowed):
    soft = HEAD_SIZE ** (-0.5)
    bend = jnp.tanh(mm_t(q, k) * (soft / CAP))
    return bend, jnp.where(allowed, jnp.exp(CAP * bend), 0.0)


def attend_body(n_q, n_kv, n_pieces, chunks, *refs):
    hd = HEAD_SIZE
    q_ref, qpos_ref, kpos_ref, w_ref = refs[:4]
    pieces = refs[4 : 4 + n_pieces]
    heads_ref, attended_ref, den_ref = refs[4 + n_pieces : 7 + n_pieces]
    outs = refs[7 + n_pieces :]
    qpos = qpos_ref[...]
    for h in range(n_q):
        kv = h // (n_q // n_kv)
        q = q_ref[:, h * hd : (h + 1) * hd]
        num, den = 0.0, 0.0
        for j, piece in enumerate(pieces):
            size = piece.shape[0]
            allowed = kpos_ref[:, j * size : (j + 1) * size] <= qpos
            _, weight = scores(q, piece[:, kv * hd : (kv + 1) * hd], allowed)
            den = den + jnp.sum(weight, axis=-1, keepdims=True)
            v = piece[:, (n_kv + kv) * hd : (n_kv + kv + 1) * hd]
            num = num + mm(weight.astype(BF), v)
        heads = num / den
        heads_ref[:, h * hd : (h + 1) * hd] = heads
        attended_ref[:, h * hd : (h + 1) * hd] = heads.astype(BF)
        den_ref[:, h * PAD : (h + 1) * PAD] = jnp.broadcast_to(den, (den.shape[0], PAD))
    put_chunks(mm_t(attended_ref[...], w_ref[...]), outs)


def put_chunks(value, outs):
    size = value.shape[0] // len(outs)
    for i, out in enumerate(outs):
        out[...] = value[i * size : (i + 1) * size].astype(BF)


def attend(q, q_block, pieces, qpos, kpos, n_q, n_kv, weights, out_block, chunks):
    hd = HEAD_SIZE
    seq_dev = qpos.shape[0]
    width = weights.shape[0]
    specs = [pl.BlockSpec((seq_dev, n_q * hd), lambda i: (q_block, 0))]
    specs += [whole(qpos.shape), whole(kpos.shape)]
    specs.append(pl.BlockSpec((width, n_q * hd), lambda i: (0, out_block)))
    arrays = [q, qpos, kpos, weights]
    for array, size, row, col in pieces:
        specs.append(pl.BlockSpec((size, 2 * n_kv * hd), lambda i, row=row, col=col: (row, col)))
        arrays.append(array)
    seq = kpos.shape[1]
    part = (seq_dev // chunks, width)
    return call(
        functools.partial(attend_body, n_q, n_kv, len(pieces), chunks),
        (
            shape((seq_dev, n_q * hd), F32),
            shape((seq_dev, n_q * hd), BF),
            shape((seq_dev, n_q * PAD), F32),
        )
        + (shape(part, BF),) * chunks,
        (1,),
        specs,
        (whole((seq_dev, n_q * hd)), whole((seq_dev, n_q * hd)), whole((seq_dev, n_q * PAD)))
        + (whole(part),) * chunks,
        flops=4 * n_q * seq_dev * seq * hd + 2 * seq_dev * n_q * hd * width,
        moved=2 * (2 * n_kv * hd * seq + 4 * seq_dev * n_q * hd + 2 * n_q * hd * width),
    )(*arrays)


def attend_back_body(n_q, n_kv, n_pieces, chunks, *refs):
    hd = HEAD_SIZE
    half = hd // 2
    soft = hd ** (-0.5)
    q_ref, qpos_ref, kpos_ref, heads_ref, den_ref, cos_ref, sin_ref, w_ref = refs[:8]
    pieces = refs[8 : 8 + n_pieces]
    grads = refs[8 + n_pieces : 8 + n_pieces + chunks]
    q_back_ref, *outs = refs[8 + n_pieces + chunks :]
    attn_grad = jnp.concatenate([g[...] for g in grads], axis=0)
    qpos = qpos_ref[...]
    group = n_q // n_kv
    for h in range(n_q):
        kv = h // group
        cols = slice(h * hd, (h + 1) * hd)
        k_cols = slice(kv * hd, (kv + 1) * hd)
        v_cols = slice((n_kv + kv) * hd, (n_kv + kv + 1) * hd)
        q = q_ref[:, cols]
        grad = mm(attn_grad, w_ref[:, cols])
        inverse = 1.0 / den_ref[:, h * PAD : h * PAD + 1]
        scaled = (grad * inverse).astype(BF)
        row_dot = jnp.sum(grad * heads_ref[:, cols], axis=-1, keepdims=True) * inverse
        q_grad = 0.0
        for j, piece in enumerate(pieces):
            size = piece.shape[0]
            allowed = kpos_ref[:, j * size : (j + 1) * size] <= qpos
            k, v = piece[:, k_cols], piece[:, v_cols]
            bend, weight = scores(q, k, allowed)
            prob = mm_t(scaled, v)
            score = (weight * (prob - row_dot) * (1.0 - bend * bend)).astype(BF)
            q_grad = q_grad + mm(score, k)
            k_term = tmm(score, q) * soft
            v_term = tmm(weight.astype(BF), scaled)
            if h % group == 0:
                outs[j][:, k_cols] = k_term
                outs[j][:, v_cols] = v_term
            else:
                outs[j][:, k_cols] += k_term
                outs[j][:, v_cols] += v_term
        q_grad = q_grad * soft
        a, b = q_grad[:, :half], q_grad[:, half:]
        q_back_ref[:, h * hd : h * hd + half] = (a * cos_ref[...] + b * sin_ref[...]).astype(BF)
        q_back_ref[:, h * hd + half : (h + 1) * hd] = (
            b * cos_ref[...] - a * sin_ref[...]
        ).astype(BF)


def attend_back(q, q_block, pieces, qpos, kpos, grads, heads, den, cos, sin, n_q, n_kv, weights, out_block):
    hd = HEAD_SIZE
    seq_dev = qpos.shape[0]
    width = weights.shape[0]
    specs = [pl.BlockSpec((seq_dev, n_q * hd), lambda i: (q_block, 0))]
    arrays = [q, qpos, kpos, heads, den, cos, sin]
    specs += [whole(a.shape) for a in arrays[1:]]
    specs.append(pl.BlockSpec((width, n_q * hd), lambda i: (0, out_block)))
    arrays.append(weights)
    out_shapes, out_specs = [shape((seq_dev, n_q * hd), BF)], [whole((seq_dev, n_q * hd))]
    for array, size, row, col in pieces:
        specs.append(pl.BlockSpec((size, 2 * n_kv * hd), lambda i, row=row, col=col: (row, col)))
        arrays.append(array)
        out_shapes.append(shape((size, 2 * n_kv * hd), F32))
        out_specs.append(whole((size, 2 * n_kv * hd)))
    arrays += grads
    specs += [whole(g.shape) for g in grads]
    seq = kpos.shape[1]
    return call(
        functools.partial(attend_back_body, n_q, n_kv, len(pieces), len(grads)),
        tuple(out_shapes),
        (1,),
        specs,
        tuple(out_specs),
        flops=10 * n_q * seq_dev * seq * hd + 2 * seq_dev * n_q * hd * width,
        moved=2 * (6 * n_kv * hd * seq + 8 * seq_dev * n_q * hd + 2 * n_q * hd * width),
    )(*arrays)


def input_back_body(n_q, n_kv, n_terms, chunks, *refs):
    hd = HEAD_SIZE
    half = hd // 2
    kc = n_kv * hd
    q_back_ref, x_ref, cos_ref, sin_ref, w_ref = refs[:5]
    terms = refs[5 : 5 + n_terms]
    back_ref, gain_ref, *outs = refs[5 + n_terms :]
    total = 0.0
    for term in terms:
        total = total + term[...].astype(F32)
    back_ref[:, : n_q * hd] = q_back_ref[...]
    for h in range(n_kv):
        start = (n_q + h) * hd
        a = total[:, h * hd : h * hd + half]
        b = total[:, h * hd + half : (h + 1) * hd]
        back_ref[:, start : start + half] = (a * cos_ref[...] + b * sin_ref[...]).astype(BF)
        back_ref[:, start + half : start + hd] = (b * cos_ref[...] - a * sin_ref[...]).astype(BF)
    back_ref[:, n_q * hd + kc :] = total[:, kc:].astype(BF)
    grad = mm_t(back_ref[...], w_ref[...])
    xhat, _ = apply_norm(x_ref[...].astype(F32))
    gain_ref[...] = jnp.broadcast_to(jnp.sum(grad * xhat, axis=0, keepdims=True), gain_ref.shape)
    put_chunks(grad, outs)


def input_back_call(q_back, terms, x, block, cos, sin, weights, n_q, n_kv, chunks):
    hd = HEAD_SIZE
    seq_dev = q_back.shape[0]
    width = weights.shape[0]
    cols = (n_q + 2 * n_kv) * hd
    part = (seq_dev // chunks, width)
    return call(
        functools.partial(input_back_body, n_q, n_kv, len(terms), chunks),
        (shape((seq_dev, cols), BF), shape((8, width), F32)) + (shape(part, BF),) * chunks,
        (1,),
        [
            whole(q_back.shape),
            pl.BlockSpec((seq_dev, width), lambda i: (block, 0)),
            whole(cos.shape),
            whole(sin.shape),
            pl.BlockSpec((width, cols), lambda i: (0, 0)),
        ]
        + [whole(t.shape) for t in terms],
        (whole((seq_dev, cols)), whole((8, width))) + (whole(part),) * chunks,
        flops=2 * seq_dev * cols * width,
        moved=2 * (width * cols + 3 * seq_dev * width + 4 * seq_dev * cols),
    )(q_back, x, cos, sin, weights, *terms)


def choose(flag_ref, total_ref, third_ref):
    total, third = total_ref[...].astype(F32), third_ref[...].astype(F32)
    return jnp.where(flag_ref[0] == 1, total, third)


def add_gain(gain_ref, rows):
    @pl.when(pl.program_id(0) == 0)
    def _():
        gain_ref[...] = jnp.zeros_like(gain_ref)

    for i, value in enumerate(rows):
        gain_ref[i : i + 1, :] += jnp.sum(value, axis=0, keepdims=True)


def post_attend_body(flag_ref, total_ref, third_ref, x_ref, scale_ref, a_ref, out_ref):
    value = choose(flag_ref, total_ref, third_ref)
    ahat, _ = apply_norm(value)
    h1hat, _ = apply_norm(x_ref[...].astype(F32) + ahat * scale_ref[1:2, :])
    a_ref[...] = value.astype(BF)
    out_ref[...] = (h1hat * scale_ref[2:3, :]).astype(BF)


def post_ffn_body(
    flag_ref, total_ref, third_ref, a_ref, x_ref, dy_ref, scale_ref, out_ref, grad_ref, gain_ref
):
    fhat, factor = apply_norm(choose(flag_ref, total_ref, third_ref))
    ahat, _ = apply_norm(a_ref[...].astype(F32))
    hidden_one = x_ref[...].astype(F32) + ahat * scale_ref[1:2, :]
    scale = scale_ref[3:4, :]
    dy = dy_ref[...].astype(F32)
    out_ref[...] = (hidden_one + fhat * scale).astype(BF)
    grad_ref[...] = norm_backward(dy * scale, fhat, factor).astype(BF)
    add_gain(gain_ref, [dy * fhat])


def post_mid_body(
    flag_ref, total_ref, third_ref, a_ref, x_ref, dy_ref, scale_ref, one_ref, grad_ref, gain_ref
):
    mid = choose(flag_ref, total_ref, third_ref)
    ahat, fac_attn = apply_norm(a_ref[...].astype(F32))
    scale_attn, scale_mid = scale_ref[1:2, :], scale_ref[2:3, :]
    h1hat, fac_mid = apply_norm(x_ref[...].astype(F32) + ahat * scale_attn)
    one_grad = dy_ref[...].astype(F32) + norm_backward(mid * scale_mid, h1hat, fac_mid)
    one_ref[...] = one_grad
    grad_ref[...] = norm_backward(one_grad * scale_attn, ahat, fac_attn).astype(BF)
    add_gain(gain_ref, [mid * h1hat, one_grad * ahat])


def post_in_body(flag_ref, total_ref, third_ref, one_ref, x_ref, scale_ref, out_ref):
    grad = choose(flag_ref, total_ref, third_ref)
    xhat, factor = apply_norm(x_ref[...].astype(F32))
    back = norm_backward(grad * scale_ref[0:1, :], xhat, factor)
    out_ref[...] = (one_ref[...] + back).astype(BF)


def post(body, flag, pair_values, chunk_arrays, row_arrays, k, scales, outs, gain=False):
    rows, width = pair_values[0].shape
    steps = 2 if rows >= 128 else 1
    tile = (rows // steps, width)
    chunk = pl.BlockSpec(tile, lambda i: (i, 0))
    row = pl.BlockSpec(tile, lambda i: (k * steps + i, 0))
    located, located_specs = [], []
    for values in chunk_arrays:
        size = values[0].shape[0]
        base = (k * rows % size) // tile[0]
        located.append(values[k * rows // size])
        located_specs.append(pl.BlockSpec(tile, lambda i, base=base: (base + i, 0)))
    arrays = [flag, *pair_values, *located, *row_arrays, scales]
    specs = [pl.BlockSpec(memory_space=pltpu.SMEM), chunk, chunk, *located_specs]
    specs += [row] * len(row_arrays) + [whole(scales.shape)]
    out_shapes = [shape((rows, width), dtype) for dtype in outs]
    out_specs = [chunk] * len(outs)
    if gain:
        out_shapes.append(shape((8, width), F32))
        out_specs.append(whole((8, width)))
    return call(
        body,
        tuple(out_shapes),
        (steps,),
        specs,
        tuple(out_specs),
        flops=20 * rows * width,
        moved=14 * rows * width,
    )(*arrays)


def ffn_body(n_x, n_out, *refs):
    xs, (wg_ref, wu_ref, wd_ref) = refs[:n_x], refs[n_x : n_x + 3]
    gate_ref, up_ref, hid_ref = refs[n_x + 3 : n_x + 6]
    outs, (x_ref, acc) = refs[n_x + 6 : n_x + 6 + n_out], refs[n_x + 6 + n_out :]
    j = pl.program_id(0)

    @pl.when(j == 0)
    def _():
        gather_rows(xs, x_ref)
        acc[...] = jnp.zeros_like(acc)

    x = x_ref[...]
    gate = mm(x, wg_ref[...])
    up = mm(x, wu_ref[...])
    bend = jnp.tanh(GELU_C * (gate + GELU_A * gate * gate * gate))
    hidden = (0.5 * gate * (1.0 + bend) * up).astype(BF)
    gate_ref[...] = gate.astype(BF)
    up_ref[...] = up.astype(BF)
    hid_ref[...] = hidden
    acc[...] += mm_t(hidden, wd_ref[...])

    @pl.when(j == pl.num_programs(0) - 1)
    def _():
        put_chunks(acc[...], outs)


def gather_rows(pieces, out_ref):
    size = pieces[0].shape[0]
    for i, piece in enumerate(pieces):
        out_ref[i * size : (i + 1) * size, :] = piece[...]


def ffn(xs, weights, ff, n_out):
    width = xs[0].shape[1]
    rows = xs[0].shape[0] * len(xs)
    tile = 256
    steps = ff // tile
    col = lambda part: pl.BlockSpec((width, tile), lambda j: (0, part * steps + j))
    act = pl.BlockSpec((rows, tile), lambda j: (0, j))
    part = (rows // n_out, width)
    return call(
        functools.partial(ffn_body, len(xs), n_out),
        (shape((rows, ff), BF),) * 3 + (shape(part, BF),) * n_out,
        (steps,),
        [whole(xs[0].shape)] * len(xs) + [col(0), col(1), col(2)],
        (act, act, act) + (whole(part),) * n_out,
        [pltpu.VMEM((rows, width), BF), pltpu.VMEM((rows, width), F32)],
        flops=6 * rows * width * ff,
        moved=6 * width * ff + 4 * rows * width + 6 * rows * ff,
    )(*xs, weights, weights, weights)


def ffn_back_body(n_y, n_out, *refs):
    ys, (wg_ref, wu_ref, wd_ref, gate_ref, up_ref) = refs[:n_y], refs[n_y : n_y + 5]
    rest = refs[n_y + 5 :]
    both_ref, outs, (y_ref, acc) = rest[0], rest[1 : 1 + n_out], rest[1 + n_out :]
    tile = gate_ref.shape[1]
    j = pl.program_id(0)

    @pl.when(j == 0)
    def _():
        gather_rows(ys, y_ref)
        acc[...] = jnp.zeros_like(acc)

    grad = mm(y_ref[...], wd_ref[...])
    gate, up = gate_ref[...].astype(F32), up_ref[...].astype(F32)
    square = gate * gate
    bend = jnp.tanh(GELU_C * gate * (1.0 + GELU_A * square))
    rise = 0.5 * (1.0 + bend)
    slope = rise + 0.5 * gate * (1.0 - bend * bend) * (GELU_C * (1.0 + 3.0 * GELU_A * square))
    d_gate = (grad * up * slope).astype(BF)
    d_up = (grad * (gate * rise)).astype(BF)
    both_ref[:, :tile] = d_gate
    both_ref[:, tile:] = d_up
    acc[...] += mm_t(d_gate, wg_ref[...]) + mm_t(d_up, wu_ref[...])

    @pl.when(j == pl.num_programs(0) - 1)
    def _():
        put_chunks(acc[...], outs)


FF_TILE = 256


def ffn_back(ys, weights, gate, up, ff, n_out):
    width = ys[0].shape[1]
    rows = ys[0].shape[0] * len(ys)
    tile = FF_TILE
    steps = ff // tile
    col = lambda part: pl.BlockSpec((width, tile), lambda j: (0, part * steps + j))
    act = pl.BlockSpec((rows, tile), lambda j: (0, j))
    part = (rows // n_out, width)
    return call(
        functools.partial(ffn_back_body, len(ys), n_out),
        (shape((rows, 2 * ff), BF),) + (shape(part, BF),) * n_out,
        (steps,),
        [whole(ys[0].shape)] * len(ys) + [col(0), col(1), col(2), act, act],
        (pl.BlockSpec((rows, 2 * tile), lambda j: (0, j)),) + (whole(part),) * n_out,
        [pltpu.VMEM((rows, width), BF), pltpu.VMEM((rows, width), F32)],
        flops=6 * rows * width * ff,
        moved=6 * width * ff + 4 * rows * width + 8 * rows * ff,
    )(*ys, weights, weights, weights, gate, up)


def sum_body(cuts, part_ref, *outs):
    total = 0.0
    for i in range(part_ref.shape[0]):
        total = total + part_ref[i].astype(F32)
    for out, spans in zip(outs, cuts):
        at = 0
        for start, stop in spans:
            out[:, at : at + stop - start] = total[:, start:stop]
            at += stop - start


def sum_parts(parts, tile, cuts):
    n, rows, cols = parts.shape
    steps = cols // tile
    sizes = [sum(stop - start for start, stop in spans) for spans in cuts]
    return call(
        functools.partial(sum_body, cuts),
        tuple(shape((rows, size * steps), F32) for size in sizes),
        (steps,),
        [pl.BlockSpec((n, rows, tile), lambda j: (0, 0, j))],
        tuple(pl.BlockSpec((rows, size), lambda j: (0, j)) for size in sizes),
        flops=n * rows * cols,
        moved=2 * n * rows * cols + 4 * rows * cols,
    )(parts)


def pack_body(*refs):
    start = 0
    for ref in refs[:-1]:
        refs[-1][:, start : start + ref.shape[1]] = ref[...].astype(BF)
        start += ref.shape[1]


def pack(arrays, steps):
    rows = arrays[0].shape[0] // steps
    cols = sum(a.shape[1] for a in arrays)
    return call(
        pack_body,
        shape((rows * steps, cols), BF),
        (steps,),
        [pl.BlockSpec((rows, a.shape[1]), lambda i: (i, 0)) for a in arrays],
        pl.BlockSpec((rows, cols), lambda i: (i, 0)),
        moved=4 * rows * steps * cols,
    )(*arrays)


class Chain:
    def __init__(self):
        self.token = None

    def after(self, *values):
        if self.token is None:
            return values
        return lax.optimization_barrier((*values, self.token))[:-1]

    def mark(self, value):
        self.token = value
        return value


class Reduce:
    def __init__(self, chain):
        self.chain, self.piece, self.first = chain, {}, {}
        self.sums, self.second, self.total, self.third = {}, {}, {}, {}
        self.line = lax.axis_size("tensor") == 4

    def send(self, k, piece):
        self.piece[k] = piece
        if self.line:
            self.first[k] = lax.ppermute(piece, "tensor", [(0, 1), (3, 2)])
        else:
            self.total[k] = lax.psum(piece.astype(F32), "tensor")

    def add(self, k):
        if self.line:
            piece, first = self.chain.after(self.piece[k], self.first[k])
            total = low(piece.astype(F32) + first.astype(F32))
            self.sums[k] = self.chain.mark(total)
            self.second[k] = lax.ppermute(total, "tensor", [(1, 2), (2, 1)])

    def join(self, k):
        if self.line:
            sums, second = self.chain.after(self.sums[k], self.second[k])
            total = low(sums.astype(F32) + second.astype(F32))
            self.total[k] = self.chain.mark(total)
            self.third[k] = lax.ppermute(total, "tensor", [(1, 0), (2, 3)])

    def load(self, pieces):
        for piece in pieces:
            self.send(len(self.piece), piece)

    def run(self, n, finish, hooks):
        for slot in range(n + 2):
            if slot < n:
                self.add(slot)
            if 0 < slot <= n:
                self.join(slot - 1)
            if slot >= 2:
                finish(slot - 2)
            if slot in hooks:
                hooks[slot]()

    def take(self, k):
        if self.line:
            return self.chain.after(self.total[k], self.third[k])
        return self.chain.after(self.total[k], self.total[k])


def local(
    tokens,
    span_order,
    w_query,
    w_key,
    value_weight,
    w_out,
    w_gate,
    w_up,
    w_down,
    gain_attn_in,
    gain_attn_out,
    gain_ffn_in,
    gain_ffn_out,
    cotangent,
):
    micros, batch, seq_dev, width = tokens.shape
    n_dp, n_ctx, n_t = lax.axis_size("dp"), lax.axis_size("ctx"), lax.axis_size("tensor")
    dpi, ctx, zi = lax.axis_index("dp"), lax.axis_index("ctx"), lax.axis_index("tensor")
    seq = seq_dev * n_ctx
    span_len = seq // span_order.shape[0]
    hd = HEAD_SIZE
    n_kv = w_key.shape[1] // hd
    n_q = w_query.shape[1] // hd
    ff = w_gate.shape[1]
    qc, kc, oc = w_query.shape[1], w_key.shape[1], w_out.shape[1]
    n_seqs, chunks = micros * batch, 2
    swap = n_ctx == 4
    pair = n_dp == 2

    row_index = jnp.arange(seq, dtype=jnp.int32)
    all_pos = span_order[row_index // span_len] * span_len + row_index % span_len
    by_dev = all_pos.reshape(n_ctx, seq_dev)
    query_pos = lax.dynamic_index_in_dim(by_dev, ctx, 0, keepdims=False)
    if swap:
        key_pos = jnp.concatenate(
            [lax.dynamic_index_in_dim(by_dev, ctx ^ j, 0, keepdims=False) for j in range(n_ctx)]
        )
    else:
        key_pos = all_pos
    qpos, kpos = query_pos[:, None], key_pos[None, :]
    cos, sin = rotation(query_pos, hd)

    gains = jnp.stack([gain_attn_in, gain_attn_out, gain_ffn_in, gain_ffn_out], axis=1)
    gains = jnp.pad(gains, ((0, 0), (0, PAD - gains.shape[1])))
    pack_attn = jnp.concatenate([w_query, w_key, value_weight, w_out, gains], axis=1)
    pack_ffn = jnp.concatenate([w_gate, w_up, w_down], axis=1)
    full_attn = lax.all_gather(pack_attn, ("dp", "ctx"), axis=0, tiled=True)
    full_ffn = lax.all_gather(pack_ffn, ("dp", "ctx"), axis=0, tiled=True)
    at_out = qc + 2 * kc
    out_block = at_out // oc
    pick = jnp.eye(8, PAD, dtype=BF)
    gain_cols = mm_t(pick, full_attn[:, at_out + oc :])
    scales = 1.0 + gain_cols

    chain = Chain()
    flips = [[(i, i ^ j) for i in range(n_ctx)] for j in range(n_ctx)]

    def half(full, owner):
        return lax.dynamic_slice_in_dim(full, owner * (width // 2), width // 2, 1)

    def swap_core(value):
        return lax.ppermute(value, "dp", [(0, 1), (1, 0)])

    def left_side(values):
        value = jnp.concatenate(chain.after(*values), axis=0)
        if not pair:
            return value
        return jnp.concatenate([half(value, dpi), swap_core(half(value, 1 - dpi))], axis=0)

    def right_side(values):
        value = jnp.concatenate(chain.after(*values), axis=0)
        return jnp.concatenate([value, swap_core(value)], axis=0) if pair else value

    def spread(grad):
        if pair:
            return lax.all_to_all(grad.reshape(n_ctx, -1, grad.shape[1]), "ctx", 0, 0)
        return lax.psum_scatter(grad, ("dp", "ctx"), scatter_dimension=0, tiled=True)[None]

    def product(left, right):
        left, right = chain.after(left, right)
        return chain.mark(tmm(left, right).astype(BF))

    def scatter(grad):
        axes = "ctx" if pair else ("dp", "ctx")
        return lax.psum_scatter(grad, axes, scatter_dimension=0, tiled=True)[None]

    token_rows = tokens.reshape(n_seqs * seq_dev, width)
    dy_rows = cotangent.reshape(n_seqs * seq_dev, width)
    xhats, _ = apply_norm(token_rows.astype(F32))
    normed = (xhats * scales[0:1]).astype(BF)
    cos_all, sin_all = jnp.tile(cos, (n_seqs, 1)), jnp.tile(sin, (n_seqs, 1))
    qkv = project(normed, full_attn, qc + 2 * kc, n_q + n_kv, cos_all, sin_all)
    kv = qkv[:, qc:]
    if swap:
        others = [lax.ppermute(kv, "ctx", flips[j]) for j in range(1, n_ctx)]
        pieces = [[(a, seq_dev, m, 0) for a in [kv] + others] for m in range(n_seqs)]
    else:
        every = lax.all_gather(kv.reshape(n_seqs, seq_dev, 2 * kc), "ctx", axis=1, tiled=True)
        every = every.reshape(n_seqs * seq, 2 * kc)
        pieces = [[(every, seq, m, 0)] for m in range(n_seqs)]

    def rows_of(value, m):
        return value[m * seq_dev : (m + 1) * seq_dev]

    st = [{}, {}]
    assert n_seqs == 2
    n_one, n_two, n_three, n_four = 4, 4, 4, 4
    inner = ((zi == 1) | (zi == n_t - 2)).astype(jnp.int32).reshape(1)
    attn_outs, normed_two, outputs, ffn_grads = [], [], [], []
    one_grads, attn_grads, input_grads = [], [], []
    gain_fin, gain_mid = [], []

    def post_attend(k):
        values = red.take(k)
        a, n = post(post_attend_body, inner, values, [], [token_rows], k, scales, [BF, BF])
        attn_outs.append(a), normed_two.append(n)
        chain.mark(n)

    def post_ffn(k):
        values, rows = red.take(k), [token_rows, dy_rows]
        out, grad, gain = post(
            post_ffn_body, inner, values, [attn_outs], rows, k, scales, [BF, BF], True
        )
        outputs.append(out), ffn_grads.append(grad), gain_fin.append(gain)
        chain.mark(grad)

    def post_mid(k):
        values, rows = red.take(k), [token_rows, dy_rows]
        one, grad, gain = post(
            post_mid_body, inner, values, [attn_outs], rows, k, scales, [F32, BF], True
        )
        one_grads.append(one), attn_grads.append(grad), gain_mid.append(gain)
        chain.mark(grad)

    def post_in(k):
        values = red.take(k)
        (grad,) = post(post_in_body, inner, values, [one_grads], [token_rows], k, scales, [BF])
        input_grads.append(grad)
        chain.mark(grad)

    def attention(m):
        s = st[m]
        (first, *rest) = chain.after(*[p[0] for p in pieces[m]])
        s["pieces"] = [(v,) + p[1:] for v, p in zip([first, *rest], pieces[m])]
        s["heads"], s["attended"], s["den"], *part = attend(
            qkv, m, s["pieces"], qpos, kpos, n_q, n_kv, full_attn, out_block, n_one // 2
        )
        chain.mark(part[0])
        red.load(part)

    red = Reduce(chain)
    attention(0)
    attention(1)
    red.run(n_one, post_attend, {})

    red = Reduce(chain)
    values = chain.after(*normed_two)
    gate, up, hidden, *part = ffn(list(values), full_ffn, ff, n_two)
    chain.mark(part[0])
    red.load(part)
    held = {}

    def hold(name, make):
        def run():
            held[name] = make()

        return run

    red.run(
        n_two,
        post_ffn,
        {
            0: hold("down_right", lambda: chain.mark(right_side([hidden]))),
            1: hold("mid_left", lambda: chain.mark(left_side(normed_two))),
            2: hold("left", lambda: chain.mark(left_side([normed]))),
        },
    )

    red = Reduce(chain)
    values = chain.after(*ffn_grads)
    d_both, *part = ffn_back(list(values), full_ffn, gate, up, ff, n_three)
    chain.mark(part[0])
    red.load(part)
    both_right = right_side([d_both])
    down_left = left_side(ffn_grads)

    def attention_back(m):
        s = st[m]
        size = n_three // 2
        grads = chain.after(*attn_grads[size * m : size * (m + 1)])
        s["q_back"], *s["terms"] = attend_back(
            qkv,
            m,
            s["pieces"],
            qpos,
            kpos,
            list(grads),
            s["heads"],
            s["den"],
            cos,
            sin,
            n_q,
            n_kv,
            full_attn,
            out_block,
        )
        chain.mark(s["q_back"])
        if swap:
            s["moved"] = [
                lax.ppermute(s["terms"][j].astype(BF), "ctx", flips[j]) for j in range(1, n_ctx)
            ]
        else:
            s["moved"] = [lax.psum_scatter(s["terms"][0], "ctx", scatter_dimension=0, tiled=True)]

    red.run(
        n_three,
        post_mid,
        {
            0: hold("g_down", lambda: scatter(product(down_left, held["down_right"]))),
            1: hold("g_gate_up", lambda: scatter(product(held["mid_left"], both_right))),
            3: lambda: attention_back(0),
        },
    )
    attention_back(1)

    def input_back(m):
        s = st[m]
        moved = list(chain.after(*s["moved"]))
        terms = [s["terms"][0]] + moved if swap else moved
        s["qkv_back"], s["gain"], *part = input_back_call(
            s["q_back"], terms, token_rows, m, cos, sin, full_attn, n_q, n_kv, n_four // 2
        )
        chain.mark(part[0])
        red.load(part)

    def tail():
        d_qkv = product(held["left"], held["right"])
        gain_cols = jnp.stack(
            [
                gain_in[0],
                sum(v[1] for v in gain_mid),
                sum(v[0] for v in gain_mid),
                sum(v[0] for v in gain_fin),
            ],
            axis=1,
        )
        if pair:
            keep = lax.dynamic_slice_in_dim(gain_cols, dpi * (width // 2), width // 2, 0)
            give = lax.dynamic_slice_in_dim(gain_cols, (1 - dpi) * (width // 2), width // 2, 0)
            gain_cols = keep + swap_core(give)
        gain_cols = jnp.pad(gain_cols, ((0, 0), (0, PAD - gain_cols.shape[1])))
        packed = chain.mark(pack(list(chain.after(d_qkv, d_out, gain_cols)), 2))
        held["g_tail"] = spread(packed)

    def finish_down():
        (value,) = chain.after(held["g_down"])
        (held["g_down"],) = sum_parts(value, ff // 3, [[(0, ff // 3)]])
        chain.mark(held["g_down"])

    def finish_both():
        (value,) = chain.after(held["g_gate_up"])
        group = 6 * FF_TILE
        starts = range(0, group, 2 * FF_TILE)
        cuts = [[(i + o, i + o + FF_TILE) for i in starts] for o in (0, FF_TILE)]
        held["g_gate"], held["g_up"] = sum_parts(value, group, cuts)
        chain.mark(held["g_up"])

    def finish_tail():
        (value,) = chain.after(held["g_tail"])
        ends = [0, qc, qc + kc, at_out, at_out + oc, at_out + oc + PAD]
        spans = [[span] for span in zip(ends[:-1], ends[1:])]
        *held["g_attn"], g_gains = sum_parts(value, ends[-1], spans)
        held["g_gains"] = mm_t(pick.astype(F32), g_gains)

    red = Reduce(chain)
    block_out = chain.mark(jnp.concatenate(chain.after(*outputs), axis=0))
    finish_down()
    input_back(0)
    d_out = product(left_side(attn_grads), right_side([s["attended"] for s in st]))
    input_back(1)
    held["right"] = right_side([s["qkv_back"] for s in st])
    gain_in = (st[0]["gain"] + st[1]["gain"])[:4]
    reach = 1
    while reach < n_t:
        steps = [(i, i ^ reach) for i in range(n_t)]
        gain_in = gain_in + lax.ppermute(gain_in, "tensor", steps)
        reach *= 2
    red.run(n_four, post_in, {2: tail, 4: finish_tail})
    finish_both()
    g_gains = held["g_gains"]
    return (
        block_out.reshape(tokens.shape),
        jnp.concatenate(input_grads, axis=0).reshape(tokens.shape),
        *held["g_attn"],
        held["g_gate"],
        held["g_up"],
        held["g_down"],
        g_gains[0],
        g_gains[1],
        g_gains[2],
        g_gains[3],
    )


def solution(mesh):
    act = P(None, "dp", "ctx", None)
    mat = P(("dp", "ctx"), "tensor")
    vec = P(("dp", "ctx"))
    return jax.shard_map(
        local,
        mesh=mesh,
        in_specs=(act, P()) + (mat,) * 7 + (vec,) * 4 + (act,),
        out_specs=(act, act) + (mat,) * 7 + (vec,) * 4,
        check_vma=False,
    )
```

```python
import functools

import jax
import jax.numpy as jnp
from jax import lax
from jax.experimental import pallas as pl
from jax.experimental.pallas import tpu as pltpu
from jax.sharding import PartitionSpec as P

HEAD_SIZE = 256
EPS = 1e-06
CAP = 50.0
BASE = 10000.0
BF = jnp.bfloat16
F32 = jnp.float32
PAD = 128
VMEM_LIMIT = 60 * 1024 * 1024
GELU_C = 0.7978845608028654
GELU_A = 0.044715


def apply_norm(values):
    factor = lax.rsqrt(jnp.mean(values * values, axis=-1, keepdims=True) + EPS)
    return values * factor, factor


def norm_backward(upstream, scaled, factor):
    return factor * (upstream - scaled * jnp.mean(upstream * scaled, axis=-1, keepdims=True))


def rotation(token_positions, width_size):
    half_width = width_size // 2
    inverse = BASE ** (-(jnp.arange(half_width, dtype=F32) * 2.0) / width_size)
    angles = token_positions.astype(F32)[:, None] * inverse[None, :]
    return jnp.cos(angles), jnp.sin(angles)


def mm(a, b):
    return jnp.dot(a, b, preferred_element_type=F32)


def mm_t(a, b):
    return lax.dot_general(a, b, (((1,), (1,)), ((), ())), preferred_element_type=F32)


def tmm(a, b):
    return lax.dot_general(a, b, (((0,), (0,)), ((), ())), preferred_element_type=F32)


def low(values):
    return lax.reduce_precision(values, 8, 7).astype(BF)


def call(body, out_shape, grid, in_specs, out_specs, scratch=(), flops=0, moved=0):
    return pl.pallas_call(
        body,
        out_shape=out_shape,
        grid_spec=pltpu.PrefetchScalarGridSpec(
            num_scalar_prefetch=0,
            grid=grid,
            in_specs=in_specs,
            out_specs=out_specs,
            scratch_shapes=list(scratch),
        ),
        compiler_params=pltpu.CompilerParams(
            dimension_semantics=("arbitrary",) * len(grid), vmem_limit_bytes=VMEM_LIMIT
        ),
        cost_estimate=pl.CostEstimate(flops=flops, bytes_accessed=moved, transcendentals=0),
    )


def shape(dims, dtype):
    return jax.ShapeDtypeStruct(dims, dtype)


def whole(dims):
    return pl.BlockSpec(dims, lambda *_: (0,) * len(dims))


def project_body(n_rot, x_ref, w_ref, cos_ref, sin_ref, out_ref):
    half = HEAD_SIZE // 2
    y = mm(x_ref[...], w_ref[...])
    rotate = pl.program_id(0) < n_rot
    cos = jnp.where(rotate, cos_ref[...], 1.0)
    sin = jnp.where(rotate, sin_ref[...], 0.0)
    a, b = y[:, :half], y[:, half:]
    out_ref[:, :half] = (a * cos - b * sin).astype(BF)
    out_ref[:, half:] = (b * cos + a * sin).astype(BF)


def project(normed, weights, columns, n_rot, cos, sin):
    rows, width = normed.shape
    return call(
        functools.partial(project_body, n_rot),
        shape((rows, columns), BF),
        (columns // HEAD_SIZE,),
        [
            whole((rows, width)),
            pl.BlockSpec((width, HEAD_SIZE), lambda j: (0, j)),
            whole(cos.shape),
            whole(sin.shape),
        ],
        pl.BlockSpec((rows, HEAD_SIZE), lambda j: (0, j)),
        flops=2 * rows * width * columns,
        moved=2 * (rows * width + width * columns + rows * columns),
    )(normed, weights, cos, sin)


def scores(q, k, allowed):
    soft = HEAD_SIZE ** (-0.5)
    bend = jnp.tanh(mm_t(q, k) * (soft / CAP))
    return bend, jnp.where(allowed, jnp.exp(CAP * bend), 0.0)


def attend_body(n_q, n_kv, n_pieces, chunks, *refs):
    hd = HEAD_SIZE
    q_ref, qpos_ref, kpos_ref, w_ref = refs[:4]
    pieces = refs[4 : 4 + n_pieces]
    heads_ref, attended_ref, den_ref = refs[4 + n_pieces : 7 + n_pieces]
    outs = refs[7 + n_pieces :]
    qpos = qpos_ref[...]
    for h in range(n_q):
        kv = h // (n_q // n_kv)
        q = q_ref[:, h * hd : (h + 1) * hd]
        num, den = 0.0, 0.0
        for j, piece in enumerate(pieces):
            size = piece.shape[0]
            allowed = kpos_ref[:, j * size : (j + 1) * size] <= qpos
            _, weight = scores(q, piece[:, kv * hd : (kv + 1) * hd], allowed)
            den = den + jnp.sum(weight, axis=-1, keepdims=True)
            v = piece[:, (n_kv + kv) * hd : (n_kv + kv + 1) * hd]
            num = num + mm(weight.astype(BF), v)
        heads = num / den
        heads_ref[:, h * hd : (h + 1) * hd] = heads
        attended_ref[:, h * hd : (h + 1) * hd] = heads.astype(BF)
        den_ref[:, h * PAD : (h + 1) * PAD] = jnp.broadcast_to(den, (den.shape[0], PAD))
    put_chunks(mm_t(attended_ref[...], w_ref[...]), outs)


def put_chunks(value, outs):
    size = value.shape[0] // len(outs)
    for i, out in enumerate(outs):
        out[...] = value[i * size : (i + 1) * size].astype(BF)


def attend(q, q_block, pieces, qpos, kpos, n_q, n_kv, weights, out_block, chunks):
    hd = HEAD_SIZE
    seq_dev = qpos.shape[0]
    width = weights.shape[0]
    specs = [pl.BlockSpec((seq_dev, n_q * hd), lambda i: (q_block, 0))]
    specs += [whole(qpos.shape), whole(kpos.shape)]
    specs.append(pl.BlockSpec((width, n_q * hd), lambda i: (0, out_block)))
    arrays = [q, qpos, kpos, weights]
    for array, size, row, col in pieces:
        specs.append(pl.BlockSpec((size, 2 * n_kv * hd), lambda i, row=row, col=col: (row, col)))
        arrays.append(array)
    seq = kpos.shape[1]
    part = (seq_dev // chunks, width)
    return call(
        functools.partial(attend_body, n_q, n_kv, len(pieces), chunks),
        (
            shape((seq_dev, n_q * hd), F32),
            shape((seq_dev, n_q * hd), BF),
            shape((seq_dev, n_q * PAD), F32),
        )
        + (shape(part, BF),) * chunks,
        (1,),
        specs,
        (whole((seq_dev, n_q * hd)), whole((seq_dev, n_q * hd)), whole((seq_dev, n_q * PAD)))
        + (whole(part),) * chunks,
        flops=4 * n_q * seq_dev * seq * hd + 2 * seq_dev * n_q * hd * width,
        moved=2 * (2 * n_kv * hd * seq + 4 * seq_dev * n_q * hd + 2 * n_q * hd * width),
    )(*arrays)


def attend_back_body(n_q, n_kv, n_pieces, chunks, *refs):
    hd = HEAD_SIZE
    half = hd // 2
    soft = hd ** (-0.5)
    q_ref, qpos_ref, kpos_ref, heads_ref, den_ref, cos_ref, sin_ref, w_ref = refs[:8]
    pieces = refs[8 : 8 + n_pieces]
    grads = refs[8 + n_pieces : 8 + n_pieces + chunks]
    q_back_ref, *outs = refs[8 + n_pieces + chunks :]
    attn_grad = jnp.concatenate([g[...] for g in grads], axis=0)
    qpos = qpos_ref[...]
    group = n_q // n_kv
    for h in range(n_q):
        kv = h // group
        cols = slice(h * hd, (h + 1) * hd)
        k_cols = slice(kv * hd, (kv + 1) * hd)
        v_cols = slice((n_kv + kv) * hd, (n_kv + kv + 1) * hd)
        q = q_ref[:, cols]
        grad = mm(attn_grad, w_ref[:, cols])
        inverse = 1.0 / den_ref[:, h * PAD : h * PAD + 1]
        scaled = (grad * inverse).astype(BF)
        row_dot = jnp.sum(grad * heads_ref[:, cols], axis=-1, keepdims=True) * inverse
        q_grad = 0.0
        for j, piece in enumerate(pieces):
            size = piece.shape[0]
            allowed = kpos_ref[:, j * size : (j + 1) * size] <= qpos
            k, v = piece[:, k_cols], piece[:, v_cols]
            bend, weight = scores(q, k, allowed)
            prob = mm_t(scaled, v)
            score = (weight * (prob - row_dot) * (1.0 - bend * bend)).astype(BF)
            q_grad = q_grad + mm(score, k)
            k_term = tmm(score, q) * soft
            v_term = tmm(weight.astype(BF), scaled)
            if h % group == 0:
                outs[j][:, k_cols] = k_term
                outs[j][:, v_cols] = v_term
            else:
                outs[j][:, k_cols] += k_term
                outs[j][:, v_cols] += v_term
        q_grad = q_grad * soft
        a, b = q_grad[:, :half], q_grad[:, half:]
        q_back_ref[:, h * hd : h * hd + half] = (a * cos_ref[...] + b * sin_ref[...]).astype(BF)
        q_back_ref[:, h * hd + half : (h + 1) * hd] = (
            b * cos_ref[...] - a * sin_ref[...]
        ).astype(BF)


def attend_back(q, q_block, pieces, qpos, kpos, grads, heads, den, cos, sin, n_q, n_kv, weights, out_block):
    hd = HEAD_SIZE
    seq_dev = qpos.shape[0]
    width = weights.shape[0]
    specs = [pl.BlockSpec((seq_dev, n_q * hd), lambda i: (q_block, 0))]
    arrays = [q, qpos, kpos, heads, den, cos, sin]
    specs += [whole(a.shape) for a in arrays[1:]]
    specs.append(pl.BlockSpec((width, n_q * hd), lambda i: (0, out_block)))
    arrays.append(weights)
    out_shapes, out_specs = [shape((seq_dev, n_q * hd), BF)], [whole((seq_dev, n_q * hd))]
    for array, size, row, col in pieces:
        specs.append(pl.BlockSpec((size, 2 * n_kv * hd), lambda i, row=row, col=col: (row, col)))
        arrays.append(array)
        out_shapes.append(shape((size, 2 * n_kv * hd), F32))
        out_specs.append(whole((size, 2 * n_kv * hd)))
    arrays += grads
    specs += [whole(g.shape) for g in grads]
    seq = kpos.shape[1]
    return call(
        functools.partial(attend_back_body, n_q, n_kv, len(pieces), len(grads)),
        tuple(out_shapes),
        (1,),
        specs,
        tuple(out_specs),
        flops=10 * n_q * seq_dev * seq * hd + 2 * seq_dev * n_q * hd * width,
        moved=2 * (6 * n_kv * hd * seq + 8 * seq_dev * n_q * hd + 2 * n_q * hd * width),
    )(*arrays)


def input_back_body(n_q, n_kv, n_terms, chunks, *refs):
    hd = HEAD_SIZE
    half = hd // 2
    kc = n_kv * hd
    q_back_ref, x_ref, cos_ref, sin_ref, w_ref = refs[:5]
    terms = refs[5 : 5 + n_terms]
    back_ref, gain_ref, *outs = refs[5 + n_terms :]
    total = 0.0
    for term in terms:
        total = total + term[...].astype(F32)
    back_ref[:, : n_q * hd] = q_back_ref[...]
    for h in range(n_kv):
        start = (n_q + h) * hd
        a = total[:, h * hd : h * hd + half]
        b = total[:, h * hd + half : (h + 1) * hd]
        back_ref[:, start : start + half] = (a * cos_ref[...] + b * sin_ref[...]).astype(BF)
        back_ref[:, start + half : start + hd] = (b * cos_ref[...] - a * sin_ref[...]).astype(BF)
    back_ref[:, n_q * hd + kc :] = total[:, kc:].astype(BF)
    grad = mm_t(back_ref[...], w_ref[...])
    xhat, _ = apply_norm(x_ref[...].astype(F32))
    gain_ref[...] = jnp.broadcast_to(jnp.sum(grad * xhat, axis=0, keepdims=True), gain_ref.shape)
    put_chunks(grad, outs)


def input_back_call(q_back, terms, x, block, cos, sin, weights, n_q, n_kv, chunks):
    hd = HEAD_SIZE
    seq_dev = q_back.shape[0]
    width = weights.shape[0]
    cols = (n_q + 2 * n_kv) * hd
    part = (seq_dev // chunks, width)
    return call(
        functools.partial(input_back_body, n_q, n_kv, len(terms), chunks),
        (shape((seq_dev, cols), BF), shape((8, width), F32)) + (shape(part, BF),) * chunks,
        (1,),
        [
            whole(q_back.shape),
            pl.BlockSpec((seq_dev, width), lambda i: (block, 0)),
            whole(cos.shape),
            whole(sin.shape),
            pl.BlockSpec((width, cols), lambda i: (0, 0)),
        ]
        + [whole(t.shape) for t in terms],
        (whole((seq_dev, cols)), whole((8, width))) + (whole(part),) * chunks,
        flops=2 * seq_dev * cols * width,
        moved=2 * (width * cols + 3 * seq_dev * width + 4 * seq_dev * cols),
    )(q_back, x, cos, sin, weights, *terms)


def choose(flag_ref, total_ref, third_ref):
    total, third = total_ref[...].astype(F32), third_ref[...].astype(F32)
    return jnp.where(flag_ref[0] == 1, total, third)


def add_gain(gain_ref, rows):
    @pl.when(pl.program_id(0) == 0)
    def _():
        gain_ref[...] = jnp.zeros_like(gain_ref)

    for i, value in enumerate(rows):
        gain_ref[i : i + 1, :] += jnp.sum(value, axis=0, keepdims=True)


def post_attend_body(flag_ref, total_ref, third_ref, x_ref, scale_ref, a_ref, out_ref):
    value = choose(flag_ref, total_ref, third_ref)
    ahat, _ = apply_norm(value)
    h1hat, _ = apply_norm(x_ref[...].astype(F32) + ahat * scale_ref[1:2, :])
    a_ref[...] = value.astype(BF)
    out_ref[...] = (h1hat * scale_ref[2:3, :]).astype(BF)


def post_ffn_body(
    flag_ref, total_ref, third_ref, a_ref, x_ref, dy_ref, scale_ref, out_ref, grad_ref, gain_ref
):
    fhat, factor = apply_norm(choose(flag_ref, total_ref, third_ref))
    ahat, _ = apply_norm(a_ref[...].astype(F32))
    hidden_one = x_ref[...].astype(F32) + ahat * scale_ref[1:2, :]
    scale = scale_ref[3:4, :]
    dy = dy_ref[...].astype(F32)
    out_ref[...] = (hidden_one + fhat * scale).astype(BF)
    grad_ref[...] = norm_backward(dy * scale, fhat, factor).astype(BF)
    add_gain(gain_ref, [dy * fhat])


def post_mid_body(
    flag_ref, total_ref, third_ref, a_ref, x_ref, dy_ref, scale_ref, one_ref, grad_ref, gain_ref
):
    mid = choose(flag_ref, total_ref, third_ref)
    ahat, fac_attn = apply_norm(a_ref[...].astype(F32))
    scale_attn, scale_mid = scale_ref[1:2, :], scale_ref[2:3, :]
    h1hat, fac_mid = apply_norm(x_ref[...].astype(F32) + ahat * scale_attn)
    one_grad = dy_ref[...].astype(F32) + norm_backward(mid * scale_mid, h1hat, fac_mid)
    one_ref[...] = one_grad
    grad_ref[...] = norm_backward(one_grad * scale_attn, ahat, fac_attn).astype(BF)
    add_gain(gain_ref, [mid * h1hat, one_grad * ahat])


def post_in_body(flag_ref, total_ref, third_ref, one_ref, x_ref, scale_ref, out_ref):
    grad = choose(flag_ref, total_ref, third_ref)
    xhat, factor = apply_norm(x_ref[...].astype(F32))
    back = norm_backward(grad * scale_ref[0:1, :], xhat, factor)
    out_ref[...] = (one_ref[...] + back).astype(BF)


def post(body, flag, pair_values, chunk_arrays, row_arrays, k, scales, outs, gain=False):
    rows, width = pair_values[0].shape
    steps = 2 if rows >= 128 else 1
    tile = (rows // steps, width)
    chunk = pl.BlockSpec(tile, lambda i: (i, 0))
    row = pl.BlockSpec(tile, lambda i: (k * steps + i, 0))
    located, located_specs = [], []
    for values in chunk_arrays:
        size = values[0].shape[0]
        base = (k * rows % size) // tile[0]
        located.append(values[k * rows // size])
        located_specs.append(pl.BlockSpec(tile, lambda i, base=base: (base + i, 0)))
    arrays = [flag, *pair_values, *located, *row_arrays, scales]
    specs = [pl.BlockSpec(memory_space=pltpu.SMEM), chunk, chunk, *located_specs]
    specs += [row] * len(row_arrays) + [whole(scales.shape)]
    out_shapes = [shape((rows, width), dtype) for dtype in outs]
    out_specs = [chunk] * len(outs)
    if gain:
        out_shapes.append(shape((8, width), F32))
        out_specs.append(whole((8, width)))
    return call(
        body,
        tuple(out_shapes),
        (steps,),
        specs,
        tuple(out_specs),
        flops=20 * rows * width,
        moved=14 * rows * width,
    )(*arrays)


def ffn_body(n_x, n_out, *refs):
    xs, (wg_ref, wu_ref, wd_ref) = refs[:n_x], refs[n_x : n_x + 3]
    gate_ref, up_ref, hid_ref = refs[n_x + 3 : n_x + 6]
    outs, (x_ref, acc) = refs[n_x + 6 : n_x + 6 + n_out], refs[n_x + 6 + n_out :]
    j = pl.program_id(0)

    @pl.when(j == 0)
    def _():
        gather_rows(xs, x_ref)
        acc[...] = jnp.zeros_like(acc)

    x = x_ref[...]
    gate = mm(x, wg_ref[...])
    up = mm(x, wu_ref[...])
    bend = jnp.tanh(GELU_C * (gate + GELU_A * gate * gate * gate))
    hidden = (0.5 * gate * (1.0 + bend) * up).astype(BF)
    gate_ref[...] = gate.astype(BF)
    up_ref[...] = up.astype(BF)
    hid_ref[...] = hidden
    acc[...] += mm_t(hidden, wd_ref[...])

    @pl.when(j == pl.num_programs(0) - 1)
    def _():
        put_chunks(acc[...], outs)


def gather_rows(pieces, out_ref):
    size = pieces[0].shape[0]
    for i, piece in enumerate(pieces):
        out_ref[i * size : (i + 1) * size, :] = piece[...]


def ffn(xs, weights, ff, n_out):
    width = xs[0].shape[1]
    rows = xs[0].shape[0] * len(xs)
    tile = 256
    steps = ff // tile
    col = lambda part: pl.BlockSpec((width, tile), lambda j: (0, part * steps + j))
    act = pl.BlockSpec((rows, tile), lambda j: (0, j))
    part = (rows // n_out, width)
    return call(
        functools.partial(ffn_body, len(xs), n_out),
        (shape((rows, ff), BF),) * 3 + (shape(part, BF),) * n_out,
        (steps,),
        [whole(xs[0].shape)] * len(xs) + [col(0), col(1), col(2)],
        (act, act, act) + (whole(part),) * n_out,
        [pltpu.VMEM((rows, width), BF), pltpu.VMEM((rows, width), F32)],
        flops=6 * rows * width * ff,
        moved=6 * width * ff + 4 * rows * width + 6 * rows * ff,
    )(*xs, weights, weights, weights)


def ffn_back_body(n_y, n_out, *refs):
    ys, (wg_ref, wu_ref, wd_ref, gate_ref, up_ref) = refs[:n_y], refs[n_y : n_y + 5]
    rest = refs[n_y + 5 :]
    both_ref, outs, (y_ref, acc) = rest[0], rest[1 : 1 + n_out], rest[1 + n_out :]
    tile = gate_ref.shape[1]
    j = pl.program_id(0)

    @pl.when(j == 0)
    def _():
        gather_rows(ys, y_ref)
        acc[...] = jnp.zeros_like(acc)

    grad = mm(y_ref[...], wd_ref[...])
    gate, up = gate_ref[...].astype(F32), up_ref[...].astype(F32)
    square = gate * gate
    bend = jnp.tanh(GELU_C * gate * (1.0 + GELU_A * square))
    rise = 0.5 * (1.0 + bend)
    slope = rise + 0.5 * gate * (1.0 - bend * bend) * (GELU_C * (1.0 + 3.0 * GELU_A * square))
    d_gate = (grad * up * slope).astype(BF)
    d_up = (grad * (gate * rise)).astype(BF)
    both_ref[:, :tile] = d_gate
    both_ref[:, tile:] = d_up
    acc[...] += mm_t(d_gate, wg_ref[...]) + mm_t(d_up, wu_ref[...])

    @pl.when(j == pl.num_programs(0) - 1)
    def _():
        put_chunks(acc[...], outs)


FF_TILE = 256


def ffn_back(ys, weights, gate, up, ff, n_out):
    width = ys[0].shape[1]
    rows = ys[0].shape[0] * len(ys)
    tile = FF_TILE
    steps = ff // tile
    col = lambda part: pl.BlockSpec((width, tile), lambda j: (0, part * steps + j))
    act = pl.BlockSpec((rows, tile), lambda j: (0, j))
    part = (rows // n_out, width)
    return call(
        functools.partial(ffn_back_body, len(ys), n_out),
        (shape((rows, 2 * ff), BF),) + (shape(part, BF),) * n_out,
        (steps,),
        [whole(ys[0].shape)] * len(ys) + [col(0), col(1), col(2), act, act],
        (pl.BlockSpec((rows, 2 * tile), lambda j: (0, j)),) + (whole(part),) * n_out,
        [pltpu.VMEM((rows, width), BF), pltpu.VMEM((rows, width), F32)],
        flops=6 * rows * width * ff,
        moved=6 * width * ff + 4 * rows * width + 8 * rows * ff,
    )(*ys, weights, weights, weights, gate, up)


def sum_body(cuts, part_ref, *outs):
    total = 0.0
    for i in range(part_ref.shape[0]):
        total = total + part_ref[i].astype(F32)
    for out, spans in zip(outs, cuts):
        at = 0
        for start, stop in spans:
            out[:, at : at + stop - start] = total[:, start:stop]
            at += stop - start


def sum_parts(parts, tile, cuts):
    n, rows, cols = parts.shape
    steps = cols // tile
    sizes = [sum(stop - start for start, stop in spans) for spans in cuts]
    return call(
        functools.partial(sum_body, cuts),
        tuple(shape((rows, size * steps), F32) for size in sizes),
        (steps,),
        [pl.BlockSpec((n, rows, tile), lambda j: (0, 0, j))],
        tuple(pl.BlockSpec((rows, size), lambda j: (0, j)) for size in sizes),
        flops=n * rows * cols,
        moved=2 * n * rows * cols + 4 * rows * cols,
    )(parts)


def pack_body(*refs):
    start = 0
    for ref in refs[:-1]:
        refs[-1][:, start : start + ref.shape[1]] = ref[...].astype(BF)
        start += ref.shape[1]


def pack(arrays, steps):
    rows = arrays[0].shape[0] // steps
    cols = sum(a.shape[1] for a in arrays)
    return call(
        pack_body,
        shape((rows * steps, cols), BF),
        (steps,),
        [pl.BlockSpec((rows, a.shape[1]), lambda i: (i, 0)) for a in arrays],
        pl.BlockSpec((rows, cols), lambda i: (i, 0)),
        moved=4 * rows * steps * cols,
    )(*arrays)


class Chain:
    def __init__(self):
        self.token = None

    def after(self, *values):
        if self.token is None:
            return values
        return lax.optimization_barrier((*values, self.token))[:-1]

    def mark(self, value):
        self.token = value
        return value


class Reduce:
    def __init__(self, chain):
        self.chain, self.piece, self.first = chain, {}, {}
        self.sums, self.second, self.total, self.third = {}, {}, {}, {}
        self.line = lax.axis_size("tensor") == 4

    def send(self, k, piece):
        self.piece[k] = piece
        if self.line:
            self.first[k] = lax.ppermute(piece, "tensor", [(0, 1), (3, 2)])
        else:
            self.total[k] = lax.psum(piece.astype(F32), "tensor")

    def add(self, k):
        if self.line:
            piece, first = self.chain.after(self.piece[k], self.first[k])
            total = low(piece.astype(F32) + first.astype(F32))
            self.sums[k] = self.chain.mark(total)
            self.second[k] = lax.ppermute(total, "tensor", [(1, 2), (2, 1)])

    def join(self, k):
        if self.line:
            sums, second = self.chain.after(self.sums[k], self.second[k])
            total = low(sums.astype(F32) + second.astype(F32))
            self.total[k] = self.chain.mark(total)
            self.third[k] = lax.ppermute(total, "tensor", [(1, 0), (2, 3)])

    def load(self, pieces):
        for piece in pieces:
            self.send(len(self.piece), piece)

    def run(self, n, finish, hooks):
        for slot in range(n + 2):
            if slot < n:
                self.add(slot)
            if 0 < slot <= n:
                self.join(slot - 1)
            if slot >= 2:
                finish(slot - 2)
            if slot in hooks:
                hooks[slot]()

    def take(self, k):
        if self.line:
            return self.chain.after(self.total[k], self.third[k])
        return self.chain.after(self.total[k], self.total[k])


def local(
    tokens,
    span_order,
    w_query,
    w_key,
    value_weight,
    w_out,
    w_gate,
    w_up,
    w_down,
    gain_attn_in,
    gain_attn_out,
    gain_ffn_in,
    gain_ffn_out,
    cotangent,
):
    micros, batch, seq_dev, width = tokens.shape
    n_dp, n_ctx, n_t = lax.axis_size("dp"), lax.axis_size("ctx"), lax.axis_size("tensor")
    dpi, ctx, zi = lax.axis_index("dp"), lax.axis_index("ctx"), lax.axis_index("tensor")
    seq = seq_dev * n_ctx
    span_len = seq // span_order.shape[0]
    hd = HEAD_SIZE
    n_kv = w_key.shape[1] // hd
    n_q = w_query.shape[1] // hd
    ff = w_gate.shape[1]
    qc, kc, oc = w_query.shape[1], w_key.shape[1], w_out.shape[1]
    n_seqs, chunks = micros * batch, 2
    swap = n_ctx == 4
    pair = n_dp == 2

    row_index = jnp.arange(seq, dtype=jnp.int32)
    all_pos = span_order[row_index // span_len] * span_len + row_index % span_len
    by_dev = all_pos.reshape(n_ctx, seq_dev)
    query_pos = lax.dynamic_index_in_dim(by_dev, ctx, 0, keepdims=False)
    if swap:
        key_pos = jnp.concatenate(
            [lax.dynamic_index_in_dim(by_dev, ctx ^ j, 0, keepdims=False) for j in range(n_ctx)]
        )
    else:
        key_pos = all_pos
    qpos, kpos = query_pos[:, None], key_pos[None, :]
    cos, sin = rotation(query_pos, hd)

    gains = jnp.stack([gain_attn_in, gain_attn_out, gain_ffn_in, gain_ffn_out], axis=1)
    gains = jnp.pad(gains, ((0, 0), (0, PAD - gains.shape[1])))
    pack_attn = jnp.concatenate([w_query, w_key, value_weight, w_out, gains], axis=1)
    pack_ffn = jnp.concatenate([w_gate, w_up, w_down], axis=1)
    full_attn = lax.all_gather(pack_attn, ("dp", "ctx"), axis=0, tiled=True)
    full_ffn = lax.all_gather(pack_ffn, ("dp", "ctx"), axis=0, tiled=True)
    at_out = qc + 2 * kc
    out_block = at_out // oc
    pick = jnp.eye(8, PAD, dtype=BF)
    gain_cols = mm_t(pick, full_attn[:, at_out + oc :])
    scales = 1.0 + gain_cols

    chain = Chain()
    flips = [[(i, i ^ j) for i in range(n_ctx)] for j in range(n_ctx)]

    def half(full, owner):
        return lax.dynamic_slice_in_dim(full, owner * (width // 2), width // 2, 1)

    def swap_core(value):
        return lax.ppermute(value, "dp", [(0, 1), (1, 0)])

    def left_side(values):
        value = jnp.concatenate(chain.after(*values), axis=0)
        if not pair:
            return value
        return jnp.concatenate([half(value, dpi), swap_core(half(value, 1 - dpi))], axis=0)

    def right_side(values):
        value = jnp.concatenate(chain.after(*values), axis=0)
        return jnp.concatenate([value, swap_core(value)], axis=0) if pair else value

    def spread(grad):
        if pair:
            return lax.all_to_all(grad.reshape(n_ctx, -1, grad.shape[1]), "ctx", 0, 0)
        return lax.psum_scatter(grad, ("dp", "ctx"), scatter_dimension=0, tiled=True)[None]

    def product(left, right):
        left, right = chain.after(left, right)
        return chain.mark(tmm(left, right).astype(BF))

    def scatter(grad):
        axes = "ctx" if pair else ("dp", "ctx")
        return lax.psum_scatter(grad, axes, scatter_dimension=0, tiled=True)[None]

    token_rows = tokens.reshape(n_seqs * seq_dev, width)
    dy_rows = cotangent.reshape(n_seqs * seq_dev, width)
    xhats, _ = apply_norm(token_rows.astype(F32))
    normed = (xhats * scales[0:1]).astype(BF)
    cos_all, sin_all = jnp.tile(cos, (n_seqs, 1)), jnp.tile(sin, (n_seqs, 1))
    qkv = project(normed, full_attn, qc + 2 * kc, n_q + n_kv, cos_all, sin_all)
    kv = qkv[:, qc:]
    if swap:
        others = [lax.ppermute(kv, "ctx", flips[j]) for j in range(1, n_ctx)]
        pieces = [[(a, seq_dev, m, 0) for a in [kv] + others] for m in range(n_seqs)]
    else:
        every = lax.all_gather(kv.reshape(n_seqs, seq_dev, 2 * kc), "ctx", axis=1, tiled=True)
        every = every.reshape(n_seqs * seq, 2 * kc)
        pieces = [[(every, seq, m, 0)] for m in range(n_seqs)]

    def rows_of(value, m):
        return value[m * seq_dev : (m + 1) * seq_dev]

    st = [{}, {}]
    assert n_seqs == 2
    n_one, n_two, n_three, n_four = 4, 4, 4, 4
    inner = ((zi == 1) | (zi == n_t - 2)).astype(jnp.int32).reshape(1)
    attn_outs, normed_two, outputs, ffn_grads = [], [], [], []
    one_grads, attn_grads, input_grads = [], [], []
    gain_fin, gain_mid = [], []

    def post_attend(k):
        values = red.take(k)
        a, n = post(post_attend_body, inner, values, [], [token_rows], k, scales, [BF, BF])
        attn_outs.append(a), normed_two.append(n)
        chain.mark(n)

    def post_ffn(k):
        values, rows = red.take(k), [token_rows, dy_rows]
        out, grad, gain = post(
            post_ffn_body, inner, values, [attn_outs], rows, k, scales, [BF, BF], True
        )
        outputs.append(out), ffn_grads.append(grad), gain_fin.append(gain)
        chain.mark(grad)

    def post_mid(k):
        values, rows = red.take(k), [token_rows, dy_rows]
        one, grad, gain = post(
            post_mid_body, inner, values, [attn_outs], rows, k, scales, [F32, BF], True
        )
        one_grads.append(one), attn_grads.append(grad), gain_mid.append(gain)
        chain.mark(grad)

    def post_in(k):
        values = red.take(k)
        (grad,) = post(post_in_body, inner, values, [one_grads], [token_rows], k, scales, [BF])
        input_grads.append(grad)
        chain.mark(grad)

    def attention(m):
        s = st[m]
        (first, *rest) = chain.after(*[p[0] for p in pieces[m]])
        s["pieces"] = [(v,) + p[1:] for v, p in zip([first, *rest], pieces[m])]
        s["heads"], s["attended"], s["den"], *part = attend(
            qkv, m, s["pieces"], qpos, kpos, n_q, n_kv, full_attn, out_block, n_one // 2
        )
        chain.mark(part[0])
        red.load(part)

    red = Reduce(chain)
    attention(0)
    attention(1)
    held = {}

    def hold(name, make):
        def run():
            held[name] = make()

        return run

    red.run(
        n_one, post_attend, {n_one + 1: hold("left", lambda: chain.mark(left_side([normed])))}
    )

    red = Reduce(chain)
    values = chain.after(*normed_two)
    gate, up, hidden, *part = ffn(list(values), full_ffn, ff, n_two)
    chain.mark(part[0])
    red.load(part)
    red.run(
        n_two,
        post_ffn,
        {
            0: hold("down_right", lambda: right_side([hidden])),
            1: hold("mid_left", lambda: left_side(normed_two)),
        },
    )

    red = Reduce(chain)
    values = chain.after(*ffn_grads)
    d_both, *part = ffn_back(list(values), full_ffn, gate, up, ff, n_three)
    chain.mark(part[0])
    red.load(part)
    both_right = right_side([d_both])
    down_left = left_side(ffn_grads)

    def attention_back(m):
        s = st[m]
        size = n_three // 2
        grads = chain.after(*attn_grads[size * m : size * (m + 1)])
        s["q_back"], *s["terms"] = attend_back(
            qkv,
            m,
            s["pieces"],
            qpos,
            kpos,
            list(grads),
            s["heads"],
            s["den"],
            cos,
            sin,
            n_q,
            n_kv,
            full_attn,
            out_block,
        )
        chain.mark(s["q_back"])
        if swap:
            s["moved"] = [
                lax.ppermute(s["terms"][j].astype(BF), "ctx", flips[j]) for j in range(1, n_ctx)
            ]
        else:
            s["moved"] = [lax.psum_scatter(s["terms"][0], "ctx", scatter_dimension=0, tiled=True)]

    red.run(
        n_three,
        post_mid,
        {
            0: hold("g_down", lambda: scatter(product(down_left, held["down_right"]))),
            1: hold("g_gate_up", lambda: scatter(product(held["mid_left"], both_right))),
            3: lambda: attention_back(0),
        },
    )
    attention_back(1)

    def input_back(m):
        s = st[m]
        moved = list(chain.after(*s["moved"]))
        terms = [s["terms"][0]] + moved if swap else moved
        s["qkv_back"], s["gain"], *part = input_back_call(
            s["q_back"], terms, token_rows, m, cos, sin, full_attn, n_q, n_kv, n_four // 2
        )
        chain.mark(part[0])
        red.load(part)

    def tail():
        d_qkv = product(held["left"], held["right"])
        owner = zi == 0
        gain_cols = jnp.stack(
            [
                st[0]["gain"][0] + st[1]["gain"][0],
                jnp.where(owner, sum(v[1] for v in gain_mid), 0.0),
                jnp.where(owner, sum(v[0] for v in gain_mid), 0.0),
                jnp.where(owner, sum(v[0] for v in gain_fin), 0.0),
            ],
            axis=1,
        )
        if pair:
            keep = lax.dynamic_slice_in_dim(gain_cols, dpi * (width // 2), width // 2, 0)
            give = lax.dynamic_slice_in_dim(gain_cols, (1 - dpi) * (width // 2), width // 2, 0)
            gain_cols = keep + swap_core(give)
        gain_cols = jnp.pad(gain_cols, ((0, 0), (0, PAD - gain_cols.shape[1])))
        packed = chain.mark(pack(list(chain.after(d_qkv, d_out, gain_cols)), 2))
        held["g_tail"] = spread(packed)

    def finish_down():
        (value,) = chain.after(held["g_down"])
        (held["g_down"],) = sum_parts(value, ff // 3, [[(0, ff // 3)]])
        chain.mark(held["g_down"])

    def finish_both():
        (value,) = chain.after(held["g_gate_up"])
        group = 6 * FF_TILE
        starts = range(0, group, 2 * FF_TILE)
        cuts = [[(i + o, i + o + FF_TILE) for i in starts] for o in (0, FF_TILE)]
        held["g_gate"], held["g_up"] = sum_parts(value, group, cuts)
        chain.mark(held["g_up"])

    def finish_tail():
        (value,) = chain.after(held["g_tail"])
        ends = [0, qc, qc + kc, at_out, at_out + oc, at_out + oc + PAD]
        *held["g_attn"], g_gains = sum_parts(value, ends[-1], [[v] for v in zip(ends, ends[1:])])
        g_gains = chain.mark(mm_t(pick.astype(F32), g_gains))
        held["g_gains"] = lax.all_to_all(
            jnp.broadcast_to(g_gains[None], (n_t,) + g_gains.shape), "tensor", 0, 0
        )

    red = Reduce(chain)
    input_back(0)
    d_out = product(left_side(attn_grads), right_side([s["attended"] for s in st]))
    input_back(1)
    held["right"] = right_side([s["qkv_back"] for s in st])

    def finish_rest():
        finish_down()
        finish_both()
        finish_tail()

    red.run(n_four, post_in, {1: tail, 4: finish_rest})
    g_gains = jnp.sum(held["g_gains"], axis=0)
    return (
        jnp.concatenate(outputs, axis=0).reshape(tokens.shape),
        jnp.concatenate(input_grads, axis=0).reshape(tokens.shape),
        *held["g_attn"],
        held["g_gate"],
        held["g_up"],
        held["g_down"],
        g_gains[0],
        g_gains[1],
        g_gains[2],
        g_gains[3],
    )


def solution(mesh):
    act = P(None, "dp", "ctx", None)
    mat = P(("dp", "ctx"), "tensor")
    vec = P(("dp", "ctx"))
    return jax.shard_map(
        local,
        mesh=mesh,
        in_specs=(act, P()) + (mat,) * 7 + (vec,) * 4 + (act,),
        out_specs=(act, act) + (mat,) * 7 + (vec,) * 4,
        check_vma=False,
    )
```

```python
import functools

import jax
import jax.numpy as jnp
from jax import lax
from jax.experimental import pallas as pl
from jax.experimental.pallas import tpu as pltpu
from jax.sharding import PartitionSpec as P

HEAD_SIZE = 256
EPS = 1e-06
CAP = 50.0
BASE = 10000.0
BF = jnp.bfloat16
F32 = jnp.float32
PAD = 128
VMEM_LIMIT = 60 * 1024 * 1024
GELU_C = 0.7978845608028654
GELU_A = 0.044715


def apply_norm(values):
    factor = lax.rsqrt(jnp.mean(values * values, axis=-1, keepdims=True) + EPS)
    return values * factor, factor


def norm_backward(upstream, scaled, factor):
    return factor * (upstream - scaled * jnp.mean(upstream * scaled, axis=-1, keepdims=True))


def rotation(token_positions, width_size):
    half_width = width_size // 2
    inverse = BASE ** (-(jnp.arange(half_width, dtype=F32) * 2.0) / width_size)
    angles = token_positions.astype(F32)[:, None] * inverse[None, :]
    return jnp.cos(angles), jnp.sin(angles)


def mm(a, b):
    return jnp.dot(a, b, preferred_element_type=F32)


def mm_t(a, b):
    return lax.dot_general(a, b, (((1,), (1,)), ((), ())), preferred_element_type=F32)


def tmm(a, b):
    return lax.dot_general(a, b, (((0,), (0,)), ((), ())), preferred_element_type=F32)


def low(values):
    return lax.reduce_precision(values, 8, 7).astype(BF)


def call(body, out_shape, grid, in_specs, out_specs, scratch=(), flops=0, moved=0, aliases=None):
    return pl.pallas_call(
        body,
        out_shape=out_shape,
        input_output_aliases=aliases or {},
        grid_spec=pltpu.PrefetchScalarGridSpec(
            num_scalar_prefetch=0,
            grid=grid,
            in_specs=in_specs,
            out_specs=out_specs,
            scratch_shapes=list(scratch),
        ),
        compiler_params=pltpu.CompilerParams(
            dimension_semantics=("arbitrary",) * len(grid), vmem_limit_bytes=VMEM_LIMIT
        ),
        cost_estimate=pl.CostEstimate(flops=flops, bytes_accessed=moved, transcendentals=0),
    )


def shape(dims, dtype):
    return jax.ShapeDtypeStruct(dims, dtype)


def whole(dims):
    return pl.BlockSpec(dims, lambda *_: (0,) * len(dims))


def project_body(n_rot, x_ref, w_ref, cos_ref, sin_ref, out_ref):
    half = HEAD_SIZE // 2
    y = mm(x_ref[...], w_ref[...])
    rotate = pl.program_id(0) < n_rot
    cos = jnp.where(rotate, cos_ref[...], 1.0)
    sin = jnp.where(rotate, sin_ref[...], 0.0)
    a, b = y[:, :half], y[:, half:]
    out_ref[:, :half] = (a * cos - b * sin).astype(BF)
    out_ref[:, half:] = (b * cos + a * sin).astype(BF)


def project(normed, weights, columns, n_rot, cos, sin):
    rows, width = normed.shape
    return call(
        functools.partial(project_body, n_rot),
        shape((rows, columns), BF),
        (columns // HEAD_SIZE,),
        [
            whole((rows, width)),
            pl.BlockSpec((width, HEAD_SIZE), lambda j: (0, j)),
            whole(cos.shape),
            whole(sin.shape),
        ],
        pl.BlockSpec((rows, HEAD_SIZE), lambda j: (0, j)),
        flops=2 * rows * width * columns,
        moved=2 * (rows * width + width * columns + rows * columns),
    )(normed, weights, cos, sin)


def scores(q, k, allowed):
    soft = HEAD_SIZE ** (-0.5)
    bend = jnp.tanh(mm_t(q, k) * (soft / CAP))
    return bend, jnp.where(allowed, jnp.exp(CAP * bend), 0.0)


def attend_body(n_q, n_kv, n_pieces, chunks, *refs):
    hd = HEAD_SIZE
    q_ref, qpos_ref, kpos_ref, w_ref = refs[:4]
    pieces = refs[4 : 4 + n_pieces]
    heads_ref, attended_ref, den_ref = refs[4 + n_pieces : 7 + n_pieces]
    outs = refs[7 + n_pieces :]
    qpos = qpos_ref[...]
    for h in range(n_q):
        kv = h // (n_q // n_kv)
        q = q_ref[:, h * hd : (h + 1) * hd]
        num, den = 0.0, 0.0
        for j, piece in enumerate(pieces):
            size = piece.shape[0]
            allowed = kpos_ref[:, j * size : (j + 1) * size] <= qpos
            _, weight = scores(q, piece[:, kv * hd : (kv + 1) * hd], allowed)
            den = den + jnp.sum(weight, axis=-1, keepdims=True)
            v = piece[:, (n_kv + kv) * hd : (n_kv + kv + 1) * hd]
            num = num + mm(weight.astype(BF), v)
        heads = num / den
        heads_ref[:, h * hd : (h + 1) * hd] = heads
        attended_ref[:, h * hd : (h + 1) * hd] = heads.astype(BF)
        den_ref[:, h * PAD : (h + 1) * PAD] = jnp.broadcast_to(den, (den.shape[0], PAD))
    put_chunks(mm_t(attended_ref[...], w_ref[...]), outs)


def put_chunks(value, outs):
    size = value.shape[0] // len(outs)
    for i, out in enumerate(outs):
        out[...] = value[i * size : (i + 1) * size].astype(BF)


def attend(q, q_block, pieces, qpos, kpos, n_q, n_kv, weights, out_block, chunks):
    hd = HEAD_SIZE
    seq_dev = qpos.shape[0]
    width = weights.shape[0]
    specs = [pl.BlockSpec((seq_dev, n_q * hd), lambda i: (q_block, 0))]
    specs += [whole(qpos.shape), whole(kpos.shape)]
    specs.append(pl.BlockSpec((width, n_q * hd), lambda i: (0, out_block)))
    arrays = [q, qpos, kpos, weights]
    for array, size, row, col in pieces:
        specs.append(pl.BlockSpec((size, 2 * n_kv * hd), lambda i, row=row, col=col: (row, col)))
        arrays.append(array)
    seq = kpos.shape[1]
    part = (seq_dev // chunks, width)
    return call(
        functools.partial(attend_body, n_q, n_kv, len(pieces), chunks),
        (
            shape((seq_dev, n_q * hd), F32),
            shape((seq_dev, n_q * hd), BF),
            shape((seq_dev, n_q * PAD), F32),
        )
        + (shape(part, BF),) * chunks,
        (1,),
        specs,
        (whole((seq_dev, n_q * hd)), whole((seq_dev, n_q * hd)), whole((seq_dev, n_q * PAD)))
        + (whole(part),) * chunks,
        flops=4 * n_q * seq_dev * seq * hd + 2 * seq_dev * n_q * hd * width,
        moved=2 * (2 * n_kv * hd * seq + 4 * seq_dev * n_q * hd + 2 * n_q * hd * width),
    )(*arrays)


def attend_back_body(n_q, n_kv, n_pieces, chunks, *refs):
    hd = HEAD_SIZE
    half = hd // 2
    soft = hd ** (-0.5)
    q_ref, qpos_ref, kpos_ref, heads_ref, den_ref, cos_ref, sin_ref, w_ref = refs[:8]
    pieces = refs[8 : 8 + n_pieces]
    grads = refs[8 + n_pieces : 8 + n_pieces + chunks]
    q_back_ref, *outs = refs[8 + n_pieces + chunks :]
    attn_grad = jnp.concatenate([g[...] for g in grads], axis=0)
    qpos = qpos_ref[...]
    group = n_q // n_kv
    for h in range(n_q):
        kv = h // group
        cols = slice(h * hd, (h + 1) * hd)
        k_cols = slice(kv * hd, (kv + 1) * hd)
        v_cols = slice((n_kv + kv) * hd, (n_kv + kv + 1) * hd)
        q = q_ref[:, cols]
        grad = mm(attn_grad, w_ref[:, cols])
        inverse = 1.0 / den_ref[:, h * PAD : h * PAD + 1]
        scaled = (grad * inverse).astype(BF)
        row_dot = jnp.sum(grad * heads_ref[:, cols], axis=-1, keepdims=True) * inverse
        q_grad = 0.0
        for j, piece in enumerate(pieces):
            size = piece.shape[0]
            allowed = kpos_ref[:, j * size : (j + 1) * size] <= qpos
            k, v = piece[:, k_cols], piece[:, v_cols]
            bend, weight = scores(q, k, allowed)
            prob = mm_t(scaled, v)
            score = (weight * (prob - row_dot) * (1.0 - bend * bend)).astype(BF)
            q_grad = q_grad + mm(score, k)
            k_term = tmm(score, q) * soft
            v_term = tmm(weight.astype(BF), scaled)
            if h % group == 0:
                outs[j][:, k_cols] = k_term
                outs[j][:, v_cols] = v_term
            else:
                outs[j][:, k_cols] += k_term
                outs[j][:, v_cols] += v_term
        q_grad = q_grad * soft
        a, b = q_grad[:, :half], q_grad[:, half:]
        q_back_ref[:, h * hd : h * hd + half] = (a * cos_ref[...] + b * sin_ref[...]).astype(BF)
        q_back_ref[:, h * hd + half : (h + 1) * hd] = (
            b * cos_ref[...] - a * sin_ref[...]
        ).astype(BF)


def attend_back(q, q_block, pieces, qpos, kpos, grads, heads, den, cos, sin, n_q, n_kv, weights, out_block):
    hd = HEAD_SIZE
    seq_dev = qpos.shape[0]
    width = weights.shape[0]
    specs = [pl.BlockSpec((seq_dev, n_q * hd), lambda i: (q_block, 0))]
    arrays = [q, qpos, kpos, heads, den, cos, sin]
    specs += [whole(a.shape) for a in arrays[1:]]
    specs.append(pl.BlockSpec((width, n_q * hd), lambda i: (0, out_block)))
    arrays.append(weights)
    out_shapes, out_specs = [shape((seq_dev, n_q * hd), BF)], [whole((seq_dev, n_q * hd))]
    for array, size, row, col in pieces:
        specs.append(pl.BlockSpec((size, 2 * n_kv * hd), lambda i, row=row, col=col: (row, col)))
        arrays.append(array)
        out_shapes.append(shape((size, 2 * n_kv * hd), F32))
        out_specs.append(whole((size, 2 * n_kv * hd)))
    arrays += grads
    specs += [whole(g.shape) for g in grads]
    seq = kpos.shape[1]
    return call(
        functools.partial(attend_back_body, n_q, n_kv, len(pieces), len(grads)),
        tuple(out_shapes),
        (1,),
        specs,
        tuple(out_specs),
        flops=10 * n_q * seq_dev * seq * hd + 2 * seq_dev * n_q * hd * width,
        moved=2 * (6 * n_kv * hd * seq + 8 * seq_dev * n_q * hd + 2 * n_q * hd * width),
    )(*arrays)


def input_back_body(n_q, n_kv, n_terms, chunks, *refs):
    hd = HEAD_SIZE
    half = hd // 2
    kc = n_kv * hd
    q_back_ref, x_ref, cos_ref, sin_ref, w_ref = refs[:5]
    terms = refs[5 : 5 + n_terms]
    back_ref, gain_ref, *outs = refs[5 + n_terms :]
    total = 0.0
    for term in terms:
        total = total + term[...].astype(F32)
    back_ref[:, : n_q * hd] = q_back_ref[...]
    for h in range(n_kv):
        start = (n_q + h) * hd
        a = total[:, h * hd : h * hd + half]
        b = total[:, h * hd + half : (h + 1) * hd]
        back_ref[:, start : start + half] = (a * cos_ref[...] + b * sin_ref[...]).astype(BF)
        back_ref[:, start + half : start + hd] = (b * cos_ref[...] - a * sin_ref[...]).astype(BF)
    back_ref[:, n_q * hd + kc :] = total[:, kc:].astype(BF)
    grad = mm_t(back_ref[...], w_ref[...])
    xhat, _ = apply_norm(x_ref[...].astype(F32))
    gain_ref[...] = jnp.broadcast_to(jnp.sum(grad * xhat, axis=0, keepdims=True), gain_ref.shape)
    put_chunks(grad, outs)


def input_back_call(q_back, terms, x, block, cos, sin, weights, n_q, n_kv, chunks):
    hd = HEAD_SIZE
    seq_dev = q_back.shape[0]
    width = weights.shape[0]
    cols = (n_q + 2 * n_kv) * hd
    part = (seq_dev // chunks, width)
    return call(
        functools.partial(input_back_body, n_q, n_kv, len(terms), chunks),
        (shape((seq_dev, cols), BF), shape((8, width), F32)) + (shape(part, BF),) * chunks,
        (1,),
        [
            whole(q_back.shape),
            pl.BlockSpec((seq_dev, width), lambda i: (block, 0)),
            whole(cos.shape),
            whole(sin.shape),
            pl.BlockSpec((width, cols), lambda i: (0, 0)),
        ]
        + [whole(t.shape) for t in terms],
        (whole((seq_dev, cols)), whole((8, width))) + (whole(part),) * chunks,
        flops=2 * seq_dev * cols * width,
        moved=2 * (width * cols + 3 * seq_dev * width + 4 * seq_dev * cols),
    )(q_back, x, cos, sin, weights, *terms)


def choose(flag_ref, total_ref, third_ref):
    total, third = total_ref[...].astype(F32), third_ref[...].astype(F32)
    return jnp.where(flag_ref[0] == 1, total, third)


def add_gain(gain_ref, rows):
    @pl.when(pl.program_id(0) == 0)
    def _():
        gain_ref[...] = jnp.zeros_like(gain_ref)

    for i, value in enumerate(rows):
        gain_ref[i : i + 1, :] += jnp.sum(value, axis=0, keepdims=True)


def post_attend_body(flag_ref, total_ref, third_ref, x_ref, scale_ref, a_ref, out_ref):
    value = choose(flag_ref, total_ref, third_ref)
    ahat, _ = apply_norm(value)
    h1hat, _ = apply_norm(x_ref[...].astype(F32) + ahat * scale_ref[1:2, :])
    a_ref[...] = value.astype(BF)
    out_ref[...] = (h1hat * scale_ref[2:3, :]).astype(BF)


def post_ffn_body(
    flag_ref, total_ref, third_ref, a_ref, x_ref, dy_ref, scale_ref, out_ref, grad_ref, gain_ref
):
    fhat, factor = apply_norm(choose(flag_ref, total_ref, third_ref))
    ahat, _ = apply_norm(a_ref[...].astype(F32))
    hidden_one = x_ref[...].astype(F32) + ahat * scale_ref[1:2, :]
    scale = scale_ref[3:4, :]
    dy = dy_ref[...].astype(F32)
    out_ref[...] = (hidden_one + fhat * scale).astype(BF)
    grad_ref[...] = norm_backward(dy * scale, fhat, factor).astype(BF)
    add_gain(gain_ref, [dy * fhat])


def post_mid_body(
    flag_ref, total_ref, third_ref, a_ref, x_ref, dy_ref, scale_ref, one_ref, grad_ref, gain_ref
):
    mid = choose(flag_ref, total_ref, third_ref)
    ahat, fac_attn = apply_norm(a_ref[...].astype(F32))
    scale_attn, scale_mid = scale_ref[1:2, :], scale_ref[2:3, :]
    h1hat, fac_mid = apply_norm(x_ref[...].astype(F32) + ahat * scale_attn)
    one_grad = dy_ref[...].astype(F32) + norm_backward(mid * scale_mid, h1hat, fac_mid)
    one_ref[...] = one_grad
    grad_ref[...] = norm_backward(one_grad * scale_attn, ahat, fac_attn).astype(BF)
    add_gain(gain_ref, [mid * h1hat, one_grad * ahat])


def post_in_body(flag_ref, total_ref, third_ref, one_ref, x_ref, scale_ref, out_ref):
    grad = choose(flag_ref, total_ref, third_ref)
    xhat, factor = apply_norm(x_ref[...].astype(F32))
    back = norm_backward(grad * scale_ref[0:1, :], xhat, factor)
    out_ref[...] = (one_ref[...] + back).astype(BF)


def skip_ref(body, index, *refs):
    body(*refs[:index], *refs[index + 1 :])


def post(body, flag, pair_values, chunk_arrays, row_arrays, k, scales, outs, gain=False, into=None):
    rows, width = pair_values[0].shape
    steps = 2 if rows >= 128 else 1
    tile = (rows // steps, width)
    chunk = pl.BlockSpec(tile, lambda i: (i, 0))
    row = pl.BlockSpec(tile, lambda i: (k * steps + i, 0))
    located, located_specs = [], []
    for values in chunk_arrays:
        size = values[0].shape[0]
        base = (k * rows % size) // tile[0]
        located.append(values[k * rows // size])
        located_specs.append(pl.BlockSpec(tile, lambda i, base=base: (base + i, 0)))
    arrays = [flag, *pair_values, *located, *row_arrays, scales]
    specs = [pl.BlockSpec(memory_space=pltpu.SMEM), chunk, chunk, *located_specs]
    specs += [row] * len(row_arrays) + [whole(scales.shape)]
    out_shapes = [shape((rows, width), dtype) for dtype in outs]
    out_specs = [chunk] * len(outs)
    if gain:
        out_shapes.append(shape((8, width), F32))
        out_specs.append(whole((8, width)))
    aliases = {}
    if into is not None:
        total, previous = into
        out_shapes[0], out_specs[0] = shape((total, width), outs[0]), row
        if previous is not None:
            aliases = {len(arrays): 0}
            body = functools.partial(skip_ref, body, len(arrays))
            arrays.append(previous)
            specs.append(pl.BlockSpec(memory_space=pl.ANY))
    return call(
        body,
        tuple(out_shapes),
        (steps,),
        specs,
        tuple(out_specs),
        flops=20 * rows * width,
        moved=14 * rows * width,
        aliases=aliases,
    )(*arrays)


def ffn_body(n_x, n_out, *refs):
    xs, (wg_ref, wu_ref, wd_ref) = refs[:n_x], refs[n_x : n_x + 3]
    gate_ref, up_ref, hid_ref = refs[n_x + 3 : n_x + 6]
    outs, (x_ref, acc) = refs[n_x + 6 : n_x + 6 + n_out], refs[n_x + 6 + n_out :]
    j = pl.program_id(0)

    @pl.when(j == 0)
    def _():
        gather_rows(xs, x_ref)
        acc[...] = jnp.zeros_like(acc)

    x = x_ref[...]
    gate = mm(x, wg_ref[...])
    up = mm(x, wu_ref[...])
    bend = jnp.tanh(GELU_C * (gate + GELU_A * gate * gate * gate))
    hidden = (0.5 * gate * (1.0 + bend) * up).astype(BF)
    gate_ref[...] = gate.astype(BF)
    up_ref[...] = up.astype(BF)
    hid_ref[...] = hidden
    acc[...] += mm_t(hidden, wd_ref[...])

    @pl.when(j == pl.num_programs(0) - 1)
    def _():
        put_chunks(acc[...], outs)


def gather_rows(pieces, out_ref):
    size = pieces[0].shape[0]
    for i, piece in enumerate(pieces):
        out_ref[i * size : (i + 1) * size, :] = piece[...]


def ffn(xs, weights, ff, n_out):
    width = xs[0].shape[1]
    rows = xs[0].shape[0] * len(xs)
    tile = 256
    steps = ff // tile
    col = lambda part: pl.BlockSpec((width, tile), lambda j: (0, part * steps + j))
    act = pl.BlockSpec((rows, tile), lambda j: (0, j))
    part = (rows // n_out, width)
    return call(
        functools.partial(ffn_body, len(xs), n_out),
        (shape((rows, ff), BF),) * 3 + (shape(part, BF),) * n_out,
        (steps,),
        [whole(xs[0].shape)] * len(xs) + [col(0), col(1), col(2)],
        (act, act, act) + (whole(part),) * n_out,
        [pltpu.VMEM((rows, width), BF), pltpu.VMEM((rows, width), F32)],
        flops=6 * rows * width * ff,
        moved=6 * width * ff + 4 * rows * width + 6 * rows * ff,
    )(*xs, weights, weights, weights)


def ffn_back_body(n_y, n_out, *refs):
    ys, (wg_ref, wu_ref, wd_ref, gate_ref, up_ref) = refs[:n_y], refs[n_y : n_y + 5]
    rest = refs[n_y + 5 :]
    both_ref, outs, (y_ref, acc) = rest[0], rest[1 : 1 + n_out], rest[1 + n_out :]
    tile = gate_ref.shape[1]
    j = pl.program_id(0)

    @pl.when(j == 0)
    def _():
        gather_rows(ys, y_ref)
        acc[...] = jnp.zeros_like(acc)

    grad = mm(y_ref[...], wd_ref[...])
    gate, up = gate_ref[...].astype(F32), up_ref[...].astype(F32)
    square = gate * gate
    bend = jnp.tanh(GELU_C * gate * (1.0 + GELU_A * square))
    rise = 0.5 * (1.0 + bend)
    slope = rise + 0.5 * gate * (1.0 - bend * bend) * (GELU_C * (1.0 + 3.0 * GELU_A * square))
    d_gate = (grad * up * slope).astype(BF)
    d_up = (grad * (gate * rise)).astype(BF)
    both_ref[:, :tile] = d_gate
    both_ref[:, tile:] = d_up
    acc[...] += mm_t(d_gate, wg_ref[...]) + mm_t(d_up, wu_ref[...])

    @pl.when(j == pl.num_programs(0) - 1)
    def _():
        put_chunks(acc[...], outs)


FF_TILE = 256


def ffn_back(ys, weights, gate, up, ff, n_out):
    width = ys[0].shape[1]
    rows = ys[0].shape[0] * len(ys)
    tile = FF_TILE
    steps = ff // tile
    col = lambda part: pl.BlockSpec((width, tile), lambda j: (0, part * steps + j))
    act = pl.BlockSpec((rows, tile), lambda j: (0, j))
    part = (rows // n_out, width)
    return call(
        functools.partial(ffn_back_body, len(ys), n_out),
        (shape((rows, 2 * ff), BF),) + (shape(part, BF),) * n_out,
        (steps,),
        [whole(ys[0].shape)] * len(ys) + [col(0), col(1), col(2), act, act],
        (pl.BlockSpec((rows, 2 * tile), lambda j: (0, j)),) + (whole(part),) * n_out,
        [pltpu.VMEM((rows, width), BF), pltpu.VMEM((rows, width), F32)],
        flops=6 * rows * width * ff,
        moved=6 * width * ff + 4 * rows * width + 8 * rows * ff,
    )(*ys, weights, weights, weights, gate, up)


def sum_body(cuts, part_ref, *outs):
    total = 0.0
    for i in range(part_ref.shape[0]):
        total = total + part_ref[i].astype(F32)
    for out, spans in zip(outs, cuts):
        at = 0
        for start, stop in spans:
            out[:, at : at + stop - start] = total[:, start:stop]
            at += stop - start


def sum_parts(parts, tile, cuts):
    n, rows, cols = parts.shape
    steps = cols // tile
    sizes = [sum(stop - start for start, stop in spans) for spans in cuts]
    return call(
        functools.partial(sum_body, cuts),
        tuple(shape((rows, size * steps), F32) for size in sizes),
        (steps,),
        [pl.BlockSpec((n, rows, tile), lambda j: (0, 0, j))],
        tuple(pl.BlockSpec((rows, size), lambda j: (0, j)) for size in sizes),
        flops=n * rows * cols,
        moved=2 * n * rows * cols + 4 * rows * cols,
    )(parts)


def pack_body(*refs):
    start = 0
    for ref in refs[:-1]:
        refs[-1][:, start : start + ref.shape[1]] = ref[...].astype(BF)
        start += ref.shape[1]


def pack(arrays, steps):
    rows = arrays[0].shape[0] // steps
    cols = sum(a.shape[1] for a in arrays)
    return call(
        pack_body,
        shape((rows * steps, cols), BF),
        (steps,),
        [pl.BlockSpec((rows, a.shape[1]), lambda i: (i, 0)) for a in arrays],
        pl.BlockSpec((rows, cols), lambda i: (i, 0)),
        moved=4 * rows * steps * cols,
    )(*arrays)


class Chain:
    def __init__(self):
        self.token = None

    def after(self, *values):
        if self.token is None:
            return values
        return lax.optimization_barrier((*values, self.token))[:-1]

    def mark(self, value):
        self.token = value
        return value


class Reduce:
    def __init__(self, chain):
        self.chain, self.piece, self.first = chain, {}, {}
        self.sums, self.second, self.total, self.third = {}, {}, {}, {}
        self.line = lax.axis_size("tensor") == 4

    def send(self, k, piece):
        self.piece[k] = piece
        if self.line:
            self.first[k] = lax.ppermute(piece, "tensor", [(0, 1), (3, 2)])
        else:
            self.total[k] = lax.psum(piece.astype(F32), "tensor")

    def add(self, k):
        if self.line:
            piece, first = self.chain.after(self.piece[k], self.first[k])
            total = low(piece.astype(F32) + first.astype(F32))
            self.sums[k] = self.chain.mark(total)
            self.second[k] = lax.ppermute(total, "tensor", [(1, 2), (2, 1)])

    def join(self, k):
        if self.line:
            sums, second = self.chain.after(self.sums[k], self.second[k])
            total = low(sums.astype(F32) + second.astype(F32))
            self.total[k] = self.chain.mark(total)
            self.third[k] = lax.ppermute(total, "tensor", [(1, 0), (2, 3)])

    def load(self, pieces):
        for piece in pieces:
            self.send(len(self.piece), piece)

    def run(self, n, finish, hooks):
        for slot in range(n + 2):
            if slot < n:
                self.add(slot)
            if 0 < slot <= n:
                self.join(slot - 1)
            if slot >= 2:
                finish(slot - 2)
            if slot in hooks:
                hooks[slot]()

    def take(self, k):
        if self.line:
            return self.chain.after(self.total[k], self.third[k])
        return self.chain.after(self.total[k], self.total[k])


def local(
    tokens,
    span_order,
    w_query,
    w_key,
    value_weight,
    w_out,
    w_gate,
    w_up,
    w_down,
    gain_attn_in,
    gain_attn_out,
    gain_ffn_in,
    gain_ffn_out,
    cotangent,
):
    micros, batch, seq_dev, width = tokens.shape
    n_dp, n_ctx, n_t = lax.axis_size("dp"), lax.axis_size("ctx"), lax.axis_size("tensor")
    dpi, ctx, zi = lax.axis_index("dp"), lax.axis_index("ctx"), lax.axis_index("tensor")
    seq = seq_dev * n_ctx
    span_len = seq // span_order.shape[0]
    hd = HEAD_SIZE
    n_kv = w_key.shape[1] // hd
    n_q = w_query.shape[1] // hd
    ff = w_gate.shape[1]
    qc, kc, oc = w_query.shape[1], w_key.shape[1], w_out.shape[1]
    n_seqs, chunks = micros * batch, 2
    swap = n_ctx == 4
    pair = n_dp == 2

    row_index = jnp.arange(seq, dtype=jnp.int32)
    all_pos = span_order[row_index // span_len] * span_len + row_index % span_len
    by_dev = all_pos.reshape(n_ctx, seq_dev)
    query_pos = lax.dynamic_index_in_dim(by_dev, ctx, 0, keepdims=False)
    if swap:
        key_pos = jnp.concatenate(
            [lax.dynamic_index_in_dim(by_dev, ctx ^ j, 0, keepdims=False) for j in range(n_ctx)]
        )
    else:
        key_pos = all_pos
    qpos, kpos = query_pos[:, None], key_pos[None, :]
    cos, sin = rotation(query_pos, hd)

    lane = lax.broadcasted_iota(jnp.int32, (gain_attn_in.shape[0], PAD), 1)
    gains = jnp.zeros(lane.shape, BF)
    for i, gain in enumerate((gain_attn_in, gain_attn_out, gain_ffn_in, gain_ffn_out)):
        gains = jnp.where(lane == i, gain[:, None], gains)
    pack_attn = pack([w_query, w_key, value_weight, w_out, gains], 1)
    pack_ffn = jnp.concatenate([w_gate, w_up, w_down], axis=1)
    full_attn = lax.all_gather(pack_attn, ("dp", "ctx"), axis=0, tiled=True)
    full_ffn = lax.all_gather(pack_ffn, ("dp", "ctx"), axis=0, tiled=True)
    at_out = qc + 2 * kc
    out_block = at_out // oc
    pick = jnp.eye(8, PAD, dtype=BF)
    gain_cols = mm_t(pick, full_attn[:, at_out + oc :])
    scales = 1.0 + gain_cols

    chain = Chain()
    flips = [[(i, i ^ j) for i in range(n_ctx)] for j in range(n_ctx)]

    def half(full, owner):
        return lax.dynamic_slice_in_dim(full, owner * (width // 2), width // 2, 1)

    def swap_core(value):
        return lax.ppermute(value, "dp", [(0, 1), (1, 0)])

    def left_side(values):
        value = jnp.concatenate(chain.after(*values), axis=0)
        if not pair:
            return value
        return jnp.concatenate([half(value, dpi), swap_core(half(value, 1 - dpi))], axis=0)

    def right_side(values):
        value = jnp.concatenate(chain.after(*values), axis=0)
        return jnp.concatenate([value, swap_core(value)], axis=0) if pair else value

    def spread(grad):
        if pair:
            return lax.all_to_all(grad.reshape(n_ctx, -1, grad.shape[1]), "ctx", 0, 0)
        return lax.psum_scatter(grad, ("dp", "ctx"), scatter_dimension=0, tiled=True)[None]

    def product(left, right):
        left, right = chain.after(left, right)
        return chain.mark(tmm(left, right).astype(BF))

    def scatter(grad):
        axes = "ctx" if pair else ("dp", "ctx")
        return lax.psum_scatter(grad, axes, scatter_dimension=0, tiled=True)[None]

    token_rows = tokens.reshape(n_seqs * seq_dev, width)
    dy_rows = cotangent.reshape(n_seqs * seq_dev, width)
    xhats, _ = apply_norm(token_rows.astype(F32))
    normed = (xhats * scales[0:1]).astype(BF)
    cos_all, sin_all = jnp.tile(cos, (n_seqs, 1)), jnp.tile(sin, (n_seqs, 1))
    qkv = project(normed, full_attn, qc + 2 * kc, n_q + n_kv, cos_all, sin_all)
    kv = qkv[:, qc:]
    if swap:
        others = [lax.ppermute(kv, "ctx", flips[j]) for j in range(1, n_ctx)]
        pieces = [[(a, seq_dev, m, 0) for a in [kv] + others] for m in range(n_seqs)]
    else:
        every = lax.all_gather(kv.reshape(n_seqs, seq_dev, 2 * kc), "ctx", axis=1, tiled=True)
        every = every.reshape(n_seqs * seq, 2 * kc)
        pieces = [[(every, seq, m, 0)] for m in range(n_seqs)]

    def rows_of(value, m):
        return value[m * seq_dev : (m + 1) * seq_dev]

    st = [{}, {}]
    assert n_seqs == 2
    n_one, n_two, n_three, n_four = 4, 4, 4, 4
    inner = ((zi == 1) | (zi == n_t - 2)).astype(jnp.int32).reshape(1)
    attn_outs, normed_two, outputs, ffn_grads = [], [], [], []
    one_grads, attn_grads, input_grads = [], [], []
    gain_fin, gain_mid = [], []

    def post_attend(k):
        values = red.take(k)
        a, n = post(post_attend_body, inner, values, [], [token_rows], k, scales, [BF, BF])
        attn_outs.append(a), normed_two.append(n)
        chain.mark(n)

    def post_ffn(k):
        values, rows = red.take(k), [token_rows, dy_rows]
        into = (n_seqs * seq_dev, outputs[-1] if outputs else None)
        out, grad, gain = post(
            post_ffn_body, inner, values, [attn_outs], rows, k, scales, [BF, BF], True, into
        )
        outputs.append(out), ffn_grads.append(grad), gain_fin.append(gain)
        chain.mark(grad)

    def post_mid(k):
        values, rows = red.take(k), [token_rows, dy_rows]
        one, grad, gain = post(
            post_mid_body, inner, values, [attn_outs], rows, k, scales, [F32, BF], True
        )
        one_grads.append(one), attn_grads.append(grad), gain_mid.append(gain)
        chain.mark(grad)

    def post_in(k):
        values = red.take(k)
        into = (n_seqs * seq_dev, input_grads[-1] if input_grads else None)
        (grad,) = post(
            post_in_body, inner, values, [one_grads], [token_rows], k, scales, [BF], False, into
        )
        input_grads.append(grad)
        chain.mark(grad)

    def attention(m):
        s = st[m]
        (first, *rest) = chain.after(*[p[0] for p in pieces[m]])
        s["pieces"] = [(v,) + p[1:] for v, p in zip([first, *rest], pieces[m])]
        s["heads"], s["attended"], s["den"], *part = attend(
            qkv, m, s["pieces"], qpos, kpos, n_q, n_kv, full_attn, out_block, n_one // 2
        )
        chain.mark(part[0])
        red.load(part)

    red = Reduce(chain)
    attention(0)
    attention(1)
    held = {}

    def hold(name, make):
        def run():
            held[name] = make()

        return run

    red.run(
        n_one, post_attend, {n_one + 1: hold("left", lambda: chain.mark(left_side([normed])))}
    )

    red = Reduce(chain)
    values = chain.after(*normed_two)
    gate, up, hidden, *part = ffn(list(values), full_ffn, ff, n_two)
    chain.mark(part[0])
    red.load(part)
    red.run(
        n_two,
        post_ffn,
        {
            0: hold("down_right", lambda: right_side([hidden])),
            1: hold("mid_left", lambda: left_side(normed_two)),
        },
    )

    red = Reduce(chain)
    values = chain.after(*ffn_grads)
    d_both, *part = ffn_back(list(values), full_ffn, gate, up, ff, n_three)
    chain.mark(part[0])
    red.load(part)
    both_right = right_side([d_both])
    down_left = left_side(ffn_grads)

    def attention_back(m):
        s = st[m]
        size = n_three // 2
        grads = chain.after(*attn_grads[size * m : size * (m + 1)])
        s["q_back"], *s["terms"] = attend_back(
            qkv,
            m,
            s["pieces"],
            qpos,
            kpos,
            list(grads),
            s["heads"],
            s["den"],
            cos,
            sin,
            n_q,
            n_kv,
            full_attn,
            out_block,
        )
        chain.mark(s["q_back"])
        if swap:
            s["moved"] = [
                lax.ppermute(s["terms"][j].astype(BF), "ctx", flips[j]) for j in range(1, n_ctx)
            ]
        else:
            s["moved"] = [lax.psum_scatter(s["terms"][0], "ctx", scatter_dimension=0, tiled=True)]

    red.run(
        n_three,
        post_mid,
        {
            0: hold("g_down", lambda: scatter(product(down_left, held["down_right"]))),
            1: hold("g_gate_up", lambda: scatter(product(held["mid_left"], both_right))),
            3: lambda: attention_back(0),
        },
    )
    attention_back(1)

    def input_back(m):
        s = st[m]
        moved = list(chain.after(*s["moved"]))
        terms = [s["terms"][0]] + moved if swap else moved
        s["qkv_back"], s["gain"], *part = input_back_call(
            s["q_back"], terms, token_rows, m, cos, sin, full_attn, n_q, n_kv, n_four // 2
        )
        chain.mark(part[0])
        red.load(part)

    def tail():
        d_qkv = product(held["left"], held["right"])
        owner = zi == 0
        gain_cols = jnp.stack(
            [
                st[0]["gain"][0] + st[1]["gain"][0],
                jnp.where(owner, sum(v[1] for v in gain_mid), 0.0),
                jnp.where(owner, sum(v[0] for v in gain_mid), 0.0),
                jnp.where(owner, sum(v[0] for v in gain_fin), 0.0),
            ],
            axis=1,
        )
        if pair:
            keep = lax.dynamic_slice_in_dim(gain_cols, dpi * (width // 2), width // 2, 0)
            give = lax.dynamic_slice_in_dim(gain_cols, (1 - dpi) * (width // 2), width // 2, 0)
            gain_cols = keep + swap_core(give)
        gain_cols = jnp.pad(gain_cols, ((0, 0), (0, PAD - gain_cols.shape[1])))
        packed = chain.mark(pack(list(chain.after(d_qkv, d_out, gain_cols)), 2))
        held["g_tail"] = spread(packed)

    def finish_down():
        (value,) = chain.after(held["g_down"])
        (held["g_down"],) = sum_parts(value, ff // 3, [[(0, ff // 3)]])
        chain.mark(held["g_down"])

    def finish_both():
        (value,) = chain.after(held["g_gate_up"])
        group = 6 * FF_TILE
        starts = range(0, group, 2 * FF_TILE)
        cuts = [[(i + o, i + o + FF_TILE) for i in starts] for o in (0, FF_TILE)]
        held["g_gate"], held["g_up"] = sum_parts(value, group, cuts)
        chain.mark(held["g_up"])

    def finish_tail():
        (value,) = chain.after(held["g_tail"])
        ends = [0, qc, qc + kc, at_out, at_out + oc, at_out + oc + PAD]
        *held["g_attn"], g_gains = sum_parts(value, ends[-1], [[v] for v in zip(ends, ends[1:])])
        g_gains = chain.mark(mm_t(pick.astype(F32), g_gains))
        held["g_gains"] = lax.all_to_all(
            jnp.broadcast_to(g_gains[None], (n_t,) + g_gains.shape), "tensor", 0, 0
        )

    red = Reduce(chain)
    input_back(0)
    d_out = product(left_side(attn_grads), right_side([s["attended"] for s in st]))
    finish_down()
    input_back(1)
    held["right"] = right_side([s["qkv_back"] for s in st])

    def finish_rest():
        finish_both()
        finish_tail()

    red.run(n_four, post_in, {1: tail, 4: finish_rest})
    g_gains = jnp.sum(held["g_gains"], axis=0)
    return (
        outputs[-1].reshape(tokens.shape),
        input_grads[-1].reshape(tokens.shape),
        *held["g_attn"],
        held["g_gate"],
        held["g_up"],
        held["g_down"],
        g_gains[0],
        g_gains[1],
        g_gains[2],
        g_gains[3],
    )


def solution(mesh):
    act = P(None, "dp", "ctx", None)
    mat = P(("dp", "ctx"), "tensor")
    vec = P(("dp", "ctx"))
    return jax.shard_map(
        local,
        mesh=mesh,
        in_specs=(act, P()) + (mat,) * 7 + (vec,) * 4 + (act,),
        out_specs=(act, act) + (mat,) * 7 + (vec,) * 4,
        check_vma=False,
    )
```

```python
import functools

import jax
import jax.numpy as jnp
from jax import lax
from jax.experimental import pallas as pl
from jax.experimental.pallas import tpu as pltpu
from jax.sharding import PartitionSpec as P

HEAD_SIZE = 256
EPS = 1e-06
CAP = 50.0
BASE = 10000.0
BF = jnp.bfloat16
F32 = jnp.float32
PAD = 128
VMEM_LIMIT = 60 * 1024 * 1024
GELU_C = 0.7978845608028654
GELU_A = 0.044715


def apply_norm(values):
    factor = lax.rsqrt(jnp.mean(values * values, axis=-1, keepdims=True) + EPS)
    return values * factor, factor


def norm_backward(upstream, scaled, factor):
    return factor * (upstream - scaled * jnp.mean(upstream * scaled, axis=-1, keepdims=True))


def rotation(token_positions, width_size):
    half_width = width_size // 2
    inverse = BASE ** (-(jnp.arange(half_width, dtype=F32) * 2.0) / width_size)
    angles = token_positions.astype(F32)[:, None] * inverse[None, :]
    return jnp.cos(angles), jnp.sin(angles)


def mm(a, b):
    return jnp.dot(a, b, preferred_element_type=F32)


def mm_t(a, b):
    return lax.dot_general(a, b, (((1,), (1,)), ((), ())), preferred_element_type=F32)


def tmm(a, b):
    return lax.dot_general(a, b, (((0,), (0,)), ((), ())), preferred_element_type=F32)


def low(values):
    return lax.reduce_precision(values, 8, 7).astype(BF)


def call(body, out_shape, grid, in_specs, out_specs, scratch=(), flops=0, moved=0, aliases=None):
    return pl.pallas_call(
        body,
        out_shape=out_shape,
        input_output_aliases=aliases or {},
        grid_spec=pltpu.PrefetchScalarGridSpec(
            num_scalar_prefetch=0,
            grid=grid,
            in_specs=in_specs,
            out_specs=out_specs,
            scratch_shapes=list(scratch),
        ),
        compiler_params=pltpu.CompilerParams(
            dimension_semantics=("arbitrary",) * len(grid), vmem_limit_bytes=VMEM_LIMIT
        ),
        cost_estimate=pl.CostEstimate(flops=flops, bytes_accessed=moved, transcendentals=0),
    )


def shape(dims, dtype):
    return jax.ShapeDtypeStruct(dims, dtype)


def whole(dims):
    return pl.BlockSpec(dims, lambda *_: (0,) * len(dims))


def project_body(n_rot, x_ref, w_ref, cos_ref, sin_ref, out_ref):
    half = HEAD_SIZE // 2
    y = mm(x_ref[...], w_ref[...])
    rotate = pl.program_id(0) < n_rot
    cos = jnp.where(rotate, cos_ref[...], 1.0)
    sin = jnp.where(rotate, sin_ref[...], 0.0)
    a, b = y[:, :half], y[:, half:]
    out_ref[:, :half] = (a * cos - b * sin).astype(BF)
    out_ref[:, half:] = (b * cos + a * sin).astype(BF)


def project(normed, weights, columns, n_rot, cos, sin):
    rows, width = normed.shape
    return call(
        functools.partial(project_body, n_rot),
        shape((rows, columns), BF),
        (columns // HEAD_SIZE,),
        [
            whole((rows, width)),
            pl.BlockSpec((width, HEAD_SIZE), lambda j: (0, j)),
            whole(cos.shape),
            whole(sin.shape),
        ],
        pl.BlockSpec((rows, HEAD_SIZE), lambda j: (0, j)),
        flops=2 * rows * width * columns,
        moved=2 * (rows * width + width * columns + rows * columns),
    )(normed, weights, cos, sin)


def scores(q, k, allowed):
    soft = HEAD_SIZE ** (-0.5)
    bend = jnp.tanh(mm_t(q, k) * (soft / CAP))
    return bend, jnp.where(allowed, jnp.exp(CAP * bend), 0.0)


def attend_body(n_q, n_kv, n_pieces, chunks, *refs):
    hd = HEAD_SIZE
    q_ref, qpos_ref, kpos_ref, w_ref = refs[:4]
    pieces = refs[4 : 4 + n_pieces]
    heads_ref, attended_ref, den_ref = refs[4 + n_pieces : 7 + n_pieces]
    outs = refs[7 + n_pieces :]
    qpos = qpos_ref[...]
    for h in range(n_q):
        kv = h // (n_q // n_kv)
        q = q_ref[:, h * hd : (h + 1) * hd]
        num, den = 0.0, 0.0
        for j, piece in enumerate(pieces):
            size = piece.shape[0]
            allowed = kpos_ref[:, j * size : (j + 1) * size] <= qpos
            _, weight = scores(q, piece[:, kv * hd : (kv + 1) * hd], allowed)
            den = den + jnp.sum(weight, axis=-1, keepdims=True)
            v = piece[:, (n_kv + kv) * hd : (n_kv + kv + 1) * hd]
            num = num + mm(weight.astype(BF), v)
        heads = num / den
        heads_ref[:, h * hd : (h + 1) * hd] = heads
        attended_ref[:, h * hd : (h + 1) * hd] = heads.astype(BF)
        den_ref[:, h * PAD : (h + 1) * PAD] = jnp.broadcast_to(den, (den.shape[0], PAD))
    put_chunks(mm_t(attended_ref[...], w_ref[...]), outs)


def put_chunks(value, outs):
    size = value.shape[0] // len(outs)
    for i, out in enumerate(outs):
        out[...] = value[i * size : (i + 1) * size].astype(BF)


def attend(q, q_block, pieces, qpos, kpos, n_q, n_kv, weights, out_block, chunks):
    hd = HEAD_SIZE
    seq_dev = qpos.shape[0]
    width = weights.shape[0]
    specs = [pl.BlockSpec((seq_dev, n_q * hd), lambda i: (q_block, 0))]
    specs += [whole(qpos.shape), whole(kpos.shape)]
    specs.append(pl.BlockSpec((width, n_q * hd), lambda i: (0, out_block)))
    arrays = [q, qpos, kpos, weights]
    for array, size, row, col in pieces:
        specs.append(pl.BlockSpec((size, 2 * n_kv * hd), lambda i, row=row, col=col: (row, col)))
        arrays.append(array)
    seq = kpos.shape[1]
    part = (seq_dev // chunks, width)
    return call(
        functools.partial(attend_body, n_q, n_kv, len(pieces), chunks),
        (
            shape((seq_dev, n_q * hd), F32),
            shape((seq_dev, n_q * hd), BF),
            shape((seq_dev, n_q * PAD), F32),
        )
        + (shape(part, BF),) * chunks,
        (1,),
        specs,
        (whole((seq_dev, n_q * hd)), whole((seq_dev, n_q * hd)), whole((seq_dev, n_q * PAD)))
        + (whole(part),) * chunks,
        flops=4 * n_q * seq_dev * seq * hd + 2 * seq_dev * n_q * hd * width,
        moved=2 * (2 * n_kv * hd * seq + 4 * seq_dev * n_q * hd + 2 * n_q * hd * width),
    )(*arrays)


def attend_back_body(n_q, n_kv, n_pieces, chunks, *refs):
    hd = HEAD_SIZE
    half = hd // 2
    soft = hd ** (-0.5)
    q_ref, qpos_ref, kpos_ref, heads_ref, den_ref, cos_ref, sin_ref, w_ref = refs[:8]
    pieces = refs[8 : 8 + n_pieces]
    grads = refs[8 + n_pieces : 8 + n_pieces + chunks]
    q_back_ref, *outs = refs[8 + n_pieces + chunks :]
    attn_grad = jnp.concatenate([g[...] for g in grads], axis=0)
    qpos = qpos_ref[...]
    group = n_q // n_kv
    for h in range(n_q):
        kv = h // group
        cols = slice(h * hd, (h + 1) * hd)
        k_cols = slice(kv * hd, (kv + 1) * hd)
        v_cols = slice((n_kv + kv) * hd, (n_kv + kv + 1) * hd)
        q = q_ref[:, cols]
        grad = mm(attn_grad, w_ref[:, cols])
        inverse = 1.0 / den_ref[:, h * PAD : h * PAD + 1]
        scaled = (grad * inverse).astype(BF)
        row_dot = jnp.sum(grad * heads_ref[:, cols], axis=-1, keepdims=True) * inverse
        q_grad = 0.0
        for j, piece in enumerate(pieces):
            size = piece.shape[0]
            allowed = kpos_ref[:, j * size : (j + 1) * size] <= qpos
            k, v = piece[:, k_cols], piece[:, v_cols]
            bend, weight = scores(q, k, allowed)
            prob = mm_t(scaled, v)
            score = (weight * (prob - row_dot) * (1.0 - bend * bend)).astype(BF)
            q_grad = q_grad + mm(score, k)
            k_term = tmm(score, q) * soft
            v_term = tmm(weight.astype(BF), scaled)
            if h % group == 0:
                outs[j][:, k_cols] = k_term
                outs[j][:, v_cols] = v_term
            else:
                outs[j][:, k_cols] += k_term
                outs[j][:, v_cols] += v_term
        q_grad = q_grad * soft
        a, b = q_grad[:, :half], q_grad[:, half:]
        q_back_ref[:, h * hd : h * hd + half] = (a * cos_ref[...] + b * sin_ref[...]).astype(BF)
        q_back_ref[:, h * hd + half : (h + 1) * hd] = (
            b * cos_ref[...] - a * sin_ref[...]
        ).astype(BF)


def attend_back(q, q_block, pieces, qpos, kpos, grads, heads, den, cos, sin, n_q, n_kv, weights, out_block):
    hd = HEAD_SIZE
    seq_dev = qpos.shape[0]
    width = weights.shape[0]
    specs = [pl.BlockSpec((seq_dev, n_q * hd), lambda i: (q_block, 0))]
    arrays = [q, qpos, kpos, heads, den, cos, sin]
    specs += [whole(a.shape) for a in arrays[1:]]
    specs.append(pl.BlockSpec((width, n_q * hd), lambda i: (0, out_block)))
    arrays.append(weights)
    out_shapes, out_specs = [shape((seq_dev, n_q * hd), BF)], [whole((seq_dev, n_q * hd))]
    for array, size, row, col in pieces:
        specs.append(pl.BlockSpec((size, 2 * n_kv * hd), lambda i, row=row, col=col: (row, col)))
        arrays.append(array)
        out_shapes.append(shape((size, 2 * n_kv * hd), F32))
        out_specs.append(whole((size, 2 * n_kv * hd)))
    arrays += grads
    specs += [whole(g.shape) for g in grads]
    seq = kpos.shape[1]
    return call(
        functools.partial(attend_back_body, n_q, n_kv, len(pieces), len(grads)),
        tuple(out_shapes),
        (1,),
        specs,
        tuple(out_specs),
        flops=10 * n_q * seq_dev * seq * hd + 2 * seq_dev * n_q * hd * width,
        moved=2 * (6 * n_kv * hd * seq + 8 * seq_dev * n_q * hd + 2 * n_q * hd * width),
    )(*arrays)


def input_back_body(n_q, n_kv, n_terms, chunks, *refs):
    hd = HEAD_SIZE
    half = hd // 2
    kc = n_kv * hd
    q_back_ref, x_ref, cos_ref, sin_ref, w_ref = refs[:5]
    terms = refs[5 : 5 + n_terms]
    back_ref, gain_ref, *outs = refs[5 + n_terms :]
    total = 0.0
    for term in terms:
        total = total + term[...].astype(F32)
    back_ref[:, : n_q * hd] = q_back_ref[...]
    for h in range(n_kv):
        start = (n_q + h) * hd
        a = total[:, h * hd : h * hd + half]
        b = total[:, h * hd + half : (h + 1) * hd]
        back_ref[:, start : start + half] = (a * cos_ref[...] + b * sin_ref[...]).astype(BF)
        back_ref[:, start + half : start + hd] = (b * cos_ref[...] - a * sin_ref[...]).astype(BF)
    back_ref[:, n_q * hd + kc :] = total[:, kc:].astype(BF)
    grad = mm_t(back_ref[...], w_ref[...])
    xhat, _ = apply_norm(x_ref[...].astype(F32))
    gain_ref[...] = jnp.broadcast_to(jnp.sum(grad * xhat, axis=0, keepdims=True), gain_ref.shape)
    put_chunks(grad, outs)


def input_back_call(q_back, terms, x, block, cos, sin, weights, n_q, n_kv, chunks):
    hd = HEAD_SIZE
    seq_dev = q_back.shape[0]
    width = weights.shape[0]
    cols = (n_q + 2 * n_kv) * hd
    part = (seq_dev // chunks, width)
    return call(
        functools.partial(input_back_body, n_q, n_kv, len(terms), chunks),
        (shape((seq_dev, cols), BF), shape((8, width), F32)) + (shape(part, BF),) * chunks,
        (1,),
        [
            whole(q_back.shape),
            pl.BlockSpec((seq_dev, width), lambda i: (block, 0)),
            whole(cos.shape),
            whole(sin.shape),
            pl.BlockSpec((width, cols), lambda i: (0, 0)),
        ]
        + [whole(t.shape) for t in terms],
        (whole((seq_dev, cols)), whole((8, width))) + (whole(part),) * chunks,
        flops=2 * seq_dev * cols * width,
        moved=2 * (width * cols + 3 * seq_dev * width + 4 * seq_dev * cols),
    )(q_back, x, cos, sin, weights, *terms)


def choose(flag_ref, total_ref, third_ref):
    total, third = total_ref[...].astype(F32), third_ref[...].astype(F32)
    return jnp.where(flag_ref[0] == 1, total, third)


def add_gain(gain_ref, rows):
    @pl.when(pl.program_id(0) == 0)
    def _():
        gain_ref[...] = jnp.zeros_like(gain_ref)

    for i, value in enumerate(rows):
        gain_ref[i : i + 1, :] += jnp.sum(value, axis=0, keepdims=True)


def post_attend_body(flag_ref, total_ref, third_ref, x_ref, scale_ref, a_ref, out_ref):
    value = choose(flag_ref, total_ref, third_ref)
    ahat, _ = apply_norm(value)
    h1hat, _ = apply_norm(x_ref[...].astype(F32) + ahat * scale_ref[1:2, :])
    a_ref[...] = value.astype(BF)
    out_ref[...] = (h1hat * scale_ref[2:3, :]).astype(BF)


def post_ffn_body(
    flag_ref, total_ref, third_ref, a_ref, x_ref, dy_ref, scale_ref, out_ref, grad_ref, gain_ref
):
    fhat, factor = apply_norm(choose(flag_ref, total_ref, third_ref))
    ahat, _ = apply_norm(a_ref[...].astype(F32))
    hidden_one = x_ref[...].astype(F32) + ahat * scale_ref[1:2, :]
    scale = scale_ref[3:4, :]
    dy = dy_ref[...].astype(F32)
    out_ref[...] = (hidden_one + fhat * scale).astype(BF)
    grad_ref[...] = norm_backward(dy * scale, fhat, factor).astype(BF)
    add_gain(gain_ref, [dy * fhat])


def post_mid_body(
    flag_ref, total_ref, third_ref, a_ref, x_ref, dy_ref, scale_ref, one_ref, grad_ref, gain_ref
):
    mid = choose(flag_ref, total_ref, third_ref)
    ahat, fac_attn = apply_norm(a_ref[...].astype(F32))
    scale_attn, scale_mid = scale_ref[1:2, :], scale_ref[2:3, :]
    h1hat, fac_mid = apply_norm(x_ref[...].astype(F32) + ahat * scale_attn)
    one_grad = dy_ref[...].astype(F32) + norm_backward(mid * scale_mid, h1hat, fac_mid)
    one_ref[...] = one_grad
    grad_ref[...] = norm_backward(one_grad * scale_attn, ahat, fac_attn).astype(BF)
    add_gain(gain_ref, [mid * h1hat, one_grad * ahat])


def post_in_body(flag_ref, total_ref, third_ref, one_ref, x_ref, scale_ref, out_ref):
    grad = choose(flag_ref, total_ref, third_ref)
    xhat, factor = apply_norm(x_ref[...].astype(F32))
    back = norm_backward(grad * scale_ref[0:1, :], xhat, factor)
    out_ref[...] = (one_ref[...] + back).astype(BF)


def skip_ref(body, index, *refs):
    body(*refs[:index], *refs[index + 1 :])


def post(body, flag, pair_values, chunk_arrays, row_arrays, k, scales, outs, gain=False, into=None):
    rows, width = pair_values[0].shape
    steps = 2 if rows >= 128 else 1
    tile = (rows // steps, width)
    chunk = pl.BlockSpec(tile, lambda i: (i, 0))
    row = pl.BlockSpec(tile, lambda i: (k * steps + i, 0))
    located, located_specs = [], []
    for values in chunk_arrays:
        size = values[0].shape[0]
        base = (k * rows % size) // tile[0]
        located.append(values[k * rows // size])
        located_specs.append(pl.BlockSpec(tile, lambda i, base=base: (base + i, 0)))
    arrays = [flag, *pair_values, *located, *row_arrays, scales]
    specs = [pl.BlockSpec(memory_space=pltpu.SMEM), chunk, chunk, *located_specs]
    specs += [row] * len(row_arrays) + [whole(scales.shape)]
    out_shapes = [shape((rows, width), dtype) for dtype in outs]
    out_specs = [chunk] * len(outs)
    if gain:
        out_shapes.append(shape((8, width), F32))
        out_specs.append(whole((8, width)))
    aliases = {}
    if into is not None:
        total, previous = into
        out_shapes[0], out_specs[0] = shape((total, width), outs[0]), row
        if previous is not None:
            aliases = {len(arrays): 0}
            body = functools.partial(skip_ref, body, len(arrays))
            arrays.append(previous)
            specs.append(pl.BlockSpec(memory_space=pl.ANY))
    return call(
        body,
        tuple(out_shapes),
        (steps,),
        specs,
        tuple(out_specs),
        flops=20 * rows * width,
        moved=14 * rows * width,
        aliases=aliases,
    )(*arrays)


def ffn_body(n_x, n_out, *refs):
    xs, (wg_ref, wu_ref, wd_ref) = refs[:n_x], refs[n_x : n_x + 3]
    gate_ref, up_ref, hid_ref = refs[n_x + 3 : n_x + 6]
    outs, (x_ref, acc) = refs[n_x + 6 : n_x + 6 + n_out], refs[n_x + 6 + n_out :]
    j = pl.program_id(0)

    @pl.when(j == 0)
    def _():
        gather_rows(xs, x_ref)
        acc[...] = jnp.zeros_like(acc)

    x = x_ref[...]
    gate = mm(x, wg_ref[...])
    up = mm(x, wu_ref[...])
    bend = jnp.tanh(GELU_C * (gate + GELU_A * gate * gate * gate))
    hidden = (0.5 * gate * (1.0 + bend) * up).astype(BF)
    gate_ref[...] = gate.astype(BF)
    up_ref[...] = up.astype(BF)
    hid_ref[...] = hidden
    acc[...] += mm_t(hidden, wd_ref[...])

    @pl.when(j == pl.num_programs(0) - 1)
    def _():
        put_chunks(acc[...], outs)


def gather_rows(pieces, out_ref):
    size = pieces[0].shape[0]
    for i, piece in enumerate(pieces):
        out_ref[i * size : (i + 1) * size, :] = piece[...]


def ffn(xs, weights, ff, n_out):
    width = xs[0].shape[1]
    rows = xs[0].shape[0] * len(xs)
    tile = 256
    steps = ff // tile
    col = lambda part: pl.BlockSpec((width, tile), lambda j: (0, part * steps + j))
    act = pl.BlockSpec((rows, tile), lambda j: (0, j))
    part = (rows // n_out, width)
    return call(
        functools.partial(ffn_body, len(xs), n_out),
        (shape((rows, ff), BF),) * 3 + (shape(part, BF),) * n_out,
        (steps,),
        [whole(xs[0].shape)] * len(xs) + [col(0), col(1), col(2)],
        (act, act, act) + (whole(part),) * n_out,
        [pltpu.VMEM((rows, width), BF), pltpu.VMEM((rows, width), F32)],
        flops=6 * rows * width * ff,
        moved=6 * width * ff + 4 * rows * width + 6 * rows * ff,
    )(*xs, weights, weights, weights)


def ffn_back_body(n_y, n_out, *refs):
    ys, (wg_ref, wu_ref, wd_ref, gate_ref, up_ref) = refs[:n_y], refs[n_y : n_y + 5]
    rest = refs[n_y + 5 :]
    both_ref, outs, (y_ref, acc) = rest[0], rest[1 : 1 + n_out], rest[1 + n_out :]
    tile = gate_ref.shape[1]
    j = pl.program_id(0)

    @pl.when(j == 0)
    def _():
        gather_rows(ys, y_ref)
        acc[...] = jnp.zeros_like(acc)

    grad = mm(y_ref[...], wd_ref[...])
    gate, up = gate_ref[...].astype(F32), up_ref[...].astype(F32)
    square = gate * gate
    bend = jnp.tanh(GELU_C * gate * (1.0 + GELU_A * square))
    rise = 0.5 * (1.0 + bend)
    slope = rise + 0.5 * gate * (1.0 - bend * bend) * (GELU_C * (1.0 + 3.0 * GELU_A * square))
    d_gate = (grad * up * slope).astype(BF)
    d_up = (grad * (gate * rise)).astype(BF)
    both_ref[:, :tile] = d_gate
    both_ref[:, tile:] = d_up
    acc[...] += mm_t(d_gate, wg_ref[...]) + mm_t(d_up, wu_ref[...])

    @pl.when(j == pl.num_programs(0) - 1)
    def _():
        put_chunks(acc[...], outs)


FF_TILE = 256


def ffn_back(ys, weights, gate, up, ff, n_out):
    width = ys[0].shape[1]
    rows = ys[0].shape[0] * len(ys)
    tile = FF_TILE
    steps = ff // tile
    col = lambda part: pl.BlockSpec((width, tile), lambda j: (0, part * steps + j))
    act = pl.BlockSpec((rows, tile), lambda j: (0, j))
    part = (rows // n_out, width)
    return call(
        functools.partial(ffn_back_body, len(ys), n_out),
        (shape((rows, 2 * ff), BF),) + (shape(part, BF),) * n_out,
        (steps,),
        [whole(ys[0].shape)] * len(ys) + [col(0), col(1), col(2), act, act],
        (pl.BlockSpec((rows, 2 * tile), lambda j: (0, j)),) + (whole(part),) * n_out,
        [pltpu.VMEM((rows, width), BF), pltpu.VMEM((rows, width), F32)],
        flops=6 * rows * width * ff,
        moved=6 * width * ff + 4 * rows * width + 8 * rows * ff,
    )(*ys, weights, weights, weights, gate, up)


def sum_body(cuts, part_ref, *outs):
    total = 0.0
    for i in range(part_ref.shape[0]):
        total = total + part_ref[i].astype(F32)
    for out, spans in zip(outs, cuts):
        at = 0
        for start, stop in spans:
            out[:, at : at + stop - start] = total[:, start:stop]
            at += stop - start


def sum_parts(parts, tile, cuts):
    n, rows, cols = parts.shape
    steps = cols // tile
    sizes = [sum(stop - start for start, stop in spans) for spans in cuts]
    return call(
        functools.partial(sum_body, cuts),
        tuple(shape((rows, size * steps), F32) for size in sizes),
        (steps,),
        [pl.BlockSpec((n, rows, tile), lambda j: (0, 0, j))],
        tuple(pl.BlockSpec((rows, size), lambda j: (0, j)) for size in sizes),
        flops=n * rows * cols,
        moved=2 * n * rows * cols + 4 * rows * cols,
    )(parts)


def pack_body(*refs):
    start = 0
    for ref in refs[:-1]:
        refs[-1][:, start : start + ref.shape[1]] = ref[...].astype(BF)
        start += ref.shape[1]


def pack(arrays, steps):
    rows = arrays[0].shape[0] // steps
    cols = sum(a.shape[1] for a in arrays)
    return call(
        pack_body,
        shape((rows * steps, cols), BF),
        (steps,),
        [pl.BlockSpec((rows, a.shape[1]), lambda i: (i, 0)) for a in arrays],
        pl.BlockSpec((rows, cols), lambda i: (i, 0)),
        moved=4 * rows * steps * cols,
    )(*arrays)


class Chain:
    def __init__(self):
        self.token = None

    def after(self, *values):
        if self.token is None:
            return values
        return lax.optimization_barrier((*values, self.token))[:-1]

    def mark(self, value):
        self.token = value
        return value


class Reduce:
    def __init__(self, chain):
        self.chain, self.piece, self.first = chain, {}, {}
        self.sums, self.second, self.total, self.third = {}, {}, {}, {}
        self.line = lax.axis_size("tensor") == 4

    def send(self, k, piece):
        self.piece[k] = piece
        if self.line:
            self.first[k] = lax.ppermute(piece, "tensor", [(0, 1), (3, 2)])
        else:
            self.total[k] = lax.psum(piece.astype(F32), "tensor")

    def add(self, k):
        if self.line:
            piece, first = self.chain.after(self.piece[k], self.first[k])
            total = low(piece.astype(F32) + first.astype(F32))
            self.sums[k] = self.chain.mark(total)
            self.second[k] = lax.ppermute(total, "tensor", [(1, 2), (2, 1)])

    def join(self, k):
        if self.line:
            sums, second = self.chain.after(self.sums[k], self.second[k])
            total = low(sums.astype(F32) + second.astype(F32))
            self.total[k] = self.chain.mark(total)
            self.third[k] = lax.ppermute(total, "tensor", [(1, 0), (2, 3)])

    def load(self, pieces):
        for piece in pieces:
            self.send(len(self.piece), piece)

    def run(self, n, finish, hooks):
        for slot in range(n + 2):
            if slot < n:
                self.add(slot)
            if 0 < slot <= n:
                self.join(slot - 1)
            if slot >= 2:
                finish(slot - 2)
            if slot in hooks:
                hooks[slot]()

    def take(self, k):
        if self.line:
            return self.chain.after(self.total[k], self.third[k])
        return self.chain.after(self.total[k], self.total[k])


def local(
    tokens,
    span_order,
    w_query,
    w_key,
    value_weight,
    w_out,
    w_gate,
    w_up,
    w_down,
    gain_attn_in,
    gain_attn_out,
    gain_ffn_in,
    gain_ffn_out,
    cotangent,
):
    micros, batch, seq_dev, width = tokens.shape
    n_dp, n_ctx, n_t = lax.axis_size("dp"), lax.axis_size("ctx"), lax.axis_size("tensor")
    dpi, ctx, zi = lax.axis_index("dp"), lax.axis_index("ctx"), lax.axis_index("tensor")
    seq = seq_dev * n_ctx
    span_len = seq // span_order.shape[0]
    hd = HEAD_SIZE
    n_kv = w_key.shape[1] // hd
    n_q = w_query.shape[1] // hd
    ff = w_gate.shape[1]
    qc, kc, oc = w_query.shape[1], w_key.shape[1], w_out.shape[1]
    n_seqs, chunks = micros * batch, 2
    swap = n_ctx == 4
    pair = n_dp == 2

    row_index = jnp.arange(seq, dtype=jnp.int32)
    all_pos = span_order[row_index // span_len] * span_len + row_index % span_len
    by_dev = all_pos.reshape(n_ctx, seq_dev)
    query_pos = lax.dynamic_index_in_dim(by_dev, ctx, 0, keepdims=False)
    if swap:
        key_pos = jnp.concatenate(
            [lax.dynamic_index_in_dim(by_dev, ctx ^ j, 0, keepdims=False) for j in range(n_ctx)]
        )
    else:
        key_pos = all_pos
    qpos, kpos = query_pos[:, None], key_pos[None, :]
    cos, sin = rotation(query_pos, hd)

    lane = lax.broadcasted_iota(jnp.int32, (gain_attn_in.shape[0], PAD), 1)
    gains = jnp.zeros(lane.shape, BF)
    for i, gain in enumerate((gain_attn_in, gain_attn_out, gain_ffn_in, gain_ffn_out)):
        gains = jnp.where(lane == i, gain[:, None], gains)
    pack_attn = pack([w_query, w_key, value_weight, w_out, gains], 1)
    pack_ffn = jnp.concatenate([w_gate, w_up, w_down], axis=1)
    full_attn = lax.all_gather(pack_attn, ("dp", "ctx"), axis=0, tiled=True)
    full_ffn = lax.all_gather(pack_ffn, ("dp", "ctx"), axis=0, tiled=True)
    at_out = qc + 2 * kc
    out_block = at_out // oc
    pick = jnp.eye(8, PAD, dtype=BF)
    gain_cols = mm_t(pick, full_attn[:, at_out + oc :])
    scales = 1.0 + gain_cols

    chain = Chain()
    flips = [[(i, i ^ j) for i in range(n_ctx)] for j in range(n_ctx)]

    def half(full, owner):
        return lax.dynamic_slice_in_dim(full, owner * (width // 2), width // 2, 1)

    def swap_core(value):
        return lax.ppermute(value, "dp", [(0, 1), (1, 0)])

    def left_side(values):
        value = jnp.concatenate(chain.after(*values), axis=0)
        if not pair:
            return value
        return jnp.concatenate([half(value, dpi), swap_core(half(value, 1 - dpi))], axis=0)

    def right_side(values):
        value = jnp.concatenate(chain.after(*values), axis=0)
        return jnp.concatenate([value, swap_core(value)], axis=0) if pair else value

    def spread(grad):
        if pair:
            return lax.all_to_all(grad.reshape(n_ctx, -1, grad.shape[1]), "ctx", 0, 0)
        return lax.psum_scatter(grad, ("dp", "ctx"), scatter_dimension=0, tiled=True)[None]

    def product(left, right):
        left, right = chain.after(left, right)
        return chain.mark(tmm(left, right).astype(BF))

    def scatter(grad):
        axes = "ctx" if pair else ("dp", "ctx")
        return lax.psum_scatter(grad, axes, scatter_dimension=0, tiled=True)[None]

    token_rows = tokens.reshape(n_seqs * seq_dev, width)
    dy_rows = cotangent.reshape(n_seqs * seq_dev, width)
    xhats, _ = apply_norm(token_rows.astype(F32))
    normed = (xhats * scales[0:1]).astype(BF)
    cos_all, sin_all = jnp.tile(cos, (n_seqs, 1)), jnp.tile(sin, (n_seqs, 1))
    qkv = project(normed, full_attn, qc + 2 * kc, n_q + n_kv, cos_all, sin_all)
    kv = qkv[:, qc:]
    if swap:
        others = [lax.ppermute(kv, "ctx", flips[j]) for j in range(1, n_ctx)]
        pieces = [[(a, seq_dev, m, 0) for a in [kv] + others] for m in range(n_seqs)]
    else:
        every = lax.all_gather(kv.reshape(n_seqs, seq_dev, 2 * kc), "ctx", axis=1, tiled=True)
        every = every.reshape(n_seqs * seq, 2 * kc)
        pieces = [[(every, seq, m, 0)] for m in range(n_seqs)]

    def rows_of(value, m):
        return value[m * seq_dev : (m + 1) * seq_dev]

    st = [{}, {}]
    assert n_seqs == 2
    n_one, n_two, n_three, n_four = 4, 4, 4, 4
    inner = ((zi == 1) | (zi == n_t - 2)).astype(jnp.int32).reshape(1)
    attn_outs, normed_two, outputs, ffn_grads = [], [], [], []
    one_grads, attn_grads, input_grads = [], [], []
    gain_fin, gain_mid = [], []

    def post_attend(k):
        values = red.take(k)
        a, n = post(post_attend_body, inner, values, [], [token_rows], k, scales, [BF, BF])
        attn_outs.append(a), normed_two.append(n)
        chain.mark(n)

    def post_ffn(k):
        values, rows = red.take(k), [token_rows, dy_rows]
        out, grad, gain = post(
            post_ffn_body, inner, values, [attn_outs], rows, k, scales, [BF, BF], True
        )
        outputs.append(out), ffn_grads.append(grad), gain_fin.append(gain)
        chain.mark(grad)

    def post_mid(k):
        values, rows = red.take(k), [token_rows, dy_rows]
        one, grad, gain = post(
            post_mid_body, inner, values, [attn_outs], rows, k, scales, [F32, BF], True
        )
        one_grads.append(one), attn_grads.append(grad), gain_mid.append(gain)
        chain.mark(grad)

    def post_in(k):
        values = red.take(k)
        into = (n_seqs * seq_dev, input_grads[-1] if input_grads else None)
        (grad,) = post(
            post_in_body, inner, values, [one_grads], [token_rows], k, scales, [BF], False, into
        )
        input_grads.append(grad)
        chain.mark(grad)

    def attention(m):
        s = st[m]
        (first, *rest) = chain.after(*[p[0] for p in pieces[m]])
        s["pieces"] = [(v,) + p[1:] for v, p in zip([first, *rest], pieces[m])]
        s["heads"], s["attended"], s["den"], *part = attend(
            qkv, m, s["pieces"], qpos, kpos, n_q, n_kv, full_attn, out_block, n_one // 2
        )
        chain.mark(part[0])
        red.load(part)

    red = Reduce(chain)
    attention(0)
    attention(1)
    held = {}

    def hold(name, make):
        def run():
            held[name] = make()

        return run

    red.run(
        n_one, post_attend, {n_one + 1: hold("left", lambda: chain.mark(left_side([normed])))}
    )

    red = Reduce(chain)
    values = chain.after(*normed_two)
    gate, up, hidden, *part = ffn(list(values), full_ffn, ff, n_two)
    chain.mark(part[0])
    red.load(part)
    red.run(
        n_two,
        post_ffn,
        {
            0: hold("down_right", lambda: right_side([hidden])),
            1: hold("mid_left", lambda: left_side(normed_two)),
        },
    )

    red = Reduce(chain)
    values = chain.after(*ffn_grads)
    d_both, *part = ffn_back(list(values), full_ffn, gate, up, ff, n_three)
    chain.mark(part[0])
    red.load(part)
    both_right = right_side([d_both])
    down_left = left_side(ffn_grads)

    def attention_back(m):
        s = st[m]
        size = n_three // 2
        grads = chain.after(*attn_grads[size * m : size * (m + 1)])
        s["q_back"], *s["terms"] = attend_back(
            qkv,
            m,
            s["pieces"],
            qpos,
            kpos,
            list(grads),
            s["heads"],
            s["den"],
            cos,
            sin,
            n_q,
            n_kv,
            full_attn,
            out_block,
        )
        chain.mark(s["q_back"])
        if swap:
            s["moved"] = [
                lax.ppermute(s["terms"][j].astype(BF), "ctx", flips[j]) for j in range(1, n_ctx)
            ]
        else:
            s["moved"] = [lax.psum_scatter(s["terms"][0], "ctx", scatter_dimension=0, tiled=True)]

    red.run(
        n_three,
        post_mid,
        {
            0: hold("g_down", lambda: scatter(product(down_left, held["down_right"]))),
            1: hold("g_gate_up", lambda: scatter(product(held["mid_left"], both_right))),
            3: lambda: attention_back(0),
        },
    )
    attention_back(1)

    def input_back(m):
        s = st[m]
        moved = list(chain.after(*s["moved"]))
        terms = [s["terms"][0]] + moved if swap else moved
        s["qkv_back"], s["gain"], *part = input_back_call(
            s["q_back"], terms, token_rows, m, cos, sin, full_attn, n_q, n_kv, n_four // 2
        )
        chain.mark(part[0])
        red.load(part)

    def tail():
        d_qkv = product(held["left"], held["right"])
        owner = zi == 0
        gain_cols = jnp.stack(
            [
                st[0]["gain"][0] + st[1]["gain"][0],
                jnp.where(owner, sum(v[1] for v in gain_mid), 0.0),
                jnp.where(owner, sum(v[0] for v in gain_mid), 0.0),
                jnp.where(owner, sum(v[0] for v in gain_fin), 0.0),
            ],
            axis=1,
        )
        if pair:
            keep = lax.dynamic_slice_in_dim(gain_cols, dpi * (width // 2), width // 2, 0)
            give = lax.dynamic_slice_in_dim(gain_cols, (1 - dpi) * (width // 2), width // 2, 0)
            gain_cols = keep + swap_core(give)
        gain_cols = jnp.pad(gain_cols, ((0, 0), (0, PAD - gain_cols.shape[1])))
        packed = chain.mark(pack(list(chain.after(d_qkv, d_out, gain_cols)), 2))
        held["g_tail"] = spread(packed)

    def finish_down():
        (value,) = chain.after(held["g_down"])
        (held["g_down"],) = sum_parts(value, ff // 3, [[(0, ff // 3)]])
        chain.mark(held["g_down"])

    def finish_both():
        (value,) = chain.after(held["g_gate_up"])
        group = 6 * FF_TILE
        starts = range(0, group, 2 * FF_TILE)
        cuts = [[(i + o, i + o + FF_TILE) for i in starts] for o in (0, FF_TILE)]
        held["g_gate"], held["g_up"] = sum_parts(value, group, cuts)
        chain.mark(held["g_up"])

    def finish_tail():
        (value,) = chain.after(held["g_tail"])
        ends = [0, qc, qc + kc, at_out, at_out + oc, at_out + oc + PAD]
        *held["g_attn"], g_gains = sum_parts(value, ends[-1], [[v] for v in zip(ends, ends[1:])])
        g_gains = chain.mark(mm_t(pick.astype(F32), g_gains))
        held["g_gains"] = lax.all_to_all(
            jnp.broadcast_to(g_gains[None], (n_t,) + g_gains.shape), "tensor", 0, 0
        )

    red = Reduce(chain)
    input_back(0)
    d_out = product(left_side(attn_grads), right_side([s["attended"] for s in st]))
    finish_down()
    input_back(1)
    held["right"] = right_side([s["qkv_back"] for s in st])

    def finish_rest():
        finish_both()
        finish_tail()

    red.run(n_four, post_in, {1: tail, 4: finish_rest})
    g_gains = jnp.sum(held["g_gains"], axis=0)
    return (
        jnp.concatenate(outputs, axis=0).reshape(tokens.shape),
        input_grads[-1].reshape(tokens.shape),
        *held["g_attn"],
        held["g_gate"],
        held["g_up"],
        held["g_down"],
        g_gains[0],
        g_gains[1],
        g_gains[2],
        g_gains[3],
    )


def solution(mesh):
    act = P(None, "dp", "ctx", None)
    mat = P(("dp", "ctx"), "tensor")
    vec = P(("dp", "ctx"))
    return jax.shard_map(
        local,
        mesh=mesh,
        in_specs=(act, P()) + (mat,) * 7 + (vec,) * 4 + (act,),
        out_specs=(act, act) + (mat,) * 7 + (vec,) * 4,
        check_vma=False,
    )
```

```python
import functools

import jax
import jax.numpy as jnp
from jax import lax
from jax.experimental import pallas as pl
from jax.experimental.pallas import tpu as pltpu
from jax.sharding import PartitionSpec as P

HEAD_SIZE = 256
EPS = 1e-06
CAP = 50.0
BASE = 10000.0
BF = jnp.bfloat16
F32 = jnp.float32
PAD = 128
VMEM_LIMIT = 60 * 1024 * 1024
GELU_C = 0.7978845608028654
GELU_A = 0.044715


def apply_norm(values):
    factor = lax.rsqrt(jnp.mean(values * values, axis=-1, keepdims=True) + EPS)
    return values * factor, factor


def norm_backward(upstream, scaled, factor):
    return factor * (upstream - scaled * jnp.mean(upstream * scaled, axis=-1, keepdims=True))


def rotation(token_positions, width_size):
    half_width = width_size // 2
    inverse = BASE ** (-(jnp.arange(half_width, dtype=F32) * 2.0) / width_size)
    angles = token_positions.astype(F32)[:, None] * inverse[None, :]
    return jnp.cos(angles), jnp.sin(angles)


def mm(a, b):
    return jnp.dot(a, b, preferred_element_type=F32)


def mm_t(a, b):
    return lax.dot_general(a, b, (((1,), (1,)), ((), ())), preferred_element_type=F32)


def tmm(a, b):
    return lax.dot_general(a, b, (((0,), (0,)), ((), ())), preferred_element_type=F32)


def low(values):
    return lax.reduce_precision(values, 8, 7).astype(BF)


def call(body, out_shape, grid, in_specs, out_specs, scratch=(), flops=0, moved=0, aliases=None):
    return pl.pallas_call(
        body,
        out_shape=out_shape,
        input_output_aliases=aliases or {},
        grid_spec=pltpu.PrefetchScalarGridSpec(
            num_scalar_prefetch=0,
            grid=grid,
            in_specs=in_specs,
            out_specs=out_specs,
            scratch_shapes=list(scratch),
        ),
        compiler_params=pltpu.CompilerParams(
            dimension_semantics=("arbitrary",) * len(grid), vmem_limit_bytes=VMEM_LIMIT
        ),
        cost_estimate=pl.CostEstimate(flops=flops, bytes_accessed=moved, transcendentals=0),
    )


def shape(dims, dtype):
    return jax.ShapeDtypeStruct(dims, dtype)


def whole(dims):
    return pl.BlockSpec(dims, lambda *_: (0,) * len(dims))


def project_body(n_rot, x_ref, w_ref, cos_ref, sin_ref, out_ref):
    half = HEAD_SIZE // 2
    y = mm(x_ref[...], w_ref[...])
    rotate = pl.program_id(0) < n_rot
    cos = jnp.where(rotate, cos_ref[...], 1.0)
    sin = jnp.where(rotate, sin_ref[...], 0.0)
    a, b = y[:, :half], y[:, half:]
    out_ref[:, :half] = (a * cos - b * sin).astype(BF)
    out_ref[:, half:] = (b * cos + a * sin).astype(BF)


def project(normed, weights, columns, n_rot, cos, sin):
    rows, width = normed.shape
    return call(
        functools.partial(project_body, n_rot),
        shape((rows, columns), BF),
        (columns // HEAD_SIZE,),
        [
            whole((rows, width)),
            pl.BlockSpec((width, HEAD_SIZE), lambda j: (0, j)),
            whole(cos.shape),
            whole(sin.shape),
        ],
        pl.BlockSpec((rows, HEAD_SIZE), lambda j: (0, j)),
        flops=2 * rows * width * columns,
        moved=2 * (rows * width + width * columns + rows * columns),
    )(normed, weights, cos, sin)


def scores(q, k, allowed):
    soft = HEAD_SIZE ** (-0.5)
    bend = jnp.tanh(mm_t(q, k) * (soft / CAP))
    return bend, jnp.where(allowed, jnp.exp(CAP * bend), 0.0)


def attend_body(n_q, n_kv, n_pieces, chunks, *refs):
    hd = HEAD_SIZE
    q_ref, qpos_ref, kpos_ref, w_ref = refs[:4]
    pieces = refs[4 : 4 + n_pieces]
    heads_ref, attended_ref, den_ref = refs[4 + n_pieces : 7 + n_pieces]
    outs = refs[7 + n_pieces :]
    qpos = qpos_ref[...]
    for h in range(n_q):
        kv = h // (n_q // n_kv)
        q = q_ref[:, h * hd : (h + 1) * hd]
        num, den = 0.0, 0.0
        for j, piece in enumerate(pieces):
            size = piece.shape[0]
            allowed = kpos_ref[:, j * size : (j + 1) * size] <= qpos
            _, weight = scores(q, piece[:, kv * hd : (kv + 1) * hd], allowed)
            den = den + jnp.sum(weight, axis=-1, keepdims=True)
            v = piece[:, (n_kv + kv) * hd : (n_kv + kv + 1) * hd]
            num = num + mm(weight.astype(BF), v)
        heads = num / den
        heads_ref[:, h * hd : (h + 1) * hd] = heads
        attended_ref[:, h * hd : (h + 1) * hd] = heads.astype(BF)
        den_ref[:, h * PAD : (h + 1) * PAD] = jnp.broadcast_to(den, (den.shape[0], PAD))
    put_chunks(mm_t(attended_ref[...], w_ref[...]), outs)


def put_chunks(value, outs):
    size = value.shape[0] // len(outs)
    for i, out in enumerate(outs):
        out[...] = value[i * size : (i + 1) * size].astype(BF)


def attend(q, q_block, pieces, qpos, kpos, n_q, n_kv, weights, out_block, chunks):
    hd = HEAD_SIZE
    seq_dev = qpos.shape[0]
    width = weights.shape[0]
    specs = [pl.BlockSpec((seq_dev, n_q * hd), lambda i: (q_block, 0))]
    specs += [whole(qpos.shape), whole(kpos.shape)]
    specs.append(pl.BlockSpec((width, n_q * hd), lambda i: (0, out_block)))
    arrays = [q, qpos, kpos, weights]
    for array, size, row, col in pieces:
        specs.append(pl.BlockSpec((size, 2 * n_kv * hd), lambda i, row=row, col=col: (row, col)))
        arrays.append(array)
    seq = kpos.shape[1]
    part = (seq_dev // chunks, width)
    return call(
        functools.partial(attend_body, n_q, n_kv, len(pieces), chunks),
        (
            shape((seq_dev, n_q * hd), F32),
            shape((seq_dev, n_q * hd), BF),
            shape((seq_dev, n_q * PAD), F32),
        )
        + (shape(part, BF),) * chunks,
        (1,),
        specs,
        (whole((seq_dev, n_q * hd)), whole((seq_dev, n_q * hd)), whole((seq_dev, n_q * PAD)))
        + (whole(part),) * chunks,
        flops=4 * n_q * seq_dev * seq * hd + 2 * seq_dev * n_q * hd * width,
        moved=2 * (2 * n_kv * hd * seq + 4 * seq_dev * n_q * hd + 2 * n_q * hd * width),
    )(*arrays)


def attend_back_body(n_q, n_kv, n_pieces, chunks, *refs):
    hd = HEAD_SIZE
    half = hd // 2
    soft = hd ** (-0.5)
    q_ref, qpos_ref, kpos_ref, heads_ref, den_ref, cos_ref, sin_ref, w_ref = refs[:8]
    pieces = refs[8 : 8 + n_pieces]
    grads = refs[8 + n_pieces : 8 + n_pieces + chunks]
    q_back_ref, *outs = refs[8 + n_pieces + chunks :]
    attn_grad = jnp.concatenate([g[...] for g in grads], axis=0)
    qpos = qpos_ref[...]
    group = n_q // n_kv
    for h in range(n_q):
        kv = h // group
        cols = slice(h * hd, (h + 1) * hd)
        k_cols = slice(kv * hd, (kv + 1) * hd)
        v_cols = slice((n_kv + kv) * hd, (n_kv + kv + 1) * hd)
        q = q_ref[:, cols]
        grad = mm(attn_grad, w_ref[:, cols])
        inverse = 1.0 / den_ref[:, h * PAD : h * PAD + 1]
        scaled = (grad * inverse).astype(BF)
        row_dot = jnp.sum(grad * heads_ref[:, cols], axis=-1, keepdims=True) * inverse
        q_grad = 0.0
        for j, piece in enumerate(pieces):
            size = piece.shape[0]
            allowed = kpos_ref[:, j * size : (j + 1) * size] <= qpos
            k, v = piece[:, k_cols], piece[:, v_cols]
            bend, weight = scores(q, k, allowed)
            prob = mm_t(scaled, v)
            score = (weight * (prob - row_dot) * (1.0 - bend * bend)).astype(BF)
            q_grad = q_grad + mm(score, k)
            k_term = tmm(score, q) * soft
            v_term = tmm(weight.astype(BF), scaled)
            if h % group == 0:
                outs[j][:, k_cols] = k_term
                outs[j][:, v_cols] = v_term
            else:
                outs[j][:, k_cols] += k_term
                outs[j][:, v_cols] += v_term
        q_grad = q_grad * soft
        a, b = q_grad[:, :half], q_grad[:, half:]
        q_back_ref[:, h * hd : h * hd + half] = (a * cos_ref[...] + b * sin_ref[...]).astype(BF)
        q_back_ref[:, h * hd + half : (h + 1) * hd] = (
            b * cos_ref[...] - a * sin_ref[...]
        ).astype(BF)


def attend_back(q, q_block, pieces, qpos, kpos, grads, heads, den, cos, sin, n_q, n_kv, weights, out_block):
    hd = HEAD_SIZE
    seq_dev = qpos.shape[0]
    width = weights.shape[0]
    specs = [pl.BlockSpec((seq_dev, n_q * hd), lambda i: (q_block, 0))]
    arrays = [q, qpos, kpos, heads, den, cos, sin]
    specs += [whole(a.shape) for a in arrays[1:]]
    specs.append(pl.BlockSpec((width, n_q * hd), lambda i: (0, out_block)))
    arrays.append(weights)
    out_shapes, out_specs = [shape((seq_dev, n_q * hd), BF)], [whole((seq_dev, n_q * hd))]
    for array, size, row, col in pieces:
        specs.append(pl.BlockSpec((size, 2 * n_kv * hd), lambda i, row=row, col=col: (row, col)))
        arrays.append(array)
        out_shapes.append(shape((size, 2 * n_kv * hd), F32))
        out_specs.append(whole((size, 2 * n_kv * hd)))
    arrays += grads
    specs += [whole(g.shape) for g in grads]
    seq = kpos.shape[1]
    return call(
        functools.partial(attend_back_body, n_q, n_kv, len(pieces), len(grads)),
        tuple(out_shapes),
        (1,),
        specs,
        tuple(out_specs),
        flops=10 * n_q * seq_dev * seq * hd + 2 * seq_dev * n_q * hd * width,
        moved=2 * (6 * n_kv * hd * seq + 8 * seq_dev * n_q * hd + 2 * n_q * hd * width),
    )(*arrays)


def input_back_body(n_q, n_kv, n_terms, chunks, *refs):
    hd = HEAD_SIZE
    half = hd // 2
    kc = n_kv * hd
    q_back_ref, x_ref, cos_ref, sin_ref, w_ref = refs[:5]
    terms = refs[5 : 5 + n_terms]
    back_ref, gain_ref, *outs = refs[5 + n_terms :]
    total = 0.0
    for term in terms:
        total = total + term[...].astype(F32)
    back_ref[:, : n_q * hd] = q_back_ref[...]
    for h in range(n_kv):
        start = (n_q + h) * hd
        a = total[:, h * hd : h * hd + half]
        b = total[:, h * hd + half : (h + 1) * hd]
        back_ref[:, start : start + half] = (a * cos_ref[...] + b * sin_ref[...]).astype(BF)
        back_ref[:, start + half : start + hd] = (b * cos_ref[...] - a * sin_ref[...]).astype(BF)
    back_ref[:, n_q * hd + kc :] = total[:, kc:].astype(BF)
    grad = mm_t(back_ref[...], w_ref[...])
    xhat, _ = apply_norm(x_ref[...].astype(F32))
    gain_ref[...] = jnp.broadcast_to(jnp.sum(grad * xhat, axis=0, keepdims=True), gain_ref.shape)
    put_chunks(grad, outs)


def input_back_call(q_back, terms, x, block, cos, sin, weights, n_q, n_kv, chunks):
    hd = HEAD_SIZE
    seq_dev = q_back.shape[0]
    width = weights.shape[0]
    cols = (n_q + 2 * n_kv) * hd
    part = (seq_dev // chunks, width)
    return call(
        functools.partial(input_back_body, n_q, n_kv, len(terms), chunks),
        (shape((seq_dev, cols), BF), shape((8, width), F32)) + (shape(part, BF),) * chunks,
        (1,),
        [
            whole(q_back.shape),
            pl.BlockSpec((seq_dev, width), lambda i: (block, 0)),
            whole(cos.shape),
            whole(sin.shape),
            pl.BlockSpec((width, cols), lambda i: (0, 0)),
        ]
        + [whole(t.shape) for t in terms],
        (whole((seq_dev, cols)), whole((8, width))) + (whole(part),) * chunks,
        flops=2 * seq_dev * cols * width,
        moved=2 * (width * cols + 3 * seq_dev * width + 4 * seq_dev * cols),
    )(q_back, x, cos, sin, weights, *terms)


def choose(flag_ref, total_ref, third_ref):
    total, third = total_ref[...].astype(F32), third_ref[...].astype(F32)
    return jnp.where(flag_ref[0] == 1, total, third)


def add_gain(gain_ref, rows):
    @pl.when(pl.program_id(0) == 0)
    def _():
        gain_ref[...] = jnp.zeros_like(gain_ref)

    for i, value in enumerate(rows):
        gain_ref[i : i + 1, :] += jnp.sum(value, axis=0, keepdims=True)


def post_attend_body(flag_ref, total_ref, third_ref, x_ref, scale_ref, a_ref, out_ref):
    value = choose(flag_ref, total_ref, third_ref)
    ahat, _ = apply_norm(value)
    h1hat, _ = apply_norm(x_ref[...].astype(F32) + ahat * scale_ref[1:2, :])
    a_ref[...] = value.astype(BF)
    out_ref[...] = (h1hat * scale_ref[2:3, :]).astype(BF)


def post_ffn_body(
    flag_ref, total_ref, third_ref, a_ref, x_ref, dy_ref, scale_ref, out_ref, grad_ref, gain_ref
):
    fhat, factor = apply_norm(choose(flag_ref, total_ref, third_ref))
    ahat, _ = apply_norm(a_ref[...].astype(F32))
    hidden_one = x_ref[...].astype(F32) + ahat * scale_ref[1:2, :]
    scale = scale_ref[3:4, :]
    dy = dy_ref[...].astype(F32)
    out_ref[...] = (hidden_one + fhat * scale).astype(BF)
    grad_ref[...] = norm_backward(dy * scale, fhat, factor).astype(BF)
    add_gain(gain_ref, [dy * fhat])


def post_mid_body(
    flag_ref, total_ref, third_ref, a_ref, x_ref, dy_ref, scale_ref, one_ref, grad_ref, gain_ref
):
    mid = choose(flag_ref, total_ref, third_ref)
    ahat, fac_attn = apply_norm(a_ref[...].astype(F32))
    scale_attn, scale_mid = scale_ref[1:2, :], scale_ref[2:3, :]
    h1hat, fac_mid = apply_norm(x_ref[...].astype(F32) + ahat * scale_attn)
    one_grad = dy_ref[...].astype(F32) + norm_backward(mid * scale_mid, h1hat, fac_mid)
    one_ref[...] = one_grad
    grad_ref[...] = norm_backward(one_grad * scale_attn, ahat, fac_attn).astype(BF)
    add_gain(gain_ref, [mid * h1hat, one_grad * ahat])


def post_in_body(flag_ref, total_ref, third_ref, one_ref, x_ref, scale_ref, out_ref):
    grad = choose(flag_ref, total_ref, third_ref)
    xhat, factor = apply_norm(x_ref[...].astype(F32))
    back = norm_backward(grad * scale_ref[0:1, :], xhat, factor)
    out_ref[...] = (one_ref[...] + back).astype(BF)


def skip_ref(body, index, *refs):
    body(*refs[:index], *refs[index + 1 :])


def post(body, flag, pair_values, chunk_arrays, row_arrays, k, scales, outs, gain=False, into=None):
    rows, width = pair_values[0].shape
    steps = 2 if rows >= 128 else 1
    tile = (rows // steps, width)
    chunk = pl.BlockSpec(tile, lambda i: (i, 0))
    row = pl.BlockSpec(tile, lambda i: (k * steps + i, 0))
    located, located_specs = [], []
    for values in chunk_arrays:
        size = values[0].shape[0]
        base = (k * rows % size) // tile[0]
        located.append(values[k * rows // size])
        located_specs.append(pl.BlockSpec(tile, lambda i, base=base: (base + i, 0)))
    arrays = [flag, *pair_values, *located, *row_arrays, scales]
    specs = [pl.BlockSpec(memory_space=pltpu.SMEM), chunk, chunk, *located_specs]
    specs += [row] * len(row_arrays) + [whole(scales.shape)]
    out_shapes = [shape((rows, width), dtype) for dtype in outs]
    out_specs = [chunk] * len(outs)
    if gain:
        out_shapes.append(shape((8, width), F32))
        out_specs.append(whole((8, width)))
    aliases = {}
    if into is not None:
        total, previous = into
        out_shapes[0], out_specs[0] = shape((total, width), outs[0]), row
        if previous is not None:
            aliases = {len(arrays): 0}
            body = functools.partial(skip_ref, body, len(arrays))
            arrays.append(previous)
            specs.append(pl.BlockSpec(memory_space=pl.ANY))
    return call(
        body,
        tuple(out_shapes),
        (steps,),
        specs,
        tuple(out_specs),
        flops=20 * rows * width,
        moved=14 * rows * width,
        aliases=aliases,
    )(*arrays)


def ffn_body(n_x, n_out, *refs):
    xs, (wg_ref, wu_ref, wd_ref) = refs[:n_x], refs[n_x : n_x + 3]
    gate_ref, up_ref, hid_ref = refs[n_x + 3 : n_x + 6]
    outs, (x_ref, acc) = refs[n_x + 6 : n_x + 6 + n_out], refs[n_x + 6 + n_out :]
    j = pl.program_id(0)

    @pl.when(j == 0)
    def _():
        gather_rows(xs, x_ref)
        acc[...] = jnp.zeros_like(acc)

    x = x_ref[...]
    gate = mm(x, wg_ref[...])
    up = mm(x, wu_ref[...])
    bend = jnp.tanh(GELU_C * (gate + GELU_A * gate * gate * gate))
    hidden = (0.5 * gate * (1.0 + bend) * up).astype(BF)
    gate_ref[...] = gate.astype(BF)
    up_ref[...] = up.astype(BF)
    hid_ref[...] = hidden
    acc[...] += mm_t(hidden, wd_ref[...])

    @pl.when(j == pl.num_programs(0) - 1)
    def _():
        put_chunks(acc[...], outs)


def gather_rows(pieces, out_ref):
    size = pieces[0].shape[0]
    for i, piece in enumerate(pieces):
        out_ref[i * size : (i + 1) * size, :] = piece[...]


def ffn(xs, weights, ff, n_out):
    width = xs[0].shape[1]
    rows = xs[0].shape[0] * len(xs)
    tile = 256
    steps = ff // tile
    col = lambda part: pl.BlockSpec((width, tile), lambda j: (0, part * steps + j))
    act = pl.BlockSpec((rows, tile), lambda j: (0, j))
    part = (rows // n_out, width)
    return call(
        functools.partial(ffn_body, len(xs), n_out),
        (shape((rows, ff), BF),) * 3 + (shape(part, BF),) * n_out,
        (steps,),
        [whole(xs[0].shape)] * len(xs) + [col(0), col(1), col(2)],
        (act, act, act) + (whole(part),) * n_out,
        [pltpu.VMEM((rows, width), BF), pltpu.VMEM((rows, width), F32)],
        flops=6 * rows * width * ff,
        moved=6 * width * ff + 4 * rows * width + 6 * rows * ff,
    )(*xs, weights, weights, weights)


def ffn_back_body(n_y, n_out, *refs):
    ys, (wg_ref, wu_ref, wd_ref, gate_ref, up_ref) = refs[:n_y], refs[n_y : n_y + 5]
    rest = refs[n_y + 5 :]
    both_ref, outs, (y_ref, acc) = rest[0], rest[1 : 1 + n_out], rest[1 + n_out :]
    tile = gate_ref.shape[1]
    j = pl.program_id(0)

    @pl.when(j == 0)
    def _():
        gather_rows(ys, y_ref)
        acc[...] = jnp.zeros_like(acc)

    grad = mm(y_ref[...], wd_ref[...])
    gate, up = gate_ref[...].astype(F32), up_ref[...].astype(F32)
    square = gate * gate
    bend = jnp.tanh(GELU_C * gate * (1.0 + GELU_A * square))
    rise = 0.5 * (1.0 + bend)
    slope = rise + 0.5 * gate * (1.0 - bend * bend) * (GELU_C * (1.0 + 3.0 * GELU_A * square))
    d_gate = (grad * up * slope).astype(BF)
    d_up = (grad * (gate * rise)).astype(BF)
    both_ref[:, :tile] = d_gate
    both_ref[:, tile:] = d_up
    acc[...] += mm_t(d_gate, wg_ref[...]) + mm_t(d_up, wu_ref[...])

    @pl.when(j == pl.num_programs(0) - 1)
    def _():
        put_chunks(acc[...], outs)


FF_TILE = 256


def ffn_back(ys, weights, gate, up, ff, n_out):
    width = ys[0].shape[1]
    rows = ys[0].shape[0] * len(ys)
    tile = FF_TILE
    steps = ff // tile
    col = lambda part: pl.BlockSpec((width, tile), lambda j: (0, part * steps + j))
    act = pl.BlockSpec((rows, tile), lambda j: (0, j))
    part = (rows // n_out, width)
    return call(
        functools.partial(ffn_back_body, len(ys), n_out),
        (shape((rows, 2 * ff), BF),) + (shape(part, BF),) * n_out,
        (steps,),
        [whole(ys[0].shape)] * len(ys) + [col(0), col(1), col(2), act, act],
        (pl.BlockSpec((rows, 2 * tile), lambda j: (0, j)),) + (whole(part),) * n_out,
        [pltpu.VMEM((rows, width), BF), pltpu.VMEM((rows, width), F32)],
        flops=6 * rows * width * ff,
        moved=6 * width * ff + 4 * rows * width + 8 * rows * ff,
    )(*ys, weights, weights, weights, gate, up)


def sum_body(cuts, part_ref, *outs):
    total = 0.0
    for i in range(part_ref.shape[0]):
        total = total + part_ref[i].astype(F32)
    for out, spans in zip(outs, cuts):
        at = 0
        for start, stop in spans:
            out[:, at : at + stop - start] = total[:, start:stop]
            at += stop - start


def sum_parts(parts, tile, cuts):
    n, rows, cols = parts.shape
    steps = cols // tile
    sizes = [sum(stop - start for start, stop in spans) for spans in cuts]
    return call(
        functools.partial(sum_body, cuts),
        tuple(shape((rows, size * steps), F32) for size in sizes),
        (steps,),
        [pl.BlockSpec((n, rows, tile), lambda j: (0, 0, j))],
        tuple(pl.BlockSpec((rows, size), lambda j: (0, j)) for size in sizes),
        flops=n * rows * cols,
        moved=2 * n * rows * cols + 4 * rows * cols,
    )(parts)


def pack_body(*refs):
    start = 0
    for ref in refs[:-1]:
        refs[-1][:, start : start + ref.shape[1]] = ref[...].astype(BF)
        start += ref.shape[1]


def pack(arrays, steps):
    rows = arrays[0].shape[0] // steps
    cols = sum(a.shape[1] for a in arrays)
    return call(
        pack_body,
        shape((rows * steps, cols), BF),
        (steps,),
        [pl.BlockSpec((rows, a.shape[1]), lambda i: (i, 0)) for a in arrays],
        pl.BlockSpec((rows, cols), lambda i: (i, 0)),
        moved=4 * rows * steps * cols,
    )(*arrays)


class Chain:
    def __init__(self):
        self.token = None

    def after(self, *values):
        if self.token is None:
            return values
        return lax.optimization_barrier((*values, self.token))[:-1]

    def mark(self, value):
        self.token = value
        return value


class Reduce:
    def __init__(self, chain):
        self.chain, self.piece, self.first = chain, {}, {}
        self.sums, self.second, self.total, self.third = {}, {}, {}, {}
        self.line = lax.axis_size("tensor") == 4

    def send(self, k, piece):
        self.piece[k] = piece
        if self.line:
            self.first[k] = lax.ppermute(piece, "tensor", [(0, 1), (3, 2)])
        else:
            self.total[k] = lax.psum(piece.astype(F32), "tensor")

    def add(self, k):
        if self.line:
            piece, first = self.chain.after(self.piece[k], self.first[k])
            total = low(piece.astype(F32) + first.astype(F32))
            self.sums[k] = self.chain.mark(total)
            self.second[k] = lax.ppermute(total, "tensor", [(1, 2), (2, 1)])

    def join(self, k):
        if self.line:
            sums, second = self.chain.after(self.sums[k], self.second[k])
            total = low(sums.astype(F32) + second.astype(F32))
            self.total[k] = self.chain.mark(total)
            self.third[k] = lax.ppermute(total, "tensor", [(1, 0), (2, 3)])

    def load(self, pieces):
        for piece in pieces:
            self.send(len(self.piece), piece)

    def run(self, n, finish, hooks):
        for slot in range(n + 2):
            if slot < n:
                self.add(slot)
            if 0 < slot <= n:
                self.join(slot - 1)
            if slot >= 2:
                finish(slot - 2)
            if slot in hooks:
                hooks[slot]()

    def take(self, k):
        if self.line:
            return self.chain.after(self.total[k], self.third[k])
        return self.chain.after(self.total[k], self.total[k])


def local(
    tokens,
    span_order,
    w_query,
    w_key,
    value_weight,
    w_out,
    w_gate,
    w_up,
    w_down,
    gain_attn_in,
    gain_attn_out,
    gain_ffn_in,
    gain_ffn_out,
    cotangent,
):
    micros, batch, seq_dev, width = tokens.shape
    n_dp, n_ctx, n_t = lax.axis_size("dp"), lax.axis_size("ctx"), lax.axis_size("tensor")
    dpi, ctx, zi = lax.axis_index("dp"), lax.axis_index("ctx"), lax.axis_index("tensor")
    seq = seq_dev * n_ctx
    span_len = seq // span_order.shape[0]
    hd = HEAD_SIZE
    n_kv = w_key.shape[1] // hd
    n_q = w_query.shape[1] // hd
    ff = w_gate.shape[1]
    qc, kc, oc = w_query.shape[1], w_key.shape[1], w_out.shape[1]
    n_seqs, chunks = micros * batch, 2
    swap = n_ctx == 4
    pair = n_dp == 2

    row_index = jnp.arange(seq, dtype=jnp.int32)
    all_pos = span_order[row_index // span_len] * span_len + row_index % span_len
    by_dev = all_pos.reshape(n_ctx, seq_dev)
    query_pos = lax.dynamic_index_in_dim(by_dev, ctx, 0, keepdims=False)
    if swap:
        key_pos = jnp.concatenate(
            [lax.dynamic_index_in_dim(by_dev, ctx ^ j, 0, keepdims=False) for j in range(n_ctx)]
        )
    else:
        key_pos = all_pos
    qpos, kpos = query_pos[:, None], key_pos[None, :]
    cos, sin = rotation(query_pos, hd)

    lane = lax.broadcasted_iota(jnp.int32, (gain_attn_in.shape[0], PAD), 1)
    gains = jnp.zeros(lane.shape, BF)
    for i, gain in enumerate((gain_attn_in, gain_attn_out, gain_ffn_in, gain_ffn_out)):
        gains = jnp.where(lane == i, gain[:, None], gains)
    pack_attn = pack([w_query, w_key, value_weight, w_out, gains], 1)
    pack_ffn = jnp.concatenate([w_gate, w_up, w_down], axis=1)
    full_attn = lax.all_gather(pack_attn, ("dp", "ctx"), axis=0, tiled=True)
    full_ffn = lax.all_gather(pack_ffn, ("dp", "ctx"), axis=0, tiled=True)
    at_out = qc + 2 * kc
    out_block = at_out // oc
    pick = jnp.eye(8, PAD, dtype=BF)
    gain_cols = mm_t(pick, full_attn[:, at_out + oc :])
    scales = 1.0 + gain_cols

    chain = Chain()
    flips = [[(i, i ^ j) for i in range(n_ctx)] for j in range(n_ctx)]

    def half(full, owner):
        return lax.dynamic_slice_in_dim(full, owner * (width // 2), width // 2, 1)

    def swap_core(value):
        return lax.ppermute(value, "dp", [(0, 1), (1, 0)])

    def left_side(values):
        value = jnp.concatenate(chain.after(*values), axis=0)
        if not pair:
            return value
        return jnp.concatenate([half(value, dpi), swap_core(half(value, 1 - dpi))], axis=0)

    def right_side(values):
        value = jnp.concatenate(chain.after(*values), axis=0)
        return jnp.concatenate([value, swap_core(value)], axis=0) if pair else value

    def spread(grad):
        if pair:
            return lax.all_to_all(grad.reshape(n_ctx, -1, grad.shape[1]), "ctx", 0, 0)
        return lax.psum_scatter(grad, ("dp", "ctx"), scatter_dimension=0, tiled=True)[None]

    def product(left, right):
        left, right = chain.after(left, right)
        return chain.mark(tmm(left, right).astype(BF))

    def scatter(grad):
        axes = "ctx" if pair else ("dp", "ctx")
        return lax.psum_scatter(grad, axes, scatter_dimension=0, tiled=True)[None]

    token_rows = tokens.reshape(n_seqs * seq_dev, width)
    dy_rows = cotangent.reshape(n_seqs * seq_dev, width)
    xhats, _ = apply_norm(token_rows.astype(F32))
    normed = (xhats * scales[0:1]).astype(BF)
    cos_all, sin_all = jnp.tile(cos, (n_seqs, 1)), jnp.tile(sin, (n_seqs, 1))
    qkv = project(normed, full_attn, qc + 2 * kc, n_q + n_kv, cos_all, sin_all)
    kv = qkv[:, qc:]
    if swap:
        others = [lax.ppermute(kv, "ctx", flips[j]) for j in range(1, n_ctx)]
        pieces = [[(a, seq_dev, m, 0) for a in [kv] + others] for m in range(n_seqs)]
    else:
        every = lax.all_gather(kv.reshape(n_seqs, seq_dev, 2 * kc), "ctx", axis=1, tiled=True)
        every = every.reshape(n_seqs * seq, 2 * kc)
        pieces = [[(every, seq, m, 0)] for m in range(n_seqs)]

    def rows_of(value, m):
        return value[m * seq_dev : (m + 1) * seq_dev]

    st = [{}, {}]
    assert n_seqs == 2
    n_one, n_two, n_three, n_four = 4, 4, 4, 4
    inner = ((zi == 1) | (zi == n_t - 2)).astype(jnp.int32).reshape(1)
    attn_outs, normed_two, outputs, ffn_grads = [], [], [], []
    one_grads, attn_grads, input_grads = [], [], []
    gain_fin, gain_mid = [], []

    def post_attend(k):
        values = red.take(k)
        a, n = post(post_attend_body, inner, values, [], [token_rows], k, scales, [BF, BF])
        attn_outs.append(a), normed_two.append(n)
        chain.mark(n)

    def post_ffn(k):
        values, rows = red.take(k), [token_rows, dy_rows]
        out, grad, gain = post(
            post_ffn_body, inner, values, [attn_outs], rows, k, scales, [BF, BF], True
        )
        outputs.append(out), ffn_grads.append(grad), gain_fin.append(gain)
        chain.mark(grad)

    def post_mid(k):
        values, rows = red.take(k), [token_rows, dy_rows]
        one, grad, gain = post(
            post_mid_body, inner, values, [attn_outs], rows, k, scales, [F32, BF], True
        )
        one_grads.append(one), attn_grads.append(grad), gain_mid.append(gain)
        chain.mark(grad)

    def post_in(k):
        values = red.take(k)
        into = (n_seqs * seq_dev, input_grads[-1] if input_grads else None)
        (grad,) = post(
            post_in_body, inner, values, [one_grads], [token_rows], k, scales, [BF], False, into
        )
        input_grads.append(grad)
        chain.mark(grad)

    def attention(m):
        s = st[m]
        (first, *rest) = chain.after(*[p[0] for p in pieces[m]])
        s["pieces"] = [(v,) + p[1:] for v, p in zip([first, *rest], pieces[m])]
        s["heads"], s["attended"], s["den"], *part = attend(
            qkv, m, s["pieces"], qpos, kpos, n_q, n_kv, full_attn, out_block, n_one // 2
        )
        chain.mark(part[0])
        red.load(part)

    red = Reduce(chain)
    attention(0)
    attention(1)
    held = {}

    def hold(name, make):
        def run():
            held[name] = make()

        return run

    red.run(
        n_one, post_attend, {n_one + 1: hold("left", lambda: chain.mark(left_side([normed])))}
    )

    red = Reduce(chain)
    values = chain.after(*normed_two)
    gate, up, hidden, *part = ffn(list(values), full_ffn, ff, n_two)
    chain.mark(part[0])
    red.load(part)
    red.run(
        n_two,
        post_ffn,
        {
            0: hold("down_right", lambda: right_side([hidden])),
            1: hold("mid_left", lambda: left_side(normed_two)),
        },
    )

    red = Reduce(chain)
    values = chain.after(*ffn_grads)
    d_both, *part = ffn_back(list(values), full_ffn, gate, up, ff, n_three)
    chain.mark(part[0])
    red.load(part)
    both_right = right_side([d_both])
    down_left = left_side(ffn_grads)

    def attention_back(m):
        s = st[m]
        size = n_three // 2
        grads = chain.after(*attn_grads[size * m : size * (m + 1)])
        s["q_back"], *s["terms"] = attend_back(
            qkv,
            m,
            s["pieces"],
            qpos,
            kpos,
            list(grads),
            s["heads"],
            s["den"],
            cos,
            sin,
            n_q,
            n_kv,
            full_attn,
            out_block,
        )
        chain.mark(s["q_back"])
        if swap:
            s["moved"] = [
                lax.ppermute(s["terms"][j].astype(BF), "ctx", flips[j]) for j in range(1, n_ctx)
            ]
        else:
            s["moved"] = [lax.psum_scatter(s["terms"][0], "ctx", scatter_dimension=0, tiled=True)]

    red.run(
        n_three,
        post_mid,
        {
            0: hold("g_down", lambda: scatter(product(down_left, held["down_right"]))),
            2: hold("g_gate_up", lambda: scatter(product(held["mid_left"], both_right))),
            3: lambda: attention_back(0),
        },
    )
    attention_back(1)

    def input_back(m):
        s = st[m]
        moved = list(chain.after(*s["moved"]))
        terms = [s["terms"][0]] + moved if swap else moved
        s["qkv_back"], s["gain"], *part = input_back_call(
            s["q_back"], terms, token_rows, m, cos, sin, full_attn, n_q, n_kv, n_four // 2
        )
        chain.mark(part[0])
        red.load(part)

    def tail():
        d_qkv = product(held["left"], held["right"])
        owner = zi == 0
        gain_cols = jnp.stack(
            [
                st[0]["gain"][0] + st[1]["gain"][0],
                jnp.where(owner, sum(v[1] for v in gain_mid), 0.0),
                jnp.where(owner, sum(v[0] for v in gain_mid), 0.0),
                jnp.where(owner, sum(v[0] for v in gain_fin), 0.0),
            ],
            axis=1,
        )
        if pair:
            keep = lax.dynamic_slice_in_dim(gain_cols, dpi * (width // 2), width // 2, 0)
            give = lax.dynamic_slice_in_dim(gain_cols, (1 - dpi) * (width // 2), width // 2, 0)
            gain_cols = keep + swap_core(give)
        gain_cols = jnp.pad(gain_cols, ((0, 0), (0, PAD - gain_cols.shape[1])))
        packed = chain.mark(pack(list(chain.after(d_qkv, d_out, gain_cols)), 2))
        held["g_tail"] = spread(packed)

    def finish_down():
        (value,) = chain.after(held["g_down"])
        (held["g_down"],) = sum_parts(value, ff // 3, [[(0, ff // 3)]])
        chain.mark(held["g_down"])

    def finish_both():
        (value,) = chain.after(held["g_gate_up"])
        group = 6 * FF_TILE
        starts = range(0, group, 2 * FF_TILE)
        cuts = [[(i + o, i + o + FF_TILE) for i in starts] for o in (0, FF_TILE)]
        held["g_gate"], held["g_up"] = sum_parts(value, group, cuts)
        chain.mark(held["g_up"])

    def finish_tail():
        (value,) = chain.after(held["g_tail"])
        ends = [0, qc, qc + kc, at_out, at_out + oc, at_out + oc + PAD]
        *held["g_attn"], g_gains = sum_parts(value, ends[-1], [[v] for v in zip(ends, ends[1:])])
        g_gains = chain.mark(mm_t(pick.astype(F32), g_gains))
        held["g_gains"] = lax.all_to_all(
            jnp.broadcast_to(g_gains[None], (n_t,) + g_gains.shape), "tensor", 0, 0
        )

    red = Reduce(chain)
    input_back(0)
    d_out = product(left_side(attn_grads), right_side([s["attended"] for s in st]))
    finish_down()
    input_back(1)
    held["right"] = right_side([s["qkv_back"] for s in st])

    def finish_rest():
        finish_both()
        finish_tail()

    red.run(n_four, post_in, {1: tail, 4: finish_rest})
    g_gains = jnp.sum(held["g_gains"], axis=0)
    return (
        jnp.concatenate(outputs, axis=0).reshape(tokens.shape),
        input_grads[-1].reshape(tokens.shape),
        *held["g_attn"],
        held["g_gate"],
        held["g_up"],
        held["g_down"],
        g_gains[0],
        g_gains[1],
        g_gains[2],
        g_gains[3],
    )


def solution(mesh):
    act = P(None, "dp", "ctx", None)
    mat = P(("dp", "ctx"), "tensor")
    vec = P(("dp", "ctx"))
    return jax.shard_map(
        local,
        mesh=mesh,
        in_specs=(act, P()) + (mat,) * 7 + (vec,) * 4 + (act,),
        out_specs=(act, act) + (mat,) * 7 + (vec,) * 4,
        check_vma=False,
    )
```
